32 devices in a mesh: shard: 4 (over x, core), rep: 8 (over z, y).
Axes of the slice: x: 2, y: 2, z: 4, core: 2. Of those that a mesh axis runs over, the one named last changes fastest.
Arguments:
- tokens: bfloat16 [64, 512, 1024], P(('shard', 'rep')), may hold values from -6 to 6
- piece_start: int32 [64], P(('shard', 'rep')), may hold values from 0 to 256, as said below
- ln1_gain: bfloat16 [1024], P('shard'), may hold values from 0.5 to 1.5
- ln1_bias: bfloat16 [1024], P('shard'), may hold values from -1 to 1
- query_key_value_weight: bfloat16 [1024, 3072], P('shard'), may hold values from -0.1875 to 0.1875
- b_qv: bfloat16 [2048], P('shard'), may hold values from -1 to 1
- attention_out_weight: bfloat16 [1024, 1024], P('shard'), may hold values from -0.75 to 0.75
- attention_out_bias: bfloat16 [1024], P('shard'), may hold values from -1 to 1
- ln2_gain: bfloat16 [1024], P('shard'), may hold values from 0.5 to 1.5
- ln2_bias: bfloat16 [1024], P('shard'), may hold values from -1 to 1
- up_weight: bfloat16 [1024, 4096], P('shard'), may hold values from -0.1875 to 0.1875
- up_bias: bfloat16 [4096], P('shard'), may hold values from -1 to 1
- down_weight: bfloat16 [4096, 1024], P('shard'), may hold values from -0.09375 to 0.09375
- down_bias: bfloat16 [1024], P('shard'), may hold values from -1 to 1
- cotangent: bfloat16 [64, 512, 1024], P(('shard', 'rep')), may hold values from -6 to 6
Outputs:
- block_out: bfloat16 [64, 512, 1024], P(('shard', 'rep'))
- input_grad: float32 [64, 512, 1024], P(('shard', 'rep'))
- grad_ln1_gain: float32 [1024], P('shard')
- grad_ln1_bias: float32 [1024], P('shard')
- grad_w_qkv: float32 [1024, 3072], P('shard')
- grad_b_qv: float32 [2048], P('shard')
- grad_w_out: float32 [1024, 1024], P('shard')
- grad_b_out: float32 [1024], P('shard')
- grad_ln2_gain: float32 [1024], P('shard')
- grad_ln2_bias: float32 [1024], P('shard')
- grad_w_up: float32 [1024, 4096], P('shard')
- grad_b_up: float32 [4096], P('shard')
- grad_w_down: float32 [4096, 1024], P('shard')
- grad_b_down: float32 [1024], P('shard')
The draws below stay inside these ranges and needn't reach their ends.
Inputs may be any that keep to these rules, and one draw needn't show every extreme that they name: `piece_start`: some sequence's piece starts at 0 and some at 256.
All inputs are finite; a program needn't handle non-finite values.
Results may differ from the reference program's by a relative error of at most 0.014.
Values may be sent and summed in bfloat16 or wider, within the bound.
No kernel may reach another device: no remote copies, remote signals or barrier semaphores. Data moves between devices by JAX's collectives and lax.ppermute only.
A program may use at most 256 MiB of HBM per device.

```python
import math
import jax
import jax.numpy as jnp
from jax import lax

D = 1024
HEADS = 16
HEAD_DIM = 64
FF = 4096
SEQ_LEN = 512
PIECE = 256
SEQS = 64


def draw_piece_start(key, part):
    starts = jax.random.randint(key, (SEQS,), 0, SEQ_LEN - PIECE + 1, dtype=jnp.int32)
    return starts.at[0].set(SEQ_LEN - PIECE).at[SEQS - 1].set(0)


def levels(key, shape, shards, low, top_value):
    def one(dim, shards_of):
        steps = jax.random.uniform(jax.random.fold_in(jax.random.fold_in(key, 6), dim), (shards_of,), jnp.float32, low / len(shards), top_value / len(shards))
        return jnp.repeat(jnp.exp(steps), shape[dim] // shards_of).reshape((-1,) + (1,) * (len(shape) - dim - 1))

    level = one(*shards[0])
    for cut in shards[1:]:
        level = level * one(*cut)
    return level


def normal_values(own_key, dims, deviation, limit, cuts=(), kind=jnp.bfloat16):
    array = jax.random.normal(own_key, dims, jnp.float32) * deviation
    if len(cuts) > 0:
        array = levels(own_key, dims, cuts, -0.22, 0.18) * array
    return jnp.clip(array, min=-limit, max=limit).astype(kind)


def setup_inputs(seed: int = 0) -> dict:
    key_list = jax.random.split(jax.random.key(seed), 16)
    tokens = normal_values(key_list[0], (SEQS, SEQ_LEN, D), 1.0, 6.0, ((0, 32),))
    piece_start = draw_piece_start(jax.random.fold_in(key_list[15], 71), 0)
    ln1_gain = jnp.clip(1.0 + 0.1 * jax.random.normal(key_list[2], (D,), jnp.float32), 0.5, 1.5).astype(jnp.bfloat16)
    ln1_bias = normal_values(key_list[3], (D,), 0.2, 1.0, ((0, 4),))
    query_key_value_weight = normal_values(key_list[4], (D, 3 * D), D ** -0.5, 0.1875, ((0, 4),))
    b_qv = normal_values(key_list[5], (2 * D,), 0.2, 1.0, ((0, 4),))
    attention_out_weight = normal_values(key_list[6], (D, D), (D // 16) ** -0.5, 0.75, ((0, 4),))
    attention_out_bias = normal_values(key_list[7], (D,), 0.2, 1.0, ((0, 4),))
    ln2_gain = jnp.clip(1.0 + 0.1 * jax.random.normal(key_list[8], (D,), jnp.float32), 0.5, 1.5).astype(jnp.bfloat16)
    ln2_bias = normal_values(key_list[9], (D,), 0.2, 1.0, ((0, 4),))
    up_weight = normal_values(key_list[10], (D, FF), D ** -0.5, 0.1875, ((0, 4),))
    up_bias = normal_values(key_list[11], (FF,), 0.2, 1.0, ((0, 4),))
    down_weight = normal_values(key_list[12], (FF, D), FF ** -0.5, 0.09375, ((0, 4),))
    down_bias = normal_values(key_list[13], (D,), 0.2, 1.0, ((0, 4),))
    cotangent = normal_values(key_list[14], (SEQS, SEQ_LEN, D), 1.0, 6.0, ((0, 32),))
    return {"tokens": tokens, "piece_start": piece_start, "ln1_gain": ln1_gain, "ln1_bias": ln1_bias, "query_key_value_weight": query_key_value_weight, "b_qv": b_qv, "attention_out_weight": attention_out_weight, "attention_out_bias": attention_out_bias, "ln2_gain": ln2_gain, "ln2_bias": ln2_bias, "up_weight": up_weight, "up_bias": up_bias, "down_weight": down_weight, "down_bias": down_bias, "cotangent": cotangent}


@jax.custom_vjp
def low(v):
    return lax.optimization_barrier(v.astype(jnp.bfloat16)).astype(jnp.float32)

@jax.custom_vjp
def lower_backward(v):
    return v

def low_keep(v):
    return (low(v), None)

def low_pass(kept, grad):
    return (grad,)

def back_keep(v):
    return (v, None)

def back_low(kept, grad):
    return (low(grad),)
low.defvjp(low_keep, low_pass)
lower_backward.defvjp(back_keep, back_low)
eps_norm = 1e-05
masked_fill = -1e+30

def normalize(values_in, gain_vec, shift_vec):
    center = values_in - lax.optimization_barrier(jnp.mean(values_in, axis=-1, keepdims=True))
    spread_sq = lax.optimization_barrier(jnp.mean(center * center, axis=-1, keepdims=True))
    return center * lax.rsqrt(spread_sq + eps_norm) * gain_vec + shift_vec

def gelu_tanh(pre_act):
    return 0.5 * pre_act * (1.0 + jnp.tanh(0.7978845608028654 * (pre_act + 0.044715 * pre_act * pre_act * pre_act)))

def visible_bias(start_at, seq_len, piece_len, head_count):
    position = jnp.arange(seq_len, dtype=jnp.int32)
    inside = (position >= start_at) & (position < start_at + piece_len)
    allowed = (position[None, :] <= position[:, None]) | inside[:, None] & inside[None, :]
    distance = jnp.abs(position[:, None] - position[None, :]).astype(jnp.float32)
    slopes = jnp.exp2(-8.0 * (jnp.arange(head_count, dtype=jnp.float32) + 1.0) / head_count)
    return (allowed, -slopes[:, None, None] * distance[None, :, :])

def attend_one(queries, key_rows, value_rows, start_at):
    allowed, alibi_bias = visible_bias(start_at, SEQ_LEN, PIECE, HEADS)
    scores = jnp.einsum('qhd,khd->hqk', queries, key_rows, precision=lax.Precision.HIGHEST) * (1.0 / math.sqrt(HEAD_DIM)) + alibi_bias
    scores = lower_backward(scores)
    scores = jnp.where(allowed[None, :, :], scores, masked_fill)
    probs = jax.nn.softmax(scores, axis=-1)
    return jnp.einsum('hqk,khd->qhd', low(probs), value_rows, precision=lax.Precision.HIGHEST)

def layer(tokens_f, start_vec, ln1_gain, ln1_bias, query_key_value_weight, b_qv, attention_out_weight, attention_out_bias, ln2_gain, ln2_bias, up_weight, up_bias, down_weight, down_bias):
    group_size, seq_len, width = tokens_f.shape
    highest_precision = lax.Precision.HIGHEST
    first_normed = low(normalize(tokens_f, ln1_gain, ln1_bias))
    joined_heads = jnp.einsum('ymv,vo->ymo', first_normed, query_key_value_weight, precision=highest_precision)
    queries = low(lower_backward(joined_heads[..., :width] + b_qv[:width]))
    key_rows = low(lower_backward(joined_heads[..., width:2 * width]))
    value_rows = low(lower_backward(joined_heads[..., 2 * width:] + b_qv[width:]))
    split_shape = (group_size, seq_len, HEADS, HEAD_DIM)
    checked = jax.checkpoint(attend_one)

    def per_sequence(seq_item):
        return checked(seq_item[0], seq_item[1], seq_item[2], seq_item[3])
    attention_result = lax.map(per_sequence, (queries.reshape(split_shape), key_rows.reshape(split_shape), value_rows.reshape(split_shape), start_vec))
    attention_result = low(lower_backward(attention_result.reshape(group_size, seq_len, width)))
    first_branch = lower_backward(jnp.einsum('ymv,vo->ymo', attention_result, attention_out_weight, precision=highest_precision) + attention_out_bias)
    middle = tokens_f + first_branch
    second_normed = low(normalize(middle, ln2_gain, ln2_bias))
    hidden_before_gelu = lower_backward(jnp.einsum('ejt,tb->ejb', second_normed, up_weight, precision=highest_precision) + up_bias)
    hidden_activation = low(gelu_tanh(hidden_before_gelu))
    second_branch = lower_backward(jnp.einsum('ntb,bi->nti', hidden_activation, down_weight, precision=highest_precision) + down_bias)
    return middle + second_branch

def reference(tokens, piece_start, ln1_gain, ln1_bias, query_key_value_weight, b_qv, attention_out_weight, attention_out_bias, ln2_gain, ln2_bias, up_weight, up_bias, down_weight, down_bias, cotangent):
    group_size = math.gcd(SEQS, max(1, 4096 // SEQ_LEN))
    rounds = SEQS // group_size
    weights = tuple((param.astype(jnp.float32) for param in (ln1_gain, ln1_bias, query_key_value_weight, b_qv, attention_out_weight, attention_out_bias, ln2_gain, ln2_bias, up_weight, up_bias, down_weight, down_bias)))
    token_groups = tokens.astype(jnp.float32).reshape(rounds, group_size, SEQ_LEN, D)
    cot_groups = cotangent.astype(jnp.float32).reshape(rounds, group_size, SEQ_LEN, D)
    start_groups = piece_start.astype(jnp.int32).reshape(rounds, group_size)

    def one_group(accum, group_item):
        tokens_f, start_vec, cot_f = group_item

        def forward(tokens_in, *params):
            return layer(tokens_in, start_vec, *params)
        outputs, pull = jax.vjp(forward, tokens_f, *weights)
        grads = pull(cot_f)
        accum = tuple((total + part for total, part in zip(accum, grads[1:])))
        return (accum, (outputs.astype(jnp.bfloat16), grads[0]))
    init = tuple((jnp.zeros(param.shape, jnp.float32) for param in weights))
    summed, (out_groups, grad_groups) = lax.scan(one_group, init, (token_groups, start_groups, cot_groups))
    return (out_groups.reshape(SEQS, SEQ_LEN, D), grad_groups.reshape(SEQS, SEQ_LEN, D), summed[0], summed[1], summed[2], summed[3], summed[4], summed[5], summed[6], summed[7], summed[8], summed[9], summed[10], summed[11])
```

```python
import functools

import jax
import jax.numpy as jnp
from jax import lax
from jax.experimental import pallas as pl
from jax.experimental.pallas import tpu as pltpu
from jax.sharding import PartitionSpec as P

HEADS = 16
PIECE = 256
HEAD_DIM = 64
PAIR = 2 * HEAD_DIM
SHARDS = 4
CHUNKS = 4
EPS = 1e-05
HIDDEN_PENALTY = 1e33

bf16 = jnp.bfloat16
f32 = jnp.float32

VEC = {
    "ln1_gain": (0, 256),
    "ln1_bias": (256, 256),
    "b_qv": (512, 512),
    "out_bias": (1024, 256),
    "ln2_gain": (1280, 256),
    "ln2_bias": (1536, 256),
    "up_bias": (1792, 1024),
    "down_bias": (2816, 256),
}
VEC_LEN = 3072

any_spec = pl.BlockSpec(memory_space=pltpu.MemorySpace.HBM)


def dot(left, right, left_dim=1, right_dim=0):
    return lax.dot_general(
        left, right, (((left_dim,), (right_dim,)), ((), ())), preferred_element_type=f32
    )


def params(mib):
    return pltpu.CompilerParams(vmem_limit_bytes=int(mib * 2**20))


def cost(flops, moved, transcendentals=0, scale=4):
    return pl.CostEstimate(
        flops=int(scale * flops), bytes_accessed=int(scale * moved), transcendentals=int(scale * transcendentals)
    )


def row_of(vec_ref, name):
    start, size = VEC[name]
    return jnp.concatenate(
        [vec_ref[shard : shard + 1, start : start + size] for shard in range(SHARDS)], axis=1
    )


def whole(shape):
    return pl.BlockSpec(shape, lambda *_: (0,) * len(shape))


def flip(value, axis, size, bit):
    return lax.ppermute(value, axis, [(i, i ^ bit) for i in range(size)])


class Moves:
    def __init__(self, mesh, starts):
        self.reps = mesh.shape["rep"]
        assert mesh.shape["shard"] == SHARDS and self.reps % 4 == 0
        self.shard = lax.axis_index("shard")
        rep = lax.axis_index("rep")
        self.low = rep & 1
        self.mid = (rep >> 1) & 1
        self.index = jnp.concatenate(
            [jnp.stack([self.shard, self.low, self.mid]).astype(jnp.int32), starts]
        )
        self.last = ()

    def wait(self, *values):
        self.index = lax.optimization_barrier((self.index, *values))[0]

    def ran(self, value):
        self.last = (value,)
        return value

    def move(self, value, axis, size, bit):
        return flip(after(value, *self.last), axis, size, bit)

    def core(self, value):
        return self.move(value, "shard", SHARDS, 1)

    def across(self, value):
        return self.move(value, "shard", SHARDS, 2)

    def rep(self, value, bit):
        return self.move(value, "rep", self.reps, bit)

    def half(self, own):
        rows = own.shape[-2] // 2
        return lax.dynamic_slice_in_dim(own, self.low * rows, rows, own.ndim - 2)

    def pick(self, value, which, size):
        return lax.dynamic_slice_in_dim(value, which * size, size, 1)

    def reduce_vec(self, value):
        value = value + self.core(value)
        value = value + self.across(value)
        row = lax.dynamic_slice_in_dim(value, self.shard, 1, 0)
        bit = 1
        while bit < self.reps:
            row = row + self.rep(row, bit)
            bit *= 2
        return row


def after(value, *earlier):
    return lax.optimization_barrier((value, *earlier))[0] if earlier else value


class ShardSum:
    def __init__(self, moves, keep, send):
        self.moves, self.keep = moves, keep
        self.got = moves.core(send)

    def cross(self):
        out = self.keep[1] + self.got[1]
        self.mine = self.keep[0] + self.got[0]
        self.moves.wait(out, self.mine)
        self.got = self.moves.across(out)

    def halves(self):
        moves, mine, got = self.moves, self.mine, self.got
        size = mine.shape[1] // 2
        return [
            moves.pick(mine, which, size) + moves.pick(got, which, size)
            for which in (moves.low, 1 - moves.low)
        ]


class RepSum:
    def __init__(self, moves, sums):
        self.moves = moves
        halves = [s.halves() for s in sums]
        self.mine = jnp.concatenate([h[0] for h in halves])
        self.send(jnp.concatenate([h[1] for h in halves]), 1)
        self.bit = 2

    def send(self, out, bit):
        self.moves.wait(out, self.mine)
        self.got = self.moves.rep(out, bit)

    def split(self):
        moves = self.moves
        size = self.mine.shape[1] // 2
        out, self.mine = [
            moves.pick(self.mine, which, size) + moves.pick(self.got, which, size)
            for which in (1 - moves.mid, moves.mid)
        ]
        self.send(out, 2)

    def add(self):
        self.mine = self.mine + self.got
        self.bit *= 2
        self.got = None
        if self.bit < self.moves.reps:
            self.send(self.mine, self.bit)

    def spread(self):
        while self.got is not None:
            self.add()
        self.send(self.mine, 2)

    def finish(self):
        self.pair = jnp.stack([self.mine, self.got])
        self.send(self.pair, 1)

    def pieces(self):
        self.moves.wait(self.got)
        return (self.pair, self.got)


def piece_copies(index_ref, pieces, target, sems):
    shard, low = index_ref[0], index_ref[1]
    rows = pieces[0].shape[-2]
    if len(pieces) == 4:
        plan = [(piece, shard ^ k, 0, rows) for k, piece in enumerate(pieces)]
    else:
        own, near, far, far_other, far_near, far_other_near = pieces
        half = rows // 2
        plan = (
            (own, shard, 0, rows),
            (near, shard ^ 1, 0, rows),
            (far, shard ^ 2, low * half, half),
            (far_other, shard ^ 2, (1 - low) * half, half),
            (far_near, shard ^ 3, low * half, half),
            (far_other_near, shard ^ 3, (1 - low) * half, half),
        )
    return [
        pltpu.make_async_copy(source, target(to, first, count), sems.at[i])
        for i, (source, to, first, count) in enumerate(plan)
    ]


def norm_parts(value):
    center = value - jnp.mean(value, axis=-1, keepdims=True)
    inverse = lax.rsqrt(jnp.mean(center * center, axis=-1, keepdims=True) + EPS)
    return center * inverse, inverse


def first_norm_body(index_ref, tokens_ref, own_ref, near_ref, far_ref, far_near_ref, normed_ref, vec_ref):
    shard = index_ref[0]

    @pl.when(pl.program_id(0) == 0)
    def _():
        for k, ref in enumerate((own_ref, near_ref, far_ref, far_near_ref)):
            vec_ref[pl.ds(shard ^ k, 1), :] = ref[...].astype(f32)

    hat, _ = norm_parts(tokens_ref[...].astype(f32))
    normed_ref[...] = (hat * row_of(vec_ref, "ln1_gain") + row_of(vec_ref, "ln1_bias")).astype(bf16)


def first_norm(index, tokens, vec_pieces, block=256):
    rows, width = tokens.shape
    row = pl.BlockSpec((block, width), lambda i, idx: (i, 0))
    return pl.pallas_call(
        first_norm_body,
        grid_spec=pltpu.PrefetchScalarGridSpec(
            num_scalar_prefetch=1,
            grid=(rows // block,),
            in_specs=[row] + [whole((1, VEC_LEN))] * 4,
            out_specs=[row, whole((SHARDS, VEC_LEN))],
        ),
        out_shape=[
            jax.ShapeDtypeStruct((rows, width), bf16),
            jax.ShapeDtypeStruct((SHARDS, VEC_LEN), f32),
        ],
        compiler_params=params(16),
        cost_estimate=cost(20 * rows * width, 4 * rows * width),
        name="first_norm",
    )(index, tokens, *vec_pieces)


def joined_body(half, index_ref, *refs):
    pieces, (normed_ref, vec_ref, out_ref, weight_ref, sems) = refs[:-5], refs[-5:]

    @pl.when(pl.program_id(0) == 0)
    def _():
        rows = pieces[0].shape[0]
        copies = piece_copies(
            index_ref,
            pieces,
            lambda to, first, count: weight_ref.at[
                pl.ds(pl.multiple_of(to * rows + first, 128), count), :
            ],
            sems,
        )
        for copy in copies:
            copy.start()
        for copy in copies:
            copy.wait()

    part = weight_ref.shape[1] // 3
    start = VEC["b_qv"][0]
    normed = normed_ref[...]
    for i in range(3):
        cols = slice(i * part, (i + 1) * part)
        value = dot(normed, weight_ref[:, cols])
        if i != 1:
            shard = half if i == 0 else 2 + half
            value = value + vec_ref[shard : shard + 1, start : start + part]
        out_ref[:, cols] = value.astype(bf16)


def joined_product(half, index, pieces, normed, vec, block=256):
    rows, width = normed.shape
    cols = pieces[0].shape[1]
    return pl.pallas_call(
        functools.partial(joined_body, half),
        grid_spec=pltpu.PrefetchScalarGridSpec(
            num_scalar_prefetch=1,
            grid=(rows // block,),
            in_specs=[any_spec] * len(pieces)
            + [pl.BlockSpec((block, width), lambda i, idx: (i, 0)), whole((SHARDS, VEC_LEN))],
            out_specs=[pl.BlockSpec((block, cols), lambda i, idx: (i, 0)), whole((width, cols))],
            scratch_shapes=[pltpu.SemaphoreType.DMA((6,))],
        ),
        out_shape=[
            jax.ShapeDtypeStruct((rows, cols), bf16),
            jax.ShapeDtypeStruct((width, cols), bf16),
        ],
        compiler_params=params(24),
        cost_estimate=cost(2 * rows * width * cols, 2 * (rows * width + rows * cols + 2 * width * cols)),
        name="joined_product",
    )(index, *pieces, normed, vec)


def penalty(start, seq_len):
    key = lax.broadcasted_iota(jnp.int32, (seq_len, seq_len), 0)
    query = lax.broadcasted_iota(jnp.int32, (seq_len, seq_len), 1)
    key_in = (key >= start) & (key < start + PIECE)
    query_in = (query >= start) & (query < start + PIECE)
    seen = (key <= query) | (key_in & query_in)
    return jnp.where(seen, jnp.abs(key - query).astype(f32), HIDDEN_PENALTY)


def slope_of(head):
    return jnp.exp2((jnp.full((1, 1), head, jnp.int32).astype(f32) + 1.0) * (-8.0 / HEADS))


def attend_forward_body(first_head, start_ref, q_ref, k_ref, v_ref, out_ref, total_ref, pen_ref):
    pair = pl.program_id(1)
    seq_len = q_ref.shape[0]

    @pl.when(pair == 0)
    def _():
        pen_ref[...] = penalty(start_ref[3 + pl.program_id(0)], seq_len)

    queries, keys = q_ref[...], k_ref[...]
    values_t = v_ref[...].T
    lane = lax.broadcasted_iota(jnp.int32, (seq_len, PAIR), 1)
    outs = []
    for e in range(2):
        chosen = (lane < HEAD_DIM) if e == 0 else (lane >= HEAD_DIM)
        key_e = jnp.where(chosen, keys * (HEAD_DIM**-0.5), 0).astype(bf16)
        scores = dot(key_e, queries, 1, 1) - slope_of(first_head + 2 * pair + e) * pen_ref[...]
        top = jnp.max(scores, axis=0, keepdims=True)
        weight = jnp.exp(scores - top)
        total = jnp.sum(weight, axis=0, keepdims=True)
        out_t = dot(values_t[e * HEAD_DIM : (e + 1) * HEAD_DIM, :], weight.astype(bf16))
        outs.append(out_t * (1.0 / total))
        total_ref[0, 0, e : e + 1, :] = top + jnp.log(total)
    out_ref[...] = jnp.concatenate(outs, axis=0).T.astype(bf16)


def attend_forward(half, index, joined):
    count = index.shape[0] - 3
    seq_len, width = joined.shape[0] // count, joined.shape[1] // 3
    pairs = width // PAIR

    def cols(first):
        return pl.BlockSpec((seq_len, PAIR), lambda s, h, st: (s, first + h))

    return pl.pallas_call(
        functools.partial(attend_forward_body, half * 2 * pairs),
        grid_spec=pltpu.PrefetchScalarGridSpec(
            num_scalar_prefetch=1,
            grid=(count, pairs),
            in_specs=[cols(0), cols(pairs), cols(2 * pairs)],
            out_specs=[cols(0), pl.BlockSpec((1, 1, 2, seq_len), lambda s, h, st: (s, h, 0, 0))],
            scratch_shapes=[pltpu.VMEM((seq_len, seq_len), f32)],
        ),
        out_shape=[
            jax.ShapeDtypeStruct((count * seq_len, width), bf16),
            jax.ShapeDtypeStruct((count, pairs, 2, seq_len), f32),
        ],
        compiler_params=params(24),
        cost_estimate=cost(
            24 * count * seq_len * seq_len * width, 8 * count * seq_len * width, count * seq_len * seq_len * 2 * pairs
        ),
        name="attend_forward",
    )(index, joined, joined, joined)


def attend_backward_body(
    first_head, start_ref, q_ref, k_ref, v_ref, out_ref, dout_ref, total_ref, dq_ref, dk_ref, dv_ref, pen_ref
):
    pair = pl.program_id(1)
    seq_len = q_ref.shape[0]
    scale = HEAD_DIM**-0.5

    @pl.when(pair == 0)
    def _():
        pen_ref[...] = penalty(start_ref[3 + pl.program_id(0)], seq_len)

    queries, keys, values, d_out = q_ref[...], k_ref[...], v_ref[...], dout_ref[...]
    lane = lax.broadcasted_iota(jnp.int32, (seq_len, PAIR), 1)
    keys_t = keys.T
    both_t = (d_out.astype(f32) * out_ref[...].astype(f32)).T
    d_q, d_k, d_v = [], [], []
    for e in range(2):
        chosen = (lane < HEAD_DIM) if e == 0 else (lane >= HEAD_DIM)
        part = slice(e * HEAD_DIM, (e + 1) * HEAD_DIM)
        key_e = jnp.where(chosen, keys * scale, 0).astype(bf16)
        value_e = jnp.where(chosen, values, 0)
        inner = jnp.sum(both_t[part, :], axis=0, keepdims=True)
        scores = dot(key_e, queries, 1, 1) - slope_of(first_head + 2 * pair + e) * pen_ref[...]
        probs = jnp.exp(scores - total_ref[0, 0, e : e + 1, :])
        d_scores = (probs * (dot(value_e, d_out, 1, 1) - inner)).astype(bf16)
        d_v.append(dot(probs.astype(bf16), d_out))
        d_k.append(dot(d_scores, queries))
        d_q.append(dot(keys_t[part, :], d_scores))
    dq_ref[...] = (jnp.concatenate(d_q, axis=0) * scale).T.astype(bf16)
    dk_ref[...] = (jnp.where(lane < HEAD_DIM, d_k[0], d_k[1]) * scale).astype(bf16)
    dv_ref[...] = jnp.where(lane < HEAD_DIM, d_v[0], d_v[1]).astype(bf16)


def attend_backward(half, index, joined, attended, d_attended, totals):
    count = index.shape[0] - 3
    seq_len, width = joined.shape[0] // count, joined.shape[1] // 3
    pairs = width // PAIR

    def cols(first):
        return pl.BlockSpec((seq_len, PAIR), lambda s, h, st: (s, first + h))

    return pl.pallas_call(
        functools.partial(attend_backward_body, half * 2 * pairs),
        grid_spec=pltpu.PrefetchScalarGridSpec(
            num_scalar_prefetch=1,
            grid=(count, pairs),
            in_specs=[
                cols(0),
                cols(pairs),
                cols(2 * pairs),
                cols(0),
                cols(half * pairs),
                pl.BlockSpec((1, 1, 2, seq_len), lambda s, h, st: (s, h, 0, 0)),
            ],
            out_specs=[cols(0)] * 3,
            scratch_shapes=[pltpu.VMEM((seq_len, seq_len), f32)],
        ),
        out_shape=[jax.ShapeDtypeStruct((count * seq_len, width), bf16)] * 3,
        compiler_params=params(24),
        cost_estimate=cost(
            36 * count * seq_len * seq_len * width, 16 * count * seq_len * width, count * seq_len * seq_len * 2 * pairs
        ),
        name="attend_backward",
    )(index, joined, joined, joined, attended, d_attended, totals)


def middle_body(index_ref, *refs):
    pieces, (a_ref, b_ref, tokens_ref, vec_ref, middle_ref, normed_ref, weight_ref, sems) = refs[:6], refs[6:]

    @pl.when(pl.program_id(0) == 0)
    def _():
        rows = pieces[0].shape[0]
        copies = piece_copies(
            index_ref,
            pieces,
            lambda to, first, count: weight_ref.at[
                pl.ds(pl.multiple_of(to * rows + first, 128), count), :
            ],
            sems,
        )
        for copy in copies:
            copy.start()
        for copy in copies:
            copy.wait()

    part = a_ref.shape[1]
    middle = tokens_ref[...].astype(f32) + row_of(vec_ref, "out_bias")
    middle = middle + dot(a_ref[...], weight_ref[:part, :]) + dot(b_ref[...], weight_ref[part:, :])
    middle_ref[...] = middle
    hat, _ = norm_parts(middle)
    normed_ref[...] = (hat * row_of(vec_ref, "ln2_gain") + row_of(vec_ref, "ln2_bias")).astype(bf16)


def middle_product(index, pieces, attended, tokens, vec, block=256):
    rows, width = tokens.shape
    row = pl.BlockSpec((block, width), lambda i, idx: (i, 0))
    part = pl.BlockSpec((block, attended[0].shape[1]), lambda i, idx: (i, 0))
    return pl.pallas_call(
        middle_body,
        grid_spec=pltpu.PrefetchScalarGridSpec(
            num_scalar_prefetch=1,
            grid=(rows // block,),
            in_specs=[any_spec] * 6 + [part, part, row, whole((SHARDS, VEC_LEN))],
            out_specs=[row, row, whole((width, width))],
            scratch_shapes=[pltpu.SemaphoreType.DMA((6,))],
        ),
        out_shape=[
            jax.ShapeDtypeStruct((rows, width), f32),
            jax.ShapeDtypeStruct((rows, width), bf16),
            jax.ShapeDtypeStruct((width, width), bf16),
        ],
        compiler_params=params(24),
        cost_estimate=cost(2 * rows * width * width, 10 * rows * width + 4 * width * width),
        name="middle_product",
    )(index, *pieces, *attended, tokens, vec)


def gelu_and_slope(pre):
    cube = 0.044715 * pre * pre
    inner = jnp.tanh(0.7978845608028654 * (pre + cube * pre))
    half = 0.5 * (1.0 + inner)
    slope = half + 0.5 * pre * (1.0 - inner * inner) * (0.7978845608028654 * (1.0 + 3.0 * cube))
    return pre * half, slope


def hidden_body(chunk, fresh, index_ref, *refs):
    pieces, refs = refs[:6], refs[6:]
    if not fresh:
        refs = refs[2:]
    normed_hbm, cot_hbm, vec_ref = refs[:3]
    hidden_out, pre_out, keep_ref, send_ref, bias_ref = refs[3:8]
    normed_ref, cot_ref, up_ref, down_ref, hidden_ref, pre_ref, slope_ref, sems, whole_sems = refs[8:]
    step = pl.program_id(0)
    shard = index_ref[0]
    block = 256

    def loads():
        def rows_of(ref, unit):
            rows = pieces[0].shape[1]
            return piece_copies(
                index_ref,
                [piece.at[unit] for piece in pieces],
                lambda to, first, count: ref.at[pl.ds(pl.multiple_of(to * rows + first, 128), count), :],
                sems.at[unit],
            )

        first = [pltpu.make_async_copy(normed_hbm, normed_ref, whole_sems.at[0])] + rows_of(up_ref, 0)
        second = [pltpu.make_async_copy(cot_hbm, cot_ref, whole_sems.at[1])] + rows_of(down_ref, 1)
        return first, second

    def stores():
        cols = pl.ds(chunk * hidden_ref.shape[1], hidden_ref.shape[1])
        return (
            pltpu.make_async_copy(hidden_ref, hidden_out.at[:, cols], whole_sems.at[2]),
            pltpu.make_async_copy(pre_ref, pre_out.at[:, cols], whole_sems.at[3]),
        )

    @pl.when(step == 0)
    def _():
        first, second = loads()
        for copy in first + second:
            copy.start()
        for copy in first:
            copy.wait()

    @pl.when(step == 1)
    def _():
        for copy in loads()[1]:
            copy.wait()

    rows_each = 256
    count = normed_ref.shape[0] // rows_each

    @pl.when(step == 0)
    def _():
        start = VEC["up_bias"][0] + chunk * block
        bias = jnp.concatenate(
            [vec_ref[one : one + 1, start : start + block] for one in range(SHARDS)], axis=1
        )
        for m in range(count):
            rows = slice(m * rows_each, (m + 1) * rows_each)
            value, slope = gelu_and_slope(dot(normed_ref[rows, :], up_ref[...]) + bias)
            value = value.astype(bf16)
            hidden_ref[rows, :] = value
            slope_ref[rows, :] = slope
        stores()[0].start()

    @pl.when(step == 1)
    def _():
        sums = jnp.zeros(bias_ref.shape, f32)
        for m in range(count):
            rows = slice(m * rows_each, (m + 1) * rows_each)
            d_pre = (dot(cot_ref[rows, :], down_ref[...], 1, 1) * slope_ref[rows, :]).astype(bf16)
            pre_ref[rows, :] = d_pre
            sums = sums + jnp.sum(d_pre.astype(f32), axis=0, keepdims=True)
        bias_ref[...] = sums
        stores()[1].start()

    @pl.when(step >= 2)
    def _():
        k = jnp.where(step < 4, 2 * (step - 2) + 1, 2 * (step - 4))
        cols = pl.ds(pl.multiple_of((shard ^ k) * block, block), block)
        left, right = normed_ref[:, cols], hidden_ref[:, cols]
        one = dot(left, pre_ref[...], 0, 0).astype(bf16)
        two = dot(right, cot_ref[...], 0, 0).astype(bf16)

        @pl.when(step < 4)
        def _():
            send_ref[0, 0] = one
            send_ref[0, 1] = two

        @pl.when(step >= 4)
        def _():
            keep_ref[0, 0] = one
            keep_ref[0, 1] = two

    @pl.when(step == 5)
    def _():
        for copy in stores():
            copy.wait()


def hidden_chunk(chunk, index, pieces, carried, normed, cot, vec, hidden_size):
    rows, width = normed.shape
    size = hidden_size // CHUNKS
    fresh = carried is None
    grads = (2, 2, width // SHARDS, size)
    outs = [
        jax.ShapeDtypeStruct((rows, hidden_size), bf16),
        jax.ShapeDtypeStruct((rows, hidden_size), bf16),
        jax.ShapeDtypeStruct(grads, bf16),
        jax.ShapeDtypeStruct(grads, bf16),
        jax.ShapeDtypeStruct((1, size), f32),
    ]
    unit = (1,) + grads[1:]
    return pl.pallas_call(
        functools.partial(hidden_body, chunk, fresh),
        grid_spec=pltpu.PrefetchScalarGridSpec(
            num_scalar_prefetch=1,
            grid=(6,),
            in_specs=[any_spec] * (8 if fresh else 10) + [whole((SHARDS, VEC_LEN))],
            out_specs=[
                any_spec,
                any_spec,
                pl.BlockSpec(unit, lambda i, idx: (jnp.maximum(i - 4, 0), 0, 0, 0)),
                pl.BlockSpec(unit, lambda i, idx: (jnp.clip(i - 2, 0, 1), 0, 0, 0)),
                pl.BlockSpec((1, size), lambda i, idx: (0, 0)),
            ],
            scratch_shapes=[
                pltpu.VMEM((rows, width), bf16),
                pltpu.VMEM((rows, width), bf16),
                pltpu.VMEM((width, size), bf16),
                pltpu.VMEM((size, width), bf16),
                pltpu.VMEM((rows, size), bf16),
                pltpu.VMEM((rows, size), bf16),
                pltpu.VMEM((rows, size), f32),
                pltpu.SemaphoreType.DMA((2, 6)),
                pltpu.SemaphoreType.DMA((4,)),
            ],
        ),
        out_shape=outs,
        input_output_aliases={} if fresh else {7: 0, 8: 1},
        compiler_params=params(48),
        cost_estimate=cost(8 * rows * width * size, 8 * rows * width + 16 * rows * size, rows * size),
        name=f"hidden_chunk{chunk}",
    )(index, *pieces, *(carried or ()), normed, cot, vec)


def norm_back(d_normed, hat, inverse, gain):
    scaled = d_normed * gain
    return inverse * (
        scaled
        - jnp.mean(scaled, axis=-1, keepdims=True)
        - hat * jnp.mean(scaled * hat, axis=-1, keepdims=True)
    )


def column_sum(value):
    return jnp.sum(value, axis=0, keepdims=True)


def chunk_loads(index_ref, pieces, unit, target, sems):
    loads = []
    for chunk in range(CHUNKS):
        group = pieces[6 * chunk : 6 * chunk + 6]
        rows = group[0].shape[1]
        loads.append(
            piece_copies(
                index_ref,
                [piece.at[unit] for piece in group],
                lambda to, first, count, chunk=chunk: target(
                    chunk, pl.multiple_of(to * rows + first, 128), count
                ),
                sems.at[chunk],
            )
        )
    return loads


def block_back_body(index_ref, *refs, blocks):
    pieces, refs = refs[: 6 * CHUNKS], refs[6 * CHUNKS :]
    pre_ref, middle_ref, cot_ref, a_ref, b_ref, weight_ref, vec_ref = refs[:7]
    d_middle_ref, d_attended_ref, keep_ref, send_ref, sums_ref = refs[7:12]
    up_ref, d_one_ref, sems = refs[12:]
    step = pl.program_id(0)
    rows = pre_ref.shape[0]
    size = up_ref.shape[1] // CHUNKS

    def rest(d_normed):
        middle = middle_ref[...]
        cot = cot_ref[...].astype(f32)
        hat, inverse = norm_parts(middle)
        d_middle = cot + norm_back(d_normed, hat, inverse, row_of(vec_ref, "ln2_gain"))
        d_one = d_middle.astype(bf16)
        d_middle_ref[...] = d_middle
        d_one_ref[pl.ds(pl.multiple_of(step * rows, rows), rows), :] = d_one
        sums_ref[0:1, :] += column_sum(d_normed * hat)
        sums_ref[1:2, :] += column_sum(d_normed)
        sums_ref[2:3, :] += column_sum(d_one.astype(f32))
        sums_ref[3:4, :] += column_sum(cot)

    @pl.when(step == 0)
    def _():
        loads = chunk_loads(
            index_ref,
            pieces,
            0,
            lambda chunk, first, count: up_ref.at[pl.ds(first, count), chunk * size : (chunk + 1) * size],
            sems,
        )
        for group in loads:
            for copy in group:
                copy.start()
        sums_ref[...] = jnp.zeros_like(sums_ref)
        d_normed = None
        for chunk, group in enumerate(loads):
            for copy in group:
                copy.wait()
            cols = slice(chunk * size, (chunk + 1) * size)
            term = dot(pre_ref[:, cols], up_ref[:, cols], 1, 1)
            d_normed = term if d_normed is None else d_normed + term
        rest(d_normed)

    @pl.when((step > 0) & (step < blocks))
    def _():
        rest(dot(pre_ref[...], up_ref[...], 1, 1))

    for t, k in enumerate((1, 3, 0, 2)):

        @pl.when(step == blocks + t)
        def _(t=t, k=k):
            block = weight_ref.shape[0] // SHARDS
            part = keep_ref.shape[3]
            d_one = d_one_ref[...]
            d_attended_ref[...] = dot(d_one, weight_ref[t * block : (t + 1) * block, :], 1, 1).astype(bf16)
            shard = index_ref[0] ^ k
            target = send_ref if t < 2 else keep_ref
            cols = pl.ds(pl.multiple_of((shard & 1) * block, block), block)

            def put(ref):
                value = dot(ref[:, cols], d_one, 0, 0).astype(bf16)
                for unit in range(2):
                    target[0, unit] = value[:, unit * part : (unit + 1) * part]

            pl.when(shard < 2)(lambda: put(a_ref))
            pl.when(shard >= 2)(lambda: put(b_ref))


def block_back(index, pieces, d_pre, middle, cot, attended, weight, vec, rows_each=256):
    rows, width = middle.shape
    size = d_pre.shape[1]
    blocks = rows // rows_each
    quarter = width // SHARDS

    def by_rows(cols):
        return pl.BlockSpec((rows_each, cols), lambda i, idx: (jnp.minimum(i, blocks - 1), 0))

    grads = (2, 2, quarter, width // 2)
    unit = (1,) + grads[1:]
    half = whole((rows, attended[0].shape[1]))
    return pl.pallas_call(
        functools.partial(block_back_body, blocks=blocks),
        grid_spec=pltpu.PrefetchScalarGridSpec(
            num_scalar_prefetch=1,
            grid=(blocks + SHARDS,),
            in_specs=[any_spec] * (6 * CHUNKS)
            + [
                by_rows(size),
                by_rows(width),
                by_rows(width),
                half,
                half,
                whole((width, width)),
                whole((SHARDS, VEC_LEN)),
            ],
            out_specs=[
                by_rows(width),
                pl.BlockSpec((rows, quarter), lambda i, idx: (0, jnp.maximum(i - blocks, 0))),
                pl.BlockSpec(unit, lambda i, idx: (jnp.maximum(i - blocks - 2, 0), 0, 0, 0)),
                pl.BlockSpec(unit, lambda i, idx: (jnp.clip(i - blocks, 0, 1), 0, 0, 0)),
                whole((8, width)),
            ],
            scratch_shapes=[
                pltpu.VMEM((width, size), bf16),
                pltpu.VMEM((rows, width), bf16),
                pltpu.SemaphoreType.DMA((CHUNKS, 6)),
            ],
        ),
        out_shape=[
            jax.ShapeDtypeStruct((rows, width), f32),
            jax.ShapeDtypeStruct((rows, width), bf16),
            jax.ShapeDtypeStruct(grads, bf16),
            jax.ShapeDtypeStruct(grads, bf16),
            jax.ShapeDtypeStruct((8, width), f32),
        ],
        compiler_params=params(48),
        cost_estimate=cost(2 * rows * width * (size + 2 * width), 2 * rows * size + 2 * width * size + 16 * rows * width),
        name="block_back",
    )(index, *pieces, d_pre, middle, cot, *attended, weight, vec)


def block_out_body(index_ref, *refs):
    pieces, (hidden_ref, middle_ref, vec_ref, out_ref, down_ref, sems) = refs[: 6 * CHUNKS], refs[6 * CHUNKS :]
    step = pl.program_id(0)
    size = down_ref.shape[0] // CHUNKS

    def rest(value):
        out_ref[...] = (middle_ref[...] + row_of(vec_ref, "down_bias") + value).astype(bf16)

    @pl.when(step == 0)
    def _():
        loads = chunk_loads(
            index_ref,
            pieces,
            1,
            lambda chunk, first, count: down_ref.at[pl.ds(chunk * size + first, count), :],
            sems,
        )
        for group in loads:
            for copy in group:
                copy.start()
        total = None
        for chunk, group in enumerate(loads):
            for copy in group:
                copy.wait()
            cols = slice(chunk * size, (chunk + 1) * size)
            term = dot(hidden_ref[:, cols], down_ref[cols, :])
            total = term if total is None else total + term
        rest(total)

    @pl.when(step > 0)
    def _():
        rest(dot(hidden_ref[...], down_ref[...]))


def block_output(index, pieces, hidden, middle, vec, rows_each=256):
    rows, width = middle.shape
    size = hidden.shape[1]

    def by_rows(cols):
        return pl.BlockSpec((rows_each, cols), lambda i, idx: (i, 0))

    return pl.pallas_call(
        block_out_body,
        grid_spec=pltpu.PrefetchScalarGridSpec(
            num_scalar_prefetch=1,
            grid=(rows // rows_each,),
            in_specs=[any_spec] * (6 * CHUNKS) + [by_rows(size), by_rows(width), whole((SHARDS, VEC_LEN))],
            out_specs=by_rows(width),
            scratch_shapes=[pltpu.VMEM((size, width), bf16), pltpu.SemaphoreType.DMA((CHUNKS, 6))],
        ),
        out_shape=jax.ShapeDtypeStruct((rows, width), bf16),
        compiler_params=params(48),
        cost_estimate=cost(2 * rows * width * size, 2 * rows * size + 2 * width * size + 6 * rows * width),
        name="block_output",
    )(index, *pieces, hidden, middle, vec)


def joined_grad_body(index_ref, normed_ref, dq_ref, dk_ref, dv_ref, keep_ref, send_ref, sums_ref):
    step = pl.program_id(0)
    part = dq_ref.shape[1]

    @pl.when(step == 0)
    def _():
        sums_ref[0:1, :] = column_sum(dq_ref[...].astype(f32))
        sums_ref[1:2, :] = column_sum(dv_ref[...].astype(f32))

    for t, k in enumerate((1, 3, 0, 2)):

        @pl.when(step == t)
        def _(t=t, k=k):
            block = keep_ref.shape[2]
            cols = pl.ds(pl.multiple_of((index_ref[0] ^ k) * block, block), block)
            left = normed_ref[:, cols]
            target = send_ref if t < 2 else keep_ref
            for i, ref in enumerate((dq_ref, dk_ref, dv_ref)):
                target[0, i] = dot(left, ref[...], 0, 0).astype(bf16)


def joined_grad(index, normed, d_q, d_k, d_v):
    rows, width = normed.shape
    part = d_q.shape[1]
    grads = (2, 3, width // SHARDS, part)
    unit = (1,) + grads[1:]
    return pl.pallas_call(
        joined_grad_body,
        grid_spec=pltpu.PrefetchScalarGridSpec(
            num_scalar_prefetch=1,
            grid=(SHARDS,),
            in_specs=[whole((rows, width))] + [whole((rows, part))] * 3,
            out_specs=[
                pl.BlockSpec(unit, lambda i, idx: (jnp.maximum(i - 2, 0), 0, 0, 0)),
                pl.BlockSpec(unit, lambda i, idx: (jnp.minimum(i, 1), 0, 0, 0)),
                whole((2, part)),
            ],
        ),
        out_shape=[
            jax.ShapeDtypeStruct(grads, bf16),
            jax.ShapeDtypeStruct(grads, bf16),
            jax.ShapeDtypeStruct((2, part), f32),
        ],
        compiler_params=params(32),
        cost_estimate=cost(6 * rows * width * part, 2 * rows * width + 6 * rows * part + 6 * width * part),
        name="joined_grad",
    )(index, normed, d_q, d_k, d_v)


def input_grad_body(index_ref, *refs, blocks):
    parts, weights = refs[:6], refs[6:8]
    tokens_ref, d_middle_ref, vec_ref, sums_ref, bqv_a_ref, bqv_b_ref = refs[8:14]
    bias_refs = refs[14 : 14 + CHUNKS]
    out_ref, grads_ref, gain_ref, shift_ref = refs[14 + CHUNKS :]
    step = pl.program_id(0)

    @pl.when(step == 0)
    def _():
        gain_ref[...] = jnp.zeros_like(gain_ref)
        shift_ref[...] = jnp.zeros_like(shift_ref)

    d_normed = None
    for half in range(2):
        for i in range(3):
            ref = parts[3 * half + i]
            part = ref.shape[1]
            term = dot(ref[...], weights[half][:, i * part : (i + 1) * part], 1, 1)
            d_normed = term if d_normed is None else d_normed + term
    hat, inverse = norm_parts(tokens_ref[...].astype(f32))
    out_ref[...] = d_middle_ref[...] + norm_back(d_normed, hat, inverse, row_of(vec_ref, "ln1_gain"))
    gain_ref[...] += column_sum(d_normed * hat)
    shift_ref[...] += column_sum(d_normed)

    @pl.when(step == blocks - 1)
    def _():
        def put(name, shard, value, offset=0):
            first = VEC[name][0] + offset
            grads_ref[shard : shard + 1, first : first + value.shape[1]] = value

        for shard in range(SHARDS):
            cols = slice(shard * 256, (shard + 1) * 256)
            put("ln1_gain", shard, gain_ref[:, cols])
            put("ln1_bias", shard, shift_ref[:, cols])
            put("ln2_gain", shard, sums_ref[0:1, cols])
            put("ln2_bias", shard, sums_ref[1:2, cols])
            put("out_bias", shard, sums_ref[2:3, cols])
            put("down_bias", shard, sums_ref[3:4, cols])
            source = bqv_a_ref if shard % 2 == 0 else bqv_b_ref
            put("b_qv", shard, source[shard // 2 : shard // 2 + 1, :])
            for chunk in range(CHUNKS):
                size = bias_refs[chunk].shape[1] // SHARDS
                put("up_bias", shard, bias_refs[chunk][:, shard * size : (shard + 1) * size], chunk * size)


def input_gradient(index, parts, weights, tokens, d_middle, vec, sums, bqv, biases, rows_each=256):
    rows, width = tokens.shape
    part = parts[0].shape[1]
    blocks = rows // rows_each

    def by_rows(cols):
        return pl.BlockSpec((rows_each, cols), lambda i, idx: (i, 0))

    return pl.pallas_call(
        functools.partial(input_grad_body, blocks=blocks),
        grid_spec=pltpu.PrefetchScalarGridSpec(
            num_scalar_prefetch=1,
            grid=(blocks,),
            in_specs=[by_rows(part)] * 6
            + [whole((width, 3 * part))] * 2
            + [by_rows(width), by_rows(width), whole((SHARDS, VEC_LEN)), whole((8, width))]
            + [whole((2, part))] * 2
            + [whole(bias.shape) for bias in biases],
            out_specs=[by_rows(width), whole((SHARDS, VEC_LEN))],
            scratch_shapes=[pltpu.VMEM((1, width), f32), pltpu.VMEM((1, width), f32)],
        ),
        out_shape=[
            jax.ShapeDtypeStruct((rows, width), f32),
            jax.ShapeDtypeStruct((SHARDS, VEC_LEN), f32),
        ],
        compiler_params=params(40),
        cost_estimate=cost(12 * rows * width * part, 10 * rows * width + 12 * rows * part + 12 * width * part),
        name="input_gradient",
    )(index, *parts, *weights, tokens, d_middle, vec, sums, *bqv, *biases)


def place_body(index_ref, pair_ref, other_ref, *refs, plan, fresh):
    outs = len(refs) - 2 if fresh else (len(refs) - 2) // 2
    out_refs = refs[-2 - outs : -2]
    scratch, sems = refs[-2:]
    low, mid = index_ref[1], index_ref[2]
    rows = pair_ref.shape[2]
    for a, ref in enumerate((pair_ref, other_ref)):
        for b in range(2):
            first = pl.multiple_of((low ^ a) * (2 * rows) + (mid ^ b) * rows, rows)
            for u in range(pair_ref.shape[1]):
                scratch[u, pl.ds(first, rows), :] = ref[b, u].astype(f32)
    copies = []
    for i, (unit, cols, width, out, row, col) in enumerate(plan):
        copies.append(
            pltpu.make_async_copy(
                scratch.at[unit, :, cols : cols + width],
                out_refs[out].at[row : row + 4 * rows, col : col + width],
                sems.at[i],
            )
        )
    for copy in copies:
        copy.start()
    for copy in copies:
        copy.wait()


def place(index, pieces, plan, shapes, carried, name):
    pair, other = pieces
    _, units, rows, width = pair.shape
    fresh = carried is None
    count = len(shapes)
    return pl.pallas_call(
        functools.partial(place_body, plan=plan, fresh=fresh),
        grid_spec=pltpu.PrefetchScalarGridSpec(
            num_scalar_prefetch=1,
            grid=(1,),
            in_specs=[whole(pair.shape), whole(other.shape)] + ([] if fresh else [any_spec] * count),
            out_specs=[any_spec] * count,
            scratch_shapes=[pltpu.VMEM((units, 4 * rows, width), f32), pltpu.SemaphoreType.DMA((len(plan),))],
        ),
        out_shape=[jax.ShapeDtypeStruct(shape, f32) for shape in shapes],
        input_output_aliases={} if fresh else {3 + i: i for i in range(count)},
        compiler_params=params(16),
        cost_estimate=cost(units * 4 * rows * width, units * 4 * rows * width * 6),
        name=name,
    )(index, pair, other, *(carried or ()))


def body(
    mesh,
    tokens,
    piece_start,
    ln1_gain,
    ln1_bias,
    query_key_value_weight,
    b_qv,
    attention_out_weight,
    attention_out_bias,
    ln2_gain,
    ln2_bias,
    up_weight,
    up_bias,
    down_weight,
    down_bias,
    cotangent,
):
    count, seq_len, width = tokens.shape
    rows = count * seq_len
    hidden_size = up_weight.shape[1]
    tokens = tokens.reshape(rows, width)
    cot = cotangent.reshape(rows, width)
    moves = Moves(mesh, piece_start)
    half = width // 2
    size = hidden_size // CHUNKS
    block = size // SHARDS

    own_vec = jnp.concatenate(
        [ln1_gain, ln1_bias, b_qv, attention_out_bias, ln2_gain, ln2_bias, up_bias, down_bias]
    ).reshape(1, VEC_LEN)

    def joined_cols(which):
        return jnp.concatenate(
            [
                query_key_value_weight[:, i * width + which * half : i * width + (which + 1) * half]
                for i in range(3)
            ],
            axis=1,
        )

    def hidden_own(chunk):
        up = jnp.concatenate(
            [
                up_weight[:, s * size + chunk * block : s * size + (chunk + 1) * block]
                for s in range(SHARDS)
            ],
            axis=1,
        )
        return jnp.stack([up, down_weight[chunk * block : (chunk + 1) * block, :]])

    far_vec = moves.across(own_vec)
    near_vec = moves.core(own_vec)
    own_a = joined_cols(0)
    far_a = moves.across(after(own_a, far_vec))
    near_a = moves.core(own_a)
    own_b = joined_cols(1)
    half_b = moves.half(own_b)
    hidden_owns = [hidden_own(chunk) for chunk in range(CHUNKS)]
    hidden_halves = [moves.half(own) for own in hidden_owns]
    out_half = moves.half(attention_out_weight)
    far_near_vec = moves.core(far_vec)
    moves.wait(half_b, out_half, *hidden_halves)
    normed, vec = first_norm(moves.index, tokens, (own_vec, near_vec, far_vec, far_near_vec))
    moves.ran(vec)

    joined, joined_weight, attended, totals = [None] * 2, [None] * 2, [None] * 2, [None] * 2
    hidden_far, hidden_near, hidden_other = [None] * CHUNKS, [None] * CHUNKS, [None] * CHUNKS
    hidden_pieces = [None] * CHUNKS

    def fetch(chunk, earlier):
        hidden_far[chunk] = moves.across(after(hidden_halves[chunk], earlier))
        hidden_near[chunk] = moves.core(after(hidden_owns[chunk], earlier))

    def relay(chunk):
        hidden_other[chunk] = moves.rep(hidden_far[chunk], 1)

    far_b = moves.across(after(half_b, far_a))
    near_b = moves.core(after(own_b, far_a))
    joined[0], joined_weight[0] = joined_product(
        0, moves.index, (own_a, near_a, far_a, moves.core(far_a)), normed, vec
    )
    moves.ran(joined[0])
    moves.wait(far_b, near_b)
    other_b = moves.rep(far_b, 1)
    fetch(0, far_b)
    attended[0], totals[0] = attend_forward(0, moves.index, joined[0])
    moves.ran(totals[0])
    moves.wait(hidden_far[0], hidden_near[0])
    relay(0)
    out_far = moves.across(after(out_half, hidden_far[0]))
    out_near = moves.core(after(attention_out_weight, hidden_far[0]))
    joined[1], joined_weight[1] = joined_product(
        1, moves.index, (own_b, near_b, far_b, other_b, moves.core(far_b), moves.core(other_b)), normed, vec
    )
    moves.ran(joined[1])
    moves.wait(out_far, out_near)
    out_other = moves.rep(out_far, 1)
    fetch(1, out_far)
    attended[1], totals[1] = attend_forward(1, moves.index, joined[1])
    moves.ran(totals[1])
    moves.wait(hidden_far[1], hidden_near[1])
    relay(1)
    fetch(2, hidden_far[1])
    middle, normed_two, out_weight = middle_product(
        moves.index,
        (attention_out_weight, out_near, out_far, out_other, moves.core(out_far), moves.core(out_other)),
        attended,
        tokens,
        vec,
    )
    moves.ran(normed_two)

    carried = None
    shard_sums, up_biases = [], []
    for chunk in range(CHUNKS):
        far, other = hidden_far[chunk], hidden_other[chunk]
        hidden_pieces[chunk] = (
            hidden_owns[chunk],
            hidden_near[chunk],
            far,
            other,
            moves.core(far),
            moves.core(other),
        )
        *carried, keep, send, bias = hidden_chunk(
            chunk, moves.index, hidden_pieces[chunk], carried, normed_two, cot, vec, hidden_size
        )
        moves.ran(bias)
        up_biases.append(bias)
        if chunk + 2 < CHUNKS:
            moves.wait(hidden_far[chunk + 2], hidden_near[chunk + 2])
            relay(chunk + 2)
        if chunk + 3 < CHUNKS:
            fetch(chunk + 3, hidden_far[chunk + 2])
        if chunk > 0:
            shard_sums[chunk - 1].cross()
        shard_sums.append(ShardSum(moves, keep, send))
    all_pieces = [piece for pieces in hidden_pieces for piece in pieces]
    hidden, d_pre = carried
    moves.wait(shard_sums[0].got)
    d_middle, d_attended, keep, send, sums = block_back(
        moves.index, all_pieces, d_pre, middle, cot, attended, out_weight, vec
    )
    moves.ran(sums)
    parts, bqv = [], []

    def backward(which):
        grads = attend_backward(which, moves.index, joined[which], attended[which], d_attended, totals[which])
        parts.extend(grads)
        moves.ran(grads[0])

    def joined_grads(which):
        keep, send, bias = joined_grad(moves.index, normed, *parts[3 * which :])
        bqv.append(bias)
        moves.ran(bias)
        return ShardSum(moves, keep, send)

    shard_sums[3].cross()
    out_sum = ShardSum(moves, keep, send)
    moves.wait(shard_sums[1].got)
    first_sum = RepSum(moves, shard_sums[:2])
    backward(0)
    out_sum.cross()
    a_sum = joined_grads(0)
    first_sum.split()
    moves.wait(shard_sums[2].got)
    second_sum = RepSum(moves, shard_sums[2:3])
    backward(1)
    a_sum.cross()
    first_sum.add()
    b_sum = joined_grads(1)
    moves.wait(shard_sums[3].got)
    third_sum = RepSum(moves, shard_sums[3:4])
    second_sum.split()
    first_sum.spread()
    input_grad, vec_grads = input_gradient(
        moves.index, parts, joined_weight, tokens, d_middle, vec, sums, bqv, up_biases
    )
    moves.ran(vec_grads)
    b_sum.cross()
    first_sum.finish()
    second_sum.add()
    third_sum.split()
    moves.wait(out_sum.got, a_sum.got)
    fourth_sum = RepSum(moves, [out_sum, a_sum])
    block_out = block_output(moves.index, all_pieces, hidden, middle, vec)
    moves.ran(block_out)
    second_sum.spread()
    third_sum.add()
    fourth_sum.split()
    last_sum = RepSum(moves, [b_sum])

    def place_hidden(chunks, pieces, grads, name):
        plan = []
        for i, chunk in enumerate(chunks):
            plan += [(2 * i, s * block, block, 0, 0, s * size + chunk * block) for s in range(SHARDS)]
            plan += [(2 * i + 1, 0, width, 1, chunk * block, 0)]
        shapes = [(width // SHARDS, hidden_size), (size, width)]
        return place(moves.index, pieces, plan, shapes, grads, name)

    grads = place_hidden((0, 1), first_sum.pieces(), None, "place_hidden_first")
    moves.ran(grads[0])
    second_sum.finish()
    third_sum.spread()
    fourth_sum.add()
    last_sum.split()
    vec_sum = moves.reduce_vec(vec_grads).reshape(VEC_LEN)
    grads = place_hidden((2,), second_sum.pieces(), grads, "place_hidden_second")
    moves.ran(grads[0])
    third_sum.finish()
    fourth_sum.spread()
    last_sum.add()
    grad_up, grad_down = place_hidden((3,), third_sum.pieces(), grads, "place_hidden_third")
    moves.ran(grad_up)
    fourth_sum.finish()
    last_sum.spread()
    last_sum.finish()
    third = width // SHARDS
    plan = [(i, 0, half, 0, 0, i * half) for i in range(2)]
    plan += [(2 + i, 0, half, 1, 0, i * width) for i in range(3)]
    shapes = [(third, width), (third, 3 * width)]
    grad_out, grad_joined = place(moves.index, fourth_sum.pieces(), plan, shapes, None, "place_fourth")
    plan = [(i, 0, half, 0, 0, i * width + half) for i in range(3)]
    (grad_joined,) = place(moves.index, last_sum.pieces(), plan, shapes[1:], (grad_joined,), "place_last")

    def vec_part(name):
        first, length = VEC[name]
        return vec_sum[first : first + length]

    return (
        block_out.reshape(count, seq_len, width),
        input_grad.reshape(count, seq_len, width),
        vec_part("ln1_gain"),
        vec_part("ln1_bias"),
        grad_joined,
        vec_part("b_qv"),
        grad_out,
        vec_part("out_bias"),
        vec_part("ln2_gain"),
        vec_part("ln2_bias"),
        grad_up,
        vec_part("up_bias"),
        grad_down,
        vec_part("down_bias"),
    )


def solution(mesh):
    batch = P(("shard", "rep"), None, None)
    vector, matrix = P("shard"), P("shard", None)
    in_specs = (
        batch,
        P(("shard", "rep")),
        vector,
        vector,
        matrix,
        vector,
        matrix,
        vector,
        vector,
        vector,
        matrix,
        vector,
        matrix,
        vector,
        batch,
    )
    out_specs = (
        batch,
        batch,
        vector,
        vector,
        matrix,
        vector,
        matrix,
        vector,
        vector,
        vector,
        matrix,
        vector,
        matrix,
        vector,
    )
    return jax.shard_map(
        functools.partial(body, mesh), mesh=mesh, in_specs=in_specs, out_specs=out_specs, check_vma=False
    )
```

```python
import functools

import jax
import jax.numpy as jnp
from jax import lax
from jax.experimental import pallas as pl
from jax.experimental.pallas import tpu as pltpu
from jax.sharding import PartitionSpec as P

HEADS = 16
PIECE = 256
HEAD_DIM = 64
PAIR = 2 * HEAD_DIM
SHARDS = 4
CHUNKS = 4
EPS = 1e-05
HIDDEN_PENALTY = 1e33

bf16 = jnp.bfloat16
f32 = jnp.float32

VEC = {
    "ln1_gain": (0, 1),
    "ln1_bias": (1, 1),
    "b_qv": (2, 2),
    "out_bias": (4, 1),
    "ln2_gain": (5, 1),
    "ln2_bias": (6, 1),
    "up_bias": (7, 4),
    "down_bias": (11, 1),
}
VEC_ROWS = 16
LANES = 256

any_spec = pl.BlockSpec(memory_space=pltpu.MemorySpace.HBM)


def dot(left, right, left_dim=1, right_dim=0):
    return lax.dot_general(
        left, right, (((left_dim,), (right_dim,)), ((), ())), preferred_element_type=f32
    )


def params(mib):
    return pltpu.CompilerParams(vmem_limit_bytes=int(mib * 2**20))


def cost(flops, moved, transcendentals=0, scale=4):
    return pl.CostEstimate(
        flops=int(scale * flops), bytes_accessed=int(scale * moved), transcendentals=int(scale * transcendentals)
    )


def vec_rows(vec_ref, rows):
    firsts = [shard * VEC_ROWS + row for shard, row in rows]
    return jnp.concatenate([vec_ref[first : first + 1, :] for first in firsts], axis=1)


def row_of(vec_ref, name):
    return vec_rows(vec_ref, [(shard, VEC[name][0]) for shard in range(SHARDS)])


def whole(shape):
    return pl.BlockSpec(shape, lambda *_: (0,) * len(shape))


def flip(value, axis, size, bit):
    return lax.ppermute(value, axis, [(i, i ^ bit) for i in range(size)])


class Moves:
    def __init__(self, mesh, starts):
        self.reps = mesh.shape["rep"]
        assert mesh.shape["shard"] == SHARDS and self.reps % 4 == 0
        self.shard = lax.axis_index("shard")
        rep = lax.axis_index("rep")
        self.low = rep & 1
        self.mid = (rep >> 1) & 1
        self.index = jnp.concatenate(
            [jnp.stack([self.shard, self.low, self.mid]).astype(jnp.int32), starts]
        )
        self.last = ()
        self.count = 0
        self.due = []

    def wait(self, *values):
        self.index = after(self.index, *values, *self.last)

    def by(self, kernels, *values):
        self.due.append((self.count + kernels, values))

    def ran(self, value):
        self.last = (value,)
        self.count += 1
        ready = [value for when, values in self.due if when <= self.count for value in values]
        self.due = [entry for entry in self.due if entry[0] > self.count]
        self.wait(*ready)
        return value

    def move(self, value, axis, size, bit):
        return flip(after(value, *self.last), axis, size, bit)

    def core(self, value):
        return self.move(value, "shard", SHARDS, 1)

    def across(self, value):
        return self.move(value, "shard", SHARDS, 2)

    def rep(self, value, bit):
        return self.move(value, "rep", self.reps, bit)

    def half(self, own):
        rows = own.shape[-2] // 2
        return lax.dynamic_slice_in_dim(own, self.low * rows, rows, own.ndim - 2)

    def pick(self, value, which, size):
        return lax.dynamic_slice_in_dim(value, which * size, size, 1)


def after(value, *earlier):
    return lax.optimization_barrier((value, *earlier))[0] if earlier else value


class ShardSum:
    def __init__(self, moves, keep, send, kernels=1):
        self.moves, self.keep = moves, keep
        self.got = moves.core(send)
        moves.by(kernels, self.got)

    def cross(self, kernels):
        self.got = after(self.got, *self.moves.last)
        out = self.keep[1] + self.got[1]
        self.mine = self.keep[0] + self.got[0]
        self.moves.wait(out, self.mine)
        self.got = self.moves.across(out)
        self.moves.by(kernels, self.got)

    def halves(self):
        moves, mine = self.moves, self.mine
        got = after(self.got, *moves.last)
        size = mine.shape[1] // 2
        return [
            moves.pick(mine, which, size) + moves.pick(got, which, size)
            for which in (moves.low, 1 - moves.low)
        ]


class RepSum:
    def __init__(self, moves, sums, kernels=1):
        self.moves = moves
        halves = [s.halves() for s in sums]
        self.mine = jnp.concatenate([h[0] for h in halves])
        self.bit = 2
        self.send(jnp.concatenate([h[1] for h in halves]), 1, kernels)

    def send(self, out, bit, kernels):
        self.moves.wait(out, self.mine)
        self.got = self.moves.rep(out, bit)
        self.moves.by(kernels, self.got)

    def split(self, kernels=1):
        moves = self.moves
        got = after(self.got, *moves.last)
        size = self.mine.shape[1] // 2
        out, self.mine = [
            moves.pick(self.mine, which, size) + moves.pick(got, which, size)
            for which in (1 - moves.mid, moves.mid)
        ]
        self.send(out, 2, kernels)

    def add(self, kernels=1):
        self.mine = self.mine + after(self.got, *self.moves.last)
        self.bit *= 2
        self.got = None
        if self.bit < self.moves.reps:
            self.send(self.mine, self.bit, kernels)

    def spread(self, kernels=1):
        while self.got is not None:
            self.add()
        self.send(self.mine, 2, kernels)

    def finish(self, kernels=1):
        self.pair = jnp.stack([self.mine, after(self.got, *self.moves.last)])
        self.send(self.pair, 1, kernels)

    def pieces(self):
        self.moves.wait(self.got)
        return (self.pair, self.got)


class VecSum:
    def __init__(self, moves, value):
        self.moves, self.value = moves, value
        self.plan = [moves.core, moves.across]
        bit = 1
        while bit < moves.reps:
            self.plan.append(functools.partial(moves.rep, bit=bit))
            bit *= 2
        self.at = 0
        self.send()

    def send(self):
        self.got = self.plan[self.at](self.value)
        self.moves.by(1, self.got)
        self.at += 1

    def step(self):
        moves = self.moves
        self.value = self.value + after(self.got, *moves.last)
        if self.at == 2:
            self.value = lax.dynamic_slice_in_dim(self.value, moves.shard * VEC_ROWS, VEC_ROWS, 0)
        moves.wait(self.value)
        if self.at < len(self.plan):
            self.send()

    def rest(self):
        while self.at < len(self.plan):
            self.step()
        self.step()
        return self.value


def piece_copies(index_ref, pieces, target, sems):
    shard, low = index_ref[0], index_ref[1]
    rows = pieces[0].shape[-2]
    if len(pieces) == 4:
        plan = [(piece, shard ^ k, 0, rows) for k, piece in enumerate(pieces)]
    else:
        own, near, far, far_other, far_near, far_other_near = pieces
        half = rows // 2
        plan = (
            (own, shard, 0, rows),
            (near, shard ^ 1, 0, rows),
            (far, shard ^ 2, low * half, half),
            (far_other, shard ^ 2, (1 - low) * half, half),
            (far_near, shard ^ 3, low * half, half),
            (far_other_near, shard ^ 3, (1 - low) * half, half),
        )
    return [
        pltpu.make_async_copy(source, target(to, first, count), sems.at[i])
        for i, (source, to, first, count) in enumerate(plan)
    ]


def norm_parts(value):
    center = value - jnp.mean(value, axis=-1, keepdims=True)
    inverse = lax.rsqrt(jnp.mean(center * center, axis=-1, keepdims=True) + EPS)
    return center * inverse, inverse


def first_norm_body(index_ref, tokens_ref, own_ref, near_ref, far_ref, far_near_ref, normed_ref, vec_ref):
    shard = index_ref[0]

    @pl.when(pl.program_id(0) == 0)
    def _():
        for k, ref in enumerate((own_ref, near_ref, far_ref, far_near_ref)):
            vec_ref[pl.ds(pl.multiple_of((shard ^ k) * VEC_ROWS, VEC_ROWS), VEC_ROWS), :] = ref[...].astype(f32)

    hat, _ = norm_parts(tokens_ref[...].astype(f32))
    normed_ref[...] = (hat * row_of(vec_ref, "ln1_gain") + row_of(vec_ref, "ln1_bias")).astype(bf16)


def first_norm(index, tokens, vec_pieces, block=256):
    rows, width = tokens.shape
    row = pl.BlockSpec((block, width), lambda i, idx: (i, 0))
    return pl.pallas_call(
        first_norm_body,
        grid_spec=pltpu.PrefetchScalarGridSpec(
            num_scalar_prefetch=1,
            grid=(rows // block,),
            in_specs=[row] + [whole((VEC_ROWS, LANES))] * 4,
            out_specs=[row, whole((SHARDS * VEC_ROWS, LANES))],
        ),
        out_shape=[
            jax.ShapeDtypeStruct((rows, width), bf16),
            jax.ShapeDtypeStruct((SHARDS * VEC_ROWS, LANES), f32),
        ],
        compiler_params=params(16),
        cost_estimate=cost(20 * rows * width, 4 * rows * width),
        name="first_norm",
    )(index, tokens, *vec_pieces)


def joined_body(half, index_ref, *refs):
    pieces, (normed_ref, vec_ref, out_ref, weight_ref, sems) = refs[:-5], refs[-5:]

    @pl.when(pl.program_id(0) == 0)
    def _():
        rows = pieces[0].shape[0]
        copies = piece_copies(
            index_ref,
            pieces,
            lambda to, first, count: weight_ref.at[
                pl.ds(pl.multiple_of(to * rows + first, 128), count), :
            ],
            sems,
        )
        for copy in copies:
            copy.start()
        for copy in copies:
            copy.wait()

    part = weight_ref.shape[1] // 3
    first = VEC["b_qv"][0]
    normed = normed_ref[...]
    for i in range(3):
        cols = slice(i * part, (i + 1) * part)
        value = dot(normed, weight_ref[:, cols])
        if i != 1:
            shard = half if i == 0 else 2 + half
            value = value + vec_rows(vec_ref, [(shard, first), (shard, first + 1)])
        out_ref[:, cols] = value.astype(bf16)


def joined_product(half, index, pieces, normed, vec, block=256):
    rows, width = normed.shape
    cols = pieces[0].shape[1]
    return pl.pallas_call(
        functools.partial(joined_body, half),
        grid_spec=pltpu.PrefetchScalarGridSpec(
            num_scalar_prefetch=1,
            grid=(rows // block,),
            in_specs=[any_spec] * len(pieces)
            + [pl.BlockSpec((block, width), lambda i, idx: (i, 0)), whole((SHARDS * VEC_ROWS, LANES))],
            out_specs=[pl.BlockSpec((block, cols), lambda i, idx: (i, 0)), whole((width, cols))],
            scratch_shapes=[pltpu.SemaphoreType.DMA((6,))],
        ),
        out_shape=[
            jax.ShapeDtypeStruct((rows, cols), bf16),
            jax.ShapeDtypeStruct((width, cols), bf16),
        ],
        compiler_params=params(24),
        cost_estimate=cost(2 * rows * width * cols, 2 * (rows * width + rows * cols + 2 * width * cols)),
        name="joined_product",
    )(index, *pieces, normed, vec)


def penalty(start, seq_len):
    key = lax.broadcasted_iota(jnp.int32, (seq_len, seq_len), 0)
    query = lax.broadcasted_iota(jnp.int32, (seq_len, seq_len), 1)
    key_in = (key >= start) & (key < start + PIECE)
    query_in = (query >= start) & (query < start + PIECE)
    seen = (key <= query) | (key_in & query_in)
    return jnp.where(seen, jnp.abs(key - query).astype(f32), HIDDEN_PENALTY)


def slope_of(head):
    return jnp.exp2((jnp.full((1, 1), head, jnp.int32).astype(f32) + 1.0) * (-8.0 / HEADS))


def attend_forward_body(first_head, start_ref, q_ref, k_ref, v_ref, out_ref, total_ref, pen_ref):
    pair = pl.program_id(1)
    seq_len = q_ref.shape[0]

    @pl.when(pair == 0)
    def _():
        pen_ref[...] = penalty(start_ref[3 + pl.program_id(0)], seq_len)

    queries, keys = q_ref[...], k_ref[...]
    values_t = v_ref[...].T
    lane = lax.broadcasted_iota(jnp.int32, (seq_len, PAIR), 1)
    outs = []
    for e in range(2):
        chosen = (lane < HEAD_DIM) if e == 0 else (lane >= HEAD_DIM)
        key_e = jnp.where(chosen, keys * (HEAD_DIM**-0.5), 0).astype(bf16)
        scores = dot(key_e, queries, 1, 1) - slope_of(first_head + 2 * pair + e) * pen_ref[...]
        top = jnp.max(scores, axis=0, keepdims=True)
        weight = jnp.exp(scores - top)
        total = jnp.sum(weight, axis=0, keepdims=True)
        out_t = dot(values_t[e * HEAD_DIM : (e + 1) * HEAD_DIM, :], weight.astype(bf16))
        outs.append(out_t * (1.0 / total))
        total_ref[0, 0, e : e + 1, :] = top + jnp.log(total)
    out_ref[...] = jnp.concatenate(outs, axis=0).T.astype(bf16)


def attend_forward(half, index, joined):
    count = index.shape[0] - 3
    seq_len, width = joined.shape[0] // count, joined.shape[1] // 3
    pairs = width // PAIR

    def cols(first):
        return pl.BlockSpec((seq_len, PAIR), lambda s, h, st: (s, first + h))

    return pl.pallas_call(
        functools.partial(attend_forward_body, half * 2 * pairs),
        grid_spec=pltpu.PrefetchScalarGridSpec(
            num_scalar_prefetch=1,
            grid=(count, pairs),
            in_specs=[cols(0), cols(pairs), cols(2 * pairs)],
            out_specs=[cols(0), pl.BlockSpec((1, 1, 2, seq_len), lambda s, h, st: (s, h, 0, 0))],
            scratch_shapes=[pltpu.VMEM((seq_len, seq_len), f32)],
        ),
        out_shape=[
            jax.ShapeDtypeStruct((count * seq_len, width), bf16),
            jax.ShapeDtypeStruct((count, pairs, 2, seq_len), f32),
        ],
        compiler_params=params(24),
        cost_estimate=cost(
            24 * count * seq_len * seq_len * width, 8 * count * seq_len * width, count * seq_len * seq_len * 2 * pairs
        ),
        name="attend_forward",
    )(index, joined, joined, joined)


def attend_backward_body(
    first_head,
    steps,
    index_ref,
    q_ref,
    k_ref,
    v_ref,
    out_ref,
    dout_ref,
    total_ref,
    normed_ref,
    dq_ref,
    dk_ref,
    dv_ref,
    keep_ref,
    send_ref,
    sums_ref,
    pen_ref,
):
    step = pl.program_id(0)
    seq_len = q_ref.shape[0]
    scale = HEAD_DIM**-0.5
    pairs = dq_ref.shape[1] // PAIR
    seq, pair = step // pairs, step % pairs

    @pl.when((step < steps) & (pair == 0))
    def _():
        pen_ref[...] = penalty(index_ref[3 + seq], seq_len)

    @pl.when(step < steps)
    def _():
        queries, keys, values, d_out = q_ref[...], k_ref[...], v_ref[...], dout_ref[...]
        lane = lax.broadcasted_iota(jnp.int32, (seq_len, PAIR), 1)
        keys_t = keys.T
        both_t = (d_out.astype(f32) * out_ref[...].astype(f32)).T
        d_q, d_k, d_v = [], [], []
        for e in range(2):
            chosen = (lane < HEAD_DIM) if e == 0 else (lane >= HEAD_DIM)
            part = slice(e * HEAD_DIM, (e + 1) * HEAD_DIM)
            key_e = jnp.where(chosen, keys * scale, 0).astype(bf16)
            value_e = jnp.where(chosen, values, 0)
            inner = jnp.sum(both_t[part, :], axis=0, keepdims=True)
            scores = dot(key_e, queries, 1, 1) - slope_of(first_head + 2 * pair + e) * pen_ref[...]
            probs = jnp.exp(scores - total_ref[0, 0, e : e + 1, :])
            d_scores = (probs * (dot(value_e, d_out, 1, 1) - inner)).astype(bf16)
            d_v.append(dot(probs.astype(bf16), d_out))
            d_k.append(dot(d_scores, queries))
            d_q.append(dot(keys_t[part, :], d_scores))
        rows = pl.ds(pl.multiple_of(seq * seq_len, seq_len), seq_len)
        cols = pl.ds(pl.multiple_of(pair * PAIR, PAIR), PAIR)
        dq_ref[rows, cols] = (jnp.concatenate(d_q, axis=0) * scale).T.astype(bf16)
        dk_ref[rows, cols] = (jnp.where(lane < HEAD_DIM, d_k[0], d_k[1]) * scale).astype(bf16)
        dv_ref[rows, cols] = jnp.where(lane < HEAD_DIM, d_v[0], d_v[1]).astype(bf16)

    @pl.when(step == steps)
    def _():
        sums_ref[0:1, :] = column_sum(dq_ref[...].astype(f32))
        sums_ref[1:2, :] = column_sum(dv_ref[...].astype(f32))

    @pl.when(step >= steps)
    def _():
        block = keep_ref.shape[2]
        t = step - steps
        k = jnp.where(t < 2, 2 * t + 1, 2 * t - 4)
        left = normed_ref[:, pl.ds(pl.multiple_of((index_ref[0] ^ k) * block, block), block)]
        for i, ref in enumerate((dq_ref, dk_ref, dv_ref)):
            value = dot(left, ref[...], 0, 0).astype(bf16)

            @pl.when(t < 2)
            def _(i=i, value=value):
                send_ref[0, i] = value

            @pl.when(t >= 2)
            def _(i=i, value=value):
                keep_ref[0, i] = value


def attend_backward(half, index, joined, attended, d_attended, totals, normed):
    count = index.shape[0] - 3
    rows, width = joined.shape[0], joined.shape[1] // 3
    seq_len = rows // count
    pairs = width // PAIR
    steps = count * pairs
    model = normed.shape[1]

    def cols(first):
        def where(i, idx):
            at = jnp.minimum(i, steps - 1)
            return (at // pairs, first + at % pairs)

        return pl.BlockSpec((seq_len, PAIR), where)

    def totals_at(i, idx):
        at = jnp.minimum(i, steps - 1)
        return (at // pairs, at % pairs, 0, 0)

    grads = (2, 3, model // SHARDS, width)
    unit = (1,) + grads[1:]
    return pl.pallas_call(
        functools.partial(attend_backward_body, half * 2 * pairs, steps),
        grid_spec=pltpu.PrefetchScalarGridSpec(
            num_scalar_prefetch=1,
            grid=(steps + SHARDS,),
            in_specs=[
                cols(0),
                cols(pairs),
                cols(2 * pairs),
                cols(0),
                cols(half * pairs),
                pl.BlockSpec((1, 1, 2, seq_len), totals_at),
                whole((rows, model)),
            ],
            out_specs=[whole((rows, width))] * 3
            + [
                pl.BlockSpec(unit, lambda i, idx: (jnp.clip(i - steps - 2, 0, 1), 0, 0, 0)),
                pl.BlockSpec(unit, lambda i, idx: (jnp.clip(i - steps, 0, 1), 0, 0, 0)),
                whole((2, width)),
            ],
            scratch_shapes=[pltpu.VMEM((seq_len, seq_len), f32)],
        ),
        out_shape=[jax.ShapeDtypeStruct((rows, width), bf16)] * 3
        + [
            jax.ShapeDtypeStruct(grads, bf16),
            jax.ShapeDtypeStruct(grads, bf16),
            jax.ShapeDtypeStruct((2, width), f32),
        ],
        compiler_params=params(40),
        cost_estimate=cost(
            36 * rows * seq_len * width + 6 * rows * model * width, 16 * rows * width, rows * seq_len * 2 * pairs
        ),
        name="attend_backward",
    )(index, joined, joined, joined, attended, d_attended, totals, normed)


def middle_body(index_ref, *refs):
    pieces, (a_ref, b_ref, tokens_ref, vec_ref, middle_ref, normed_ref, weight_ref, sems) = refs[:6], refs[6:]

    @pl.when(pl.program_id(0) == 0)
    def _():
        rows = pieces[0].shape[0]
        copies = piece_copies(
            index_ref,
            pieces,
            lambda to, first, count: weight_ref.at[
                pl.ds(pl.multiple_of(to * rows + first, 128), count), :
            ],
            sems,
        )
        for copy in copies:
            copy.start()
        for copy in copies:
            copy.wait()

    part = a_ref.shape[1]
    middle = tokens_ref[...].astype(f32) + row_of(vec_ref, "out_bias")
    middle = middle + dot(a_ref[...], weight_ref[:part, :]) + dot(b_ref[...], weight_ref[part:, :])
    middle_ref[...] = middle
    hat, _ = norm_parts(middle)
    normed_ref[...] = (hat * row_of(vec_ref, "ln2_gain") + row_of(vec_ref, "ln2_bias")).astype(bf16)


def middle_product(index, pieces, attended, tokens, vec, block=256):
    rows, width = tokens.shape
    row = pl.BlockSpec((block, width), lambda i, idx: (i, 0))
    part = pl.BlockSpec((block, attended[0].shape[1]), lambda i, idx: (i, 0))
    return pl.pallas_call(
        middle_body,
        grid_spec=pltpu.PrefetchScalarGridSpec(
            num_scalar_prefetch=1,
            grid=(rows // block,),
            in_specs=[any_spec] * 6 + [part, part, row, whole((SHARDS * VEC_ROWS, LANES))],
            out_specs=[row, row, whole((width, width))],
            scratch_shapes=[pltpu.SemaphoreType.DMA((6,))],
        ),
        out_shape=[
            jax.ShapeDtypeStruct((rows, width), f32),
            jax.ShapeDtypeStruct((rows, width), bf16),
            jax.ShapeDtypeStruct((width, width), bf16),
        ],
        compiler_params=params(24),
        cost_estimate=cost(2 * rows * width * width, 10 * rows * width + 4 * width * width),
        name="middle_product",
    )(index, *pieces, *attended, tokens, vec)


def gelu_and_slope(pre):
    cube = 0.044715 * pre * pre
    inner = jnp.tanh(0.7978845608028654 * (pre + cube * pre))
    half = 0.5 * (1.0 + inner)
    slope = half + 0.5 * pre * (1.0 - inner * inner) * (0.7978845608028654 * (1.0 + 3.0 * cube))
    return pre * half, slope


def hidden_body(chunk, fresh, index_ref, *refs):
    pieces, refs = refs[:6], refs[6:]
    if not fresh:
        refs = refs[2:]
    normed_hbm, cot_hbm, vec_ref = refs[:3]
    hidden_out, pre_out, keep_ref, send_ref, bias_ref = refs[3:8]
    normed_ref, cot_ref, up_ref, down_ref, hidden_ref, pre_ref, slope_ref, sems, whole_sems = refs[8:]
    step = pl.program_id(0)
    shard = index_ref[0]
    block = 256

    def loads():
        def rows_of(ref, unit):
            rows = pieces[0].shape[1]
            return piece_copies(
                index_ref,
                [piece.at[unit] for piece in pieces],
                lambda to, first, count: ref.at[pl.ds(pl.multiple_of(to * rows + first, 128), count), :],
                sems.at[unit],
            )

        first = [pltpu.make_async_copy(normed_hbm, normed_ref, whole_sems.at[0])] + rows_of(up_ref, 0)
        second = [pltpu.make_async_copy(cot_hbm, cot_ref, whole_sems.at[1])] + rows_of(down_ref, 1)
        return first, second

    def stores():
        cols = pl.ds(chunk * hidden_ref.shape[1], hidden_ref.shape[1])
        return (
            pltpu.make_async_copy(hidden_ref, hidden_out.at[:, cols], whole_sems.at[2]),
            pltpu.make_async_copy(pre_ref, pre_out.at[:, cols], whole_sems.at[3]),
        )

    @pl.when(step == 0)
    def _():
        first, second = loads()
        for copy in first + second:
            copy.start()
        for copy in first:
            copy.wait()

    @pl.when(step == 1)
    def _():
        for copy in loads()[1]:
            copy.wait()

    rows_each = 256
    count = normed_ref.shape[0] // rows_each

    @pl.when(step == 0)
    def _():
        bias = vec_rows(vec_ref, [(one, VEC["up_bias"][0] + chunk) for one in range(SHARDS)])
        for m in range(count):
            rows = slice(m * rows_each, (m + 1) * rows_each)
            value, slope = gelu_and_slope(dot(normed_ref[rows, :], up_ref[...]) + bias)
            value = value.astype(bf16)
            hidden_ref[rows, :] = value
            slope_ref[rows, :] = slope
        stores()[0].start()

    @pl.when(step == 1)
    def _():
        sums = jnp.zeros(bias_ref.shape, f32)
        for m in range(count):
            rows = slice(m * rows_each, (m + 1) * rows_each)
            d_pre = (dot(cot_ref[rows, :], down_ref[...], 1, 1) * slope_ref[rows, :]).astype(bf16)
            pre_ref[rows, :] = d_pre
            sums = sums + jnp.sum(d_pre.astype(f32), axis=0, keepdims=True)
        bias_ref[...] = sums
        stores()[1].start()

    @pl.when(step >= 2)
    def _():
        k = jnp.where(step < 4, 2 * (step - 2) + 1, 2 * (step - 4))
        cols = pl.ds(pl.multiple_of((shard ^ k) * block, block), block)
        left, right = normed_ref[:, cols], hidden_ref[:, cols]
        one = dot(left, pre_ref[...], 0, 0).astype(bf16)
        two = dot(right, cot_ref[...], 0, 0).astype(bf16)

        @pl.when(step < 4)
        def _():
            send_ref[0, 0] = one
            send_ref[0, 1] = two

        @pl.when(step >= 4)
        def _():
            keep_ref[0, 0] = one
            keep_ref[0, 1] = two

    @pl.when(step == 5)
    def _():
        for copy in stores():
            copy.wait()


def hidden_chunk(chunk, index, pieces, carried, normed, cot, vec, hidden_size):
    rows, width = normed.shape
    size = hidden_size // CHUNKS
    fresh = carried is None
    grads = (2, 2, width // SHARDS, size)
    outs = [
        jax.ShapeDtypeStruct((rows, hidden_size), bf16),
        jax.ShapeDtypeStruct((rows, hidden_size), bf16),
        jax.ShapeDtypeStruct(grads, bf16),
        jax.ShapeDtypeStruct(grads, bf16),
        jax.ShapeDtypeStruct((1, size), f32),
    ]
    unit = (1,) + grads[1:]
    return pl.pallas_call(
        functools.partial(hidden_body, chunk, fresh),
        grid_spec=pltpu.PrefetchScalarGridSpec(
            num_scalar_prefetch=1,
            grid=(6,),
            in_specs=[any_spec] * (8 if fresh else 10) + [whole((SHARDS * VEC_ROWS, LANES))],
            out_specs=[
                any_spec,
                any_spec,
                pl.BlockSpec(unit, lambda i, idx: (jnp.maximum(i - 4, 0), 0, 0, 0)),
                pl.BlockSpec(unit, lambda i, idx: (jnp.clip(i - 2, 0, 1), 0, 0, 0)),
                pl.BlockSpec((1, size), lambda i, idx: (0, 0)),
            ],
            scratch_shapes=[
                pltpu.VMEM((rows, width), bf16),
                pltpu.VMEM((rows, width), bf16),
                pltpu.VMEM((width, size), bf16),
                pltpu.VMEM((size, width), bf16),
                pltpu.VMEM((rows, size), bf16),
                pltpu.VMEM((rows, size), bf16),
                pltpu.VMEM((rows, size), f32),
                pltpu.SemaphoreType.DMA((2, 6)),
                pltpu.SemaphoreType.DMA((4,)),
            ],
        ),
        out_shape=outs,
        input_output_aliases={} if fresh else {7: 0, 8: 1},
        compiler_params=params(48),
        cost_estimate=cost(8 * rows * width * size, 8 * rows * width + 16 * rows * size, rows * size),
        name=f"hidden_chunk{chunk}",
    )(index, *pieces, *(carried or ()), normed, cot, vec)


def norm_back(d_normed, hat, inverse, gain):
    scaled = d_normed * gain
    return inverse * (
        scaled
        - jnp.mean(scaled, axis=-1, keepdims=True)
        - hat * jnp.mean(scaled * hat, axis=-1, keepdims=True)
    )


def column_sum(value):
    return jnp.sum(value, axis=0, keepdims=True)


def chunk_loads(index_ref, pieces, unit, target, sems):
    loads = []
    for chunk in range(CHUNKS):
        group = pieces[6 * chunk : 6 * chunk + 6]
        rows = group[0].shape[1]
        loads.append(
            piece_copies(
                index_ref,
                [piece.at[unit] for piece in group],
                lambda to, first, count, chunk=chunk: target(
                    chunk, pl.multiple_of(to * rows + first, 128), count
                ),
                sems.at[chunk],
            )
        )
    return loads


def block_back_body(index_ref, *refs, blocks):
    pieces, refs = refs[: 6 * CHUNKS], refs[6 * CHUNKS :]
    pre_ref, middle_ref, cot_ref, a_ref, b_ref, weight_ref, vec_ref = refs[:7]
    d_middle_ref, d_attended_ref, keep_ref, send_ref, sums_ref = refs[7:12]
    up_ref, d_one_ref, sems = refs[12:]
    step = pl.program_id(0)
    rows = pre_ref.shape[0]
    size = up_ref.shape[1] // CHUNKS

    def rest(d_normed):
        middle = middle_ref[...]
        cot = cot_ref[...].astype(f32)
        hat, inverse = norm_parts(middle)
        d_middle = cot + norm_back(d_normed, hat, inverse, row_of(vec_ref, "ln2_gain"))
        d_one = d_middle.astype(bf16)
        d_middle_ref[...] = d_middle
        d_one_ref[pl.ds(pl.multiple_of(step * rows, rows), rows), :] = d_one
        sums_ref[0:1, :] += column_sum(d_normed * hat)
        sums_ref[1:2, :] += column_sum(d_normed)
        sums_ref[2:3, :] += column_sum(d_one.astype(f32))
        sums_ref[3:4, :] += column_sum(cot)

    @pl.when(step == 0)
    def _():
        loads = chunk_loads(
            index_ref,
            pieces,
            0,
            lambda chunk, first, count: up_ref.at[pl.ds(first, count), chunk * size : (chunk + 1) * size],
            sems,
        )
        for group in loads:
            for copy in group:
                copy.start()
        sums_ref[...] = jnp.zeros_like(sums_ref)
        d_normed = None
        for chunk, group in enumerate(loads):
            for copy in group:
                copy.wait()
            cols = slice(chunk * size, (chunk + 1) * size)
            term = dot(pre_ref[:, cols], up_ref[:, cols], 1, 1)
            d_normed = term if d_normed is None else d_normed + term
        rest(d_normed)

    @pl.when((step > 0) & (step < blocks))
    def _():
        rest(dot(pre_ref[...], up_ref[...], 1, 1))

    for t, k in enumerate((1, 3, 0, 2)):

        @pl.when(step == blocks + t)
        def _(t=t, k=k):
            block = weight_ref.shape[0] // SHARDS
            part = keep_ref.shape[3]
            d_one = d_one_ref[...]
            d_attended_ref[...] = dot(d_one, weight_ref[t * block : (t + 1) * block, :], 1, 1).astype(bf16)
            shard = index_ref[0] ^ k
            target = send_ref if t < 2 else keep_ref
            cols = pl.ds(pl.multiple_of((shard & 1) * block, block), block)

            def put(ref):
                value = dot(ref[:, cols], d_one, 0, 0).astype(bf16)
                for unit in range(2):
                    target[0, unit] = value[:, unit * part : (unit + 1) * part]

            pl.when(shard < 2)(lambda: put(a_ref))
            pl.when(shard >= 2)(lambda: put(b_ref))


def block_back(index, pieces, d_pre, middle, cot, attended, weight, vec, rows_each=256):
    rows, width = middle.shape
    size = d_pre.shape[1]
    blocks = rows // rows_each
    quarter = width // SHARDS

    def by_rows(cols):
        return pl.BlockSpec((rows_each, cols), lambda i, idx: (jnp.minimum(i, blocks - 1), 0))

    grads = (2, 2, quarter, width // 2)
    unit = (1,) + grads[1:]
    half = whole((rows, attended[0].shape[1]))
    return pl.pallas_call(
        functools.partial(block_back_body, blocks=blocks),
        grid_spec=pltpu.PrefetchScalarGridSpec(
            num_scalar_prefetch=1,
            grid=(blocks + SHARDS,),
            in_specs=[any_spec] * (6 * CHUNKS)
            + [
                by_rows(size),
                by_rows(width),
                by_rows(width),
                half,
                half,
                whole((width, width)),
                whole((SHARDS * VEC_ROWS, LANES)),
            ],
            out_specs=[
                by_rows(width),
                pl.BlockSpec((rows, quarter), lambda i, idx: (0, jnp.maximum(i - blocks, 0))),
                pl.BlockSpec(unit, lambda i, idx: (jnp.maximum(i - blocks - 2, 0), 0, 0, 0)),
                pl.BlockSpec(unit, lambda i, idx: (jnp.clip(i - blocks, 0, 1), 0, 0, 0)),
                whole((8, width)),
            ],
            scratch_shapes=[
                pltpu.VMEM((width, size), bf16),
                pltpu.VMEM((rows, width), bf16),
                pltpu.SemaphoreType.DMA((CHUNKS, 6)),
            ],
        ),
        out_shape=[
            jax.ShapeDtypeStruct((rows, width), f32),
            jax.ShapeDtypeStruct((rows, width), bf16),
            jax.ShapeDtypeStruct(grads, bf16),
            jax.ShapeDtypeStruct(grads, bf16),
            jax.ShapeDtypeStruct((8, width), f32),
        ],
        compiler_params=params(48),
        cost_estimate=cost(2 * rows * width * (size + 2 * width), 2 * rows * size + 2 * width * size + 16 * rows * width),
        name="block_back",
    )(index, *pieces, d_pre, middle, cot, *attended, weight, vec)


def block_out_body(index_ref, *refs):
    pieces, (hidden_ref, middle_ref, vec_ref, out_ref, down_ref, sems) = refs[: 6 * CHUNKS], refs[6 * CHUNKS :]
    step = pl.program_id(0)
    size = down_ref.shape[0] // CHUNKS

    def rest(value):
        out_ref[...] = (middle_ref[...] + row_of(vec_ref, "down_bias") + value).astype(bf16)

    @pl.when(step == 0)
    def _():
        loads = chunk_loads(
            index_ref,
            pieces,
            1,
            lambda chunk, first, count: down_ref.at[pl.ds(chunk * size + first, count), :],
            sems,
        )
        for group in loads:
            for copy in group:
                copy.start()
        total = None
        for chunk, group in enumerate(loads):
            for copy in group:
                copy.wait()
            cols = slice(chunk * size, (chunk + 1) * size)
            term = dot(hidden_ref[:, cols], down_ref[cols, :])
            total = term if total is None else total + term
        rest(total)

    @pl.when(step > 0)
    def _():
        rest(dot(hidden_ref[...], down_ref[...]))


def block_output(index, pieces, hidden, middle, vec, rows_each=256):
    rows, width = middle.shape
    size = hidden.shape[1]

    def by_rows(cols):
        return pl.BlockSpec((rows_each, cols), lambda i, idx: (i, 0))

    return pl.pallas_call(
        block_out_body,
        grid_spec=pltpu.PrefetchScalarGridSpec(
            num_scalar_prefetch=1,
            grid=(rows // rows_each,),
            in_specs=[any_spec] * (6 * CHUNKS) + [by_rows(size), by_rows(width), whole((SHARDS * VEC_ROWS, LANES))],
            out_specs=by_rows(width),
            scratch_shapes=[pltpu.VMEM((size, width), bf16), pltpu.SemaphoreType.DMA((CHUNKS, 6))],
        ),
        out_shape=jax.ShapeDtypeStruct((rows, width), bf16),
        compiler_params=params(48),
        cost_estimate=cost(2 * rows * width * size, 2 * rows * size + 2 * width * size + 6 * rows * width),
        name="block_output",
    )(index, *pieces, hidden, middle, vec)


def input_grad_body(index_ref, *refs, blocks):
    parts, weights = refs[:6], refs[6:8]
    tokens_ref, d_middle_ref, vec_ref, sums_ref, bqv_a_ref, bqv_b_ref = refs[8:14]
    bias_refs = refs[14 : 14 + CHUNKS]
    out_ref, grads_ref, gain_ref, shift_ref = refs[14 + CHUNKS :]
    step = pl.program_id(0)

    @pl.when(step == 0)
    def _():
        gain_ref[...] = jnp.zeros_like(gain_ref)
        shift_ref[...] = jnp.zeros_like(shift_ref)

    d_normed = None
    for half in range(2):
        for i in range(3):
            ref = parts[3 * half + i]
            part = ref.shape[1]
            term = dot(ref[...], weights[half][:, i * part : (i + 1) * part], 1, 1)
            d_normed = term if d_normed is None else d_normed + term
    hat, inverse = norm_parts(tokens_ref[...].astype(f32))
    out_ref[...] = d_middle_ref[...] + norm_back(d_normed, hat, inverse, row_of(vec_ref, "ln1_gain"))
    gain_ref[...] += column_sum(d_normed * hat)
    shift_ref[...] += column_sum(d_normed)

    @pl.when(step == blocks - 1)
    def _():
        grads_ref[...] = jnp.zeros_like(grads_ref)

        def put(name, shard, value, offset=0):
            first = shard * VEC_ROWS + VEC[name][0] + offset
            for i in range(value.shape[1] // LANES):
                grads_ref[first + i : first + i + 1, :] = value[:, i * LANES : (i + 1) * LANES]

        for shard in range(SHARDS):
            cols = slice(shard * 256, (shard + 1) * 256)
            put("ln1_gain", shard, gain_ref[:, cols])
            put("ln1_bias", shard, shift_ref[:, cols])
            put("ln2_gain", shard, sums_ref[0:1, cols])
            put("ln2_bias", shard, sums_ref[1:2, cols])
            put("out_bias", shard, sums_ref[2:3, cols])
            put("down_bias", shard, sums_ref[3:4, cols])
            source = bqv_a_ref if shard % 2 == 0 else bqv_b_ref
            put("b_qv", shard, source[shard // 2 : shard // 2 + 1, :])
            for chunk in range(CHUNKS):
                size = bias_refs[chunk].shape[1] // SHARDS
                put("up_bias", shard, bias_refs[chunk][:, shard * size : (shard + 1) * size], chunk)


def input_gradient(index, parts, weights, tokens, d_middle, vec, sums, bqv, biases, rows_each=256):
    rows, width = tokens.shape
    part = parts[0].shape[1]
    blocks = rows // rows_each

    def by_rows(cols):
        return pl.BlockSpec((rows_each, cols), lambda i, idx: (i, 0))

    return pl.pallas_call(
        functools.partial(input_grad_body, blocks=blocks),
        grid_spec=pltpu.PrefetchScalarGridSpec(
            num_scalar_prefetch=1,
            grid=(blocks,),
            in_specs=[by_rows(part)] * 6
            + [whole((width, 3 * part))] * 2
            + [by_rows(width), by_rows(width), whole((SHARDS * VEC_ROWS, LANES)), whole((8, width))]
            + [whole((2, part))] * 2
            + [whole(bias.shape) for bias in biases],
            out_specs=[by_rows(width), whole((SHARDS * VEC_ROWS, LANES))],
            scratch_shapes=[pltpu.VMEM((1, width), f32), pltpu.VMEM((1, width), f32)],
        ),
        out_shape=[
            jax.ShapeDtypeStruct((rows, width), f32),
            jax.ShapeDtypeStruct((SHARDS * VEC_ROWS, LANES), f32),
        ],
        compiler_params=params(40),
        cost_estimate=cost(12 * rows * width * part, 10 * rows * width + 12 * rows * part + 12 * width * part),
        name="input_gradient",
    )(index, *parts, *weights, tokens, d_middle, vec, sums, *bqv, *biases)


def place_body(index_ref, pair_ref, other_ref, *refs, plan, fresh):
    outs = len(refs) - 2 if fresh else (len(refs) - 2) // 2
    out_refs = refs[-2 - outs : -2]
    scratch, sems = refs[-2:]
    low, mid = index_ref[1], index_ref[2]
    rows = pair_ref.shape[2]
    for a, ref in enumerate((pair_ref, other_ref)):
        for b in range(2):
            first = pl.multiple_of((low ^ a) * (2 * rows) + (mid ^ b) * rows, rows)
            for u in range(pair_ref.shape[1]):
                scratch[u, pl.ds(first, rows), :] = ref[b, u].astype(f32)
    copies = []
    for i, (unit, cols, width, out, row, col) in enumerate(plan):
        copies.append(
            pltpu.make_async_copy(
                scratch.at[unit, :, cols : cols + width],
                out_refs[out].at[row : row + 4 * rows, col : col + width],
                sems.at[i],
            )
        )
    for copy in copies:
        copy.start()
    for copy in copies:
        copy.wait()


def place(index, pieces, plan, shapes, carried, name):
    pair, other = pieces
    _, units, rows, width = pair.shape
    fresh = carried is None
    count = len(shapes)
    return pl.pallas_call(
        functools.partial(place_body, plan=plan, fresh=fresh),
        grid_spec=pltpu.PrefetchScalarGridSpec(
            num_scalar_prefetch=1,
            grid=(1,),
            in_specs=[whole(pair.shape), whole(other.shape)] + ([] if fresh else [any_spec] * count),
            out_specs=[any_spec] * count,
            scratch_shapes=[pltpu.VMEM((units, 4 * rows, width), f32), pltpu.SemaphoreType.DMA((len(plan),))],
        ),
        out_shape=[jax.ShapeDtypeStruct(shape, f32) for shape in shapes],
        input_output_aliases={} if fresh else {3 + i: i for i in range(count)},
        compiler_params=params(16),
        cost_estimate=cost(units * 4 * rows * width, units * 4 * rows * width * 6),
        name=name,
    )(index, pair, other, *(carried or ()))


def body(
    mesh,
    tokens,
    piece_start,
    ln1_gain,
    ln1_bias,
    query_key_value_weight,
    b_qv,
    attention_out_weight,
    attention_out_bias,
    ln2_gain,
    ln2_bias,
    up_weight,
    up_bias,
    down_weight,
    down_bias,
    cotangent,
):
    count, seq_len, width = tokens.shape
    rows = count * seq_len
    hidden_size = up_weight.shape[1]
    tokens = tokens.reshape(rows, width)
    cot = cotangent.reshape(rows, width)
    moves = Moves(mesh, piece_start)
    half = width // 2
    size = hidden_size // CHUNKS
    block = size // SHARDS

    def as_rows(value):
        return value.reshape(-1, LANES)

    own_vec = jnp.concatenate(
        [
            as_rows(value)
            for value in (ln1_gain, ln1_bias, b_qv, attention_out_bias, ln2_gain, ln2_bias, up_bias, down_bias)
        ]
        + [jnp.zeros((VEC_ROWS - 12, LANES), bf16)]
    )

    def joined_cols(which):
        return jnp.concatenate(
            [
                query_key_value_weight[:, i * width + which * half : i * width + (which + 1) * half]
                for i in range(3)
            ],
            axis=1,
        )

    def hidden_own(chunk):
        up = jnp.concatenate(
            [
                up_weight[:, s * size + chunk * block : s * size + (chunk + 1) * block]
                for s in range(SHARDS)
            ],
            axis=1,
        )
        return jnp.stack([up, down_weight[chunk * block : (chunk + 1) * block, :]])

    far_vec = moves.across(own_vec)
    near_vec = moves.core(own_vec)
    own_a = joined_cols(0)
    far_a = moves.across(own_a)
    near_a = moves.core(own_a)
    own_b = joined_cols(1)
    half_b = moves.half(own_b)
    hidden_owns = [hidden_own(chunk) for chunk in range(CHUNKS)]
    hidden_halves = [moves.half(own) for own in hidden_owns]
    out_half = moves.half(attention_out_weight)
    far_near_vec = moves.core(far_vec)
    moves.wait(half_b, out_half, *hidden_halves)
    normed, vec = first_norm(moves.index, tokens, (own_vec, near_vec, far_vec, far_near_vec))
    moves.ran(vec)

    joined, joined_weight, attended, totals = [None] * 2, [None] * 2, [None] * 2, [None] * 2
    hidden_far, hidden_near, hidden_other = [None] * CHUNKS, [None] * CHUNKS, [None] * CHUNKS
    hidden_pieces = [None] * CHUNKS

    def fetch(chunk, kernels):
        hidden_far[chunk] = moves.across(hidden_halves[chunk])
        hidden_near[chunk] = moves.core(hidden_owns[chunk])
        moves.by(kernels, hidden_far[chunk], hidden_near[chunk])

    def relay(chunk, kernels):
        hidden_other[chunk] = moves.rep(hidden_far[chunk], 1)
        moves.by(kernels, hidden_other[chunk])

    far_b = moves.across(half_b)
    near_b = moves.core(own_b)
    moves.by(1, far_b, near_b)
    joined[0], joined_weight[0] = joined_product(
        0, moves.index, (own_a, near_a, far_a, moves.core(far_a)), normed, vec
    )
    moves.ran(joined[0])
    other_b = moves.rep(far_b, 1)
    moves.by(1, other_b)
    fetch(0, 1)
    attended[0], totals[0] = attend_forward(0, moves.index, joined[0])
    moves.ran(totals[0])
    relay(0, 2)
    out_far = moves.across(out_half)
    out_near = moves.core(attention_out_weight)
    moves.by(1, out_far, out_near)
    joined[1], joined_weight[1] = joined_product(
        1, moves.index, (own_b, near_b, far_b, other_b, moves.core(far_b), moves.core(other_b)), normed, vec
    )
    moves.ran(joined[1])
    out_other = moves.rep(out_far, 1)
    moves.by(1, out_other)
    fetch(1, 1)
    attended[1], totals[1] = attend_forward(1, moves.index, joined[1])
    moves.ran(totals[1])
    relay(1, 2)
    fetch(2, 2)
    middle, normed_two, out_weight = middle_product(
        moves.index,
        (attention_out_weight, out_near, out_far, out_other, moves.core(out_far), moves.core(out_other)),
        attended,
        tokens,
        vec,
    )
    moves.ran(normed_two)

    carried = None
    shard_sums, up_biases = [], []

    def hidden_step(chunk):
        nonlocal carried
        far, other = hidden_far[chunk], hidden_other[chunk]
        hidden_pieces[chunk] = (
            hidden_owns[chunk],
            hidden_near[chunk],
            far,
            other,
            moves.core(far),
            moves.core(other),
        )
        *carried, keep, send, bias = hidden_chunk(
            chunk, moves.index, hidden_pieces[chunk], carried, normed_two, cot, vec, hidden_size
        )
        moves.ran(bias)
        up_biases.append(bias)
        shard_sums.append(ShardSum(moves, keep, send))

    fetch(3, 1)
    hidden_step(0)
    relay(2, 1)
    hidden_step(1)
    relay(3, 1)
    shard_sums[0].cross(1)
    hidden_step(2)
    shard_sums[1].cross(1)
    hidden_step(3)
    shard_sums[2].cross(1)
    first_sum = RepSum(moves, shard_sums[:2])
    all_pieces = [piece for pieces in hidden_pieces for piece in pieces]
    hidden, d_pre = carried
    d_middle, d_attended, keep, send, sums = block_back(
        moves.index, all_pieces, d_pre, middle, cot, attended, out_weight, vec
    )
    moves.ran(sums)
    parts, bqv = [], []

    def backward(which):
        *grads, keep, send, bias = attend_backward(
            which, moves.index, joined[which], attended[which], d_attended, totals[which], normed
        )
        parts.extend(grads)
        bqv.append(bias)
        moves.ran(bias)
        return ShardSum(moves, keep, send)

    shard_sums[3].cross(1)
    out_sum = ShardSum(moves, keep, send)
    first_sum.split()
    second_sum = RepSum(moves, shard_sums[2:3])
    a_sum = backward(0)
    out_sum.cross(1)
    first_sum.add()
    second_sum.split()
    third_sum = RepSum(moves, shard_sums[3:4])
    b_sum = backward(1)
    a_sum.cross(1)
    first_sum.spread()
    second_sum.add()
    third_sum.split()
    input_grad, vec_grads = input_gradient(
        moves.index, parts, joined_weight, tokens, d_middle, vec, sums, bqv, up_biases
    )
    moves.ran(vec_grads)
    b_sum.cross(1)
    fourth_sum = RepSum(moves, [out_sum, a_sum])
    first_sum.finish()
    second_sum.spread()
    third_sum.add()
    block_out = block_output(moves.index, all_pieces, hidden, middle, vec)
    moves.ran(block_out)

    def place_hidden(chunks, pieces, grads, name):
        plan = []
        for i, chunk in enumerate(chunks):
            plan += [(2 * i, s * block, block, 0, 0, s * size + chunk * block) for s in range(SHARDS)]
            plan += [(2 * i + 1, 0, width, 1, chunk * block, 0)]
        shapes = [(width // SHARDS, hidden_size), (size, width)]
        grads = place(moves.index, pieces, plan, shapes, grads, name)
        moves.ran(grads[0])
        return grads

    last_sum = RepSum(moves, [b_sum])
    fourth_sum.split()
    second_sum.finish()
    third_sum.spread()
    vec_sum = VecSum(moves, vec_grads)
    grads = place_hidden((0, 1), first_sum.pieces(), None, "place_hidden_first")
    last_sum.split()
    fourth_sum.add()
    third_sum.finish()
    vec_sum.step()
    grads = place_hidden((2,), second_sum.pieces(), grads, "place_hidden_second")
    last_sum.add()
    fourth_sum.spread()
    vec_sum.step()
    grad_up, grad_down = place_hidden((3,), third_sum.pieces(), grads, "place_hidden_third")
    fourth_sum.finish()
    last_sum.spread()
    vec_sum.step()
    last_sum.finish()
    vec_sum = vec_sum.rest()
    third = width // SHARDS
    plan = [(i, 0, half, 0, 0, i * half) for i in range(2)]
    plan += [(2 + i, 0, half, 1, 0, i * width) for i in range(3)]
    shapes = [(third, width), (third, 3 * width)]
    grad_out, grad_joined = place(moves.index, fourth_sum.pieces(), plan, shapes, None, "place_fourth")
    plan = [(i, 0, half, 0, 0, i * width + half) for i in range(3)]
    (grad_joined,) = place(moves.index, last_sum.pieces(), plan, shapes[1:], (grad_joined,), "place_last")

    def vec_part(name):
        first, count = VEC[name]
        return vec_sum[first : first + count].reshape(count * LANES)

    return (
        block_out.reshape(count, seq_len, width),
        input_grad.reshape(count, seq_len, width),
        vec_part("ln1_gain"),
        vec_part("ln1_bias"),
        grad_joined,
        vec_part("b_qv"),
        grad_out,
        vec_part("out_bias"),
        vec_part("ln2_gain"),
        vec_part("ln2_bias"),
        grad_up,
        vec_part("up_bias"),
        grad_down,
        vec_part("down_bias"),
    )


def solution(mesh):
    batch = P(("shard", "rep"), None, None)
    vector, matrix = P("shard"), P("shard", None)
    in_specs = (
        batch,
        P(("shard", "rep")),
        vector,
        vector,
        matrix,
        vector,
        matrix,
        vector,
        vector,
        vector,
        matrix,
        vector,
        matrix,
        vector,
        batch,
    )
    out_specs = (
        batch,
        batch,
        vector,
        vector,
        matrix,
        vector,
        matrix,
        vector,
        vector,
        vector,
        matrix,
        vector,
        matrix,
        vector,
    )
    return jax.shard_map(
        functools.partial(body, mesh), mesh=mesh, in_specs=in_specs, out_specs=out_specs, check_vma=False
    )
```

```python
import functools

import jax
import jax.numpy as jnp
from jax import lax
from jax.experimental import pallas as pl
from jax.experimental.pallas import tpu as pltpu
from jax.sharding import PartitionSpec as P

HEADS = 16
PIECE = 256
HEAD_DIM = 64
PAIR = 2 * HEAD_DIM
SHARDS = 4
CHUNKS = 4
EPS = 1e-05
HIDDEN_PENALTY = 1e33

bf16 = jnp.bfloat16
f32 = jnp.float32

VEC = {
    "ln1_gain": (0, 1),
    "ln1_bias": (1, 1),
    "b_qv": (2, 2),
    "out_bias": (4, 1),
    "ln2_gain": (5, 1),
    "ln2_bias": (6, 1),
    "up_bias": (7, 4),
    "down_bias": (11, 1),
}
VEC_ROWS = 16
LANES = 256

any_spec = pl.BlockSpec(memory_space=pltpu.MemorySpace.HBM)


def dot(left, right, left_dim=1, right_dim=0):
    return lax.dot_general(
        left, right, (((left_dim,), (right_dim,)), ((), ())), preferred_element_type=f32
    )


def params(mib):
    return pltpu.CompilerParams(vmem_limit_bytes=int(mib * 2**20))


def cost(flops, moved, transcendentals=0, scale=8):
    return pl.CostEstimate(
        flops=int(scale * flops), bytes_accessed=int(scale * moved), transcendentals=int(scale * transcendentals)
    )


def vec_rows(vec_ref, rows):
    firsts = [shard * VEC_ROWS + row for shard, row in rows]
    return jnp.concatenate([vec_ref[first : first + 1, :] for first in firsts], axis=1)


def row_of(vec_ref, name):
    return vec_rows(vec_ref, [(shard, VEC[name][0]) for shard in range(SHARDS)])


def whole(shape):
    return pl.BlockSpec(shape, lambda *_: (0,) * len(shape))


def flip(value, axis, size, bit):
    return lax.ppermute(value, axis, [(i, i ^ bit) for i in range(size)])


class Moves:
    def __init__(self, mesh, starts):
        self.reps = mesh.shape["rep"]
        assert mesh.shape["shard"] == SHARDS and self.reps % 4 == 0
        self.shard = lax.axis_index("shard")
        rep = lax.axis_index("rep")
        self.low = rep & 1
        self.mid = (rep >> 1) & 1
        self.index = jnp.concatenate(
            [jnp.stack([self.shard, self.low, self.mid]).astype(jnp.int32), starts]
        )
        self.last = ()
        self.count = 0
        self.due = []

    def wait(self, *values):
        self.index = after(self.index, *values, *self.last)

    def by(self, kernels, *values):
        self.due.append((self.count + kernels, values))

    def ran(self, value):
        self.last = (value,)
        self.count += 1
        ready = [value for when, values in self.due if when <= self.count for value in values]
        self.due = [entry for entry in self.due if entry[0] > self.count]
        self.wait(*ready)
        return value

    def move(self, value, axis, size, bit):
        return flip(after(value, *self.last), axis, size, bit)

    def core(self, value):
        return self.move(value, "shard", SHARDS, 1)

    def across(self, value):
        return self.move(value, "shard", SHARDS, 2)

    def rep(self, value, bit):
        return self.move(value, "rep", self.reps, bit)

    def half(self, own):
        rows = own.shape[-2] // 2
        return lax.dynamic_slice_in_dim(own, self.low * rows, rows, own.ndim - 2)

    def pick(self, value, which, size):
        return lax.dynamic_slice_in_dim(value, which * size, size, 1)


def after(value, *earlier):
    return lax.optimization_barrier((value, *earlier))[0] if earlier else value


class ShardSum:
    def __init__(self, moves, keep, send, kernels=1):
        self.moves, self.keep = moves, keep
        self.got = moves.core(send)
        moves.by(kernels, self.got)

    def cross(self, kernels):
        self.got = after(self.got, *self.moves.last)
        out = self.keep[1] + self.got[1]
        self.mine = self.keep[0] + self.got[0]
        self.moves.wait(out, self.mine)
        self.got = self.moves.across(out)
        self.moves.by(kernels, self.got)

    def halves(self):
        moves, mine = self.moves, self.mine
        got = after(self.got, *moves.last)
        size = mine.shape[1] // 2
        return [
            moves.pick(mine, which, size) + moves.pick(got, which, size)
            for which in (moves.low, 1 - moves.low)
        ]


class RepSum:
    def __init__(self, moves, sums, kernels=1):
        self.moves = moves
        halves = [s.halves() for s in sums]
        self.mine = jnp.concatenate([h[0] for h in halves])
        self.bit = 2
        self.send(jnp.concatenate([h[1] for h in halves]), 1, kernels)

    def send(self, out, bit, kernels):
        self.moves.wait(out, self.mine)
        self.got = self.moves.rep(out, bit)
        self.moves.by(kernels, self.got)

    def split(self, kernels=1):
        moves = self.moves
        got = after(self.got, *moves.last)
        size = self.mine.shape[1] // 2
        out, self.mine = [
            moves.pick(self.mine, which, size) + moves.pick(got, which, size)
            for which in (1 - moves.mid, moves.mid)
        ]
        self.send(out, 2, kernels)

    def add(self, kernels=1):
        self.mine = self.mine + after(self.got, *self.moves.last)
        self.bit *= 2
        self.got = None
        if self.bit < self.moves.reps:
            self.send(self.mine, self.bit, kernels)

    def spread(self, kernels=1):
        while self.got is not None:
            self.add()
        self.send(self.mine, 2, kernels)

    def finish(self, kernels=1):
        self.pair = jnp.stack([self.mine, after(self.got, *self.moves.last)])
        self.send(self.pair, 1, kernels)

    def pieces(self):
        self.moves.wait(self.got)
        return (self.pair, self.got)


class VecSum:
    def __init__(self, moves, value):
        self.moves, self.value = moves, value
        self.plan = [moves.core, moves.across]
        bit = 1
        while bit < moves.reps:
            self.plan.append(functools.partial(moves.rep, bit=bit))
            bit *= 2
        self.at = 0
        self.send()

    def send(self):
        self.got = self.plan[self.at](self.value)
        self.moves.by(1, self.got)
        self.at += 1

    def step(self):
        moves = self.moves
        self.value = self.value + after(self.got, *moves.last)
        if self.at == 2:
            self.value = lax.dynamic_slice_in_dim(self.value, moves.shard * VEC_ROWS, VEC_ROWS, 0)
        moves.wait(self.value)
        if self.at < len(self.plan):
            self.send()

    def rest(self):
        while self.at < len(self.plan):
            self.step()
        self.step()
        return self.value


def piece_copies(index_ref, pieces, target, sems):
    shard, low = index_ref[0], index_ref[1]
    rows = pieces[0].shape[-2]
    if len(pieces) == 4:
        plan = [(piece, shard ^ k, 0, rows) for k, piece in enumerate(pieces)]
    else:
        own, near, far, far_other, far_near, far_other_near = pieces
        half = rows // 2
        plan = (
            (own, shard, 0, rows),
            (near, shard ^ 1, 0, rows),
            (far, shard ^ 2, low * half, half),
            (far_other, shard ^ 2, (1 - low) * half, half),
            (far_near, shard ^ 3, low * half, half),
            (far_other_near, shard ^ 3, (1 - low) * half, half),
        )
    return [
        pltpu.make_async_copy(source, target(to, first, count), sems.at[i])
        for i, (source, to, first, count) in enumerate(plan)
    ]


def norm_parts(value):
    center = value - jnp.mean(value, axis=-1, keepdims=True)
    inverse = lax.rsqrt(jnp.mean(center * center, axis=-1, keepdims=True) + EPS)
    return center * inverse, inverse


def first_norm_body(index_ref, tokens_ref, own_ref, near_ref, far_ref, far_near_ref, normed_ref, vec_ref):
    shard = index_ref[0]

    @pl.when(pl.program_id(0) == 0)
    def _():
        for k, ref in enumerate((own_ref, near_ref, far_ref, far_near_ref)):
            vec_ref[pl.ds(pl.multiple_of((shard ^ k) * VEC_ROWS, VEC_ROWS), VEC_ROWS), :] = ref[...].astype(f32)

    hat, _ = norm_parts(tokens_ref[...].astype(f32))
    normed_ref[...] = (hat * row_of(vec_ref, "ln1_gain") + row_of(vec_ref, "ln1_bias")).astype(bf16)


def first_norm(index, tokens, vec_pieces, block=256):
    rows, width = tokens.shape
    row = pl.BlockSpec((block, width), lambda i, idx: (i, 0))
    return pl.pallas_call(
        first_norm_body,
        grid_spec=pltpu.PrefetchScalarGridSpec(
            num_scalar_prefetch=1,
            grid=(rows // block,),
            in_specs=[row] + [whole((VEC_ROWS, LANES))] * 4,
            out_specs=[row, whole((SHARDS * VEC_ROWS, LANES))],
        ),
        out_shape=[
            jax.ShapeDtypeStruct((rows, width), bf16),
            jax.ShapeDtypeStruct((SHARDS * VEC_ROWS, LANES), f32),
        ],
        compiler_params=params(16),
        cost_estimate=cost(20 * rows * width, 4 * rows * width),
        name="first_norm",
    )(index, tokens, *vec_pieces)


def joined_body(half, index_ref, *refs):
    pieces, (normed_ref, vec_ref, out_ref, weight_ref, sems) = refs[:-5], refs[-5:]

    @pl.when(pl.program_id(0) == 0)
    def _():
        rows = pieces[0].shape[0]
        copies = piece_copies(
            index_ref,
            pieces,
            lambda to, first, count: weight_ref.at[
                pl.ds(pl.multiple_of(to * rows + first, 128), count), :
            ],
            sems,
        )
        for copy in copies:
            copy.start()
        for copy in copies:
            copy.wait()

    part = weight_ref.shape[1] // 3
    first = VEC["b_qv"][0]
    normed = normed_ref[...]
    for i in range(3):
        cols = slice(i * part, (i + 1) * part)
        value = dot(normed, weight_ref[:, cols])
        if i != 1:
            shard = half if i == 0 else 2 + half
            value = value + vec_rows(vec_ref, [(shard, first), (shard, first + 1)])
        out_ref[:, cols] = value.astype(bf16)


def joined_product(half, index, pieces, normed, vec, block=256):
    rows, width = normed.shape
    cols = pieces[0].shape[1]
    return pl.pallas_call(
        functools.partial(joined_body, half),
        grid_spec=pltpu.PrefetchScalarGridSpec(
            num_scalar_prefetch=1,
            grid=(rows // block,),
            in_specs=[any_spec] * len(pieces)
            + [pl.BlockSpec((block, width), lambda i, idx: (i, 0)), whole((SHARDS * VEC_ROWS, LANES))],
            out_specs=[pl.BlockSpec((block, cols), lambda i, idx: (i, 0)), whole((width, cols))],
            scratch_shapes=[pltpu.SemaphoreType.DMA((6,))],
        ),
        out_shape=[
            jax.ShapeDtypeStruct((rows, cols), bf16),
            jax.ShapeDtypeStruct((width, cols), bf16),
        ],
        compiler_params=params(24),
        cost_estimate=cost(2 * rows * width * cols, 2 * (rows * width + rows * cols + 2 * width * cols)),
        name="joined_product",
    )(index, *pieces, normed, vec)


def penalty(start, seq_len):
    key = lax.broadcasted_iota(jnp.int32, (seq_len, seq_len), 0)
    query = lax.broadcasted_iota(jnp.int32, (seq_len, seq_len), 1)
    key_in = (key >= start) & (key < start + PIECE)
    query_in = (query >= start) & (query < start + PIECE)
    seen = (key <= query) | (key_in & query_in)
    return jnp.where(seen, jnp.abs(key - query).astype(f32), HIDDEN_PENALTY)


def slope_of(head):
    return jnp.exp2((jnp.full((1, 1), head, jnp.int32).astype(f32) + 1.0) * (-8.0 / HEADS))


def attend_forward_body(first_head, start_ref, q_ref, k_ref, v_ref, out_ref, total_ref, pen_ref):
    pair = pl.program_id(1)
    seq_len = q_ref.shape[0]

    @pl.when(pair == 0)
    def _():
        pen_ref[...] = penalty(start_ref[3 + pl.program_id(0)], seq_len)

    queries, keys = q_ref[...], k_ref[...]
    values_t = v_ref[...].T
    lane = lax.broadcasted_iota(jnp.int32, (seq_len, PAIR), 1)
    outs = []
    for e in range(2):
        chosen = (lane < HEAD_DIM) if e == 0 else (lane >= HEAD_DIM)
        key_e = jnp.where(chosen, keys * (HEAD_DIM**-0.5), 0).astype(bf16)
        scores = dot(key_e, queries, 1, 1) - slope_of(first_head + 2 * pair + e) * pen_ref[...]
        top = jnp.max(scores, axis=0, keepdims=True)
        weight = jnp.exp(scores - top)
        total = jnp.sum(weight, axis=0, keepdims=True)
        out_t = dot(values_t[e * HEAD_DIM : (e + 1) * HEAD_DIM, :], weight.astype(bf16))
        outs.append(out_t * (1.0 / total))
        total_ref[0, 0, e : e + 1, :] = top + jnp.log(total)
    out_ref[...] = jnp.concatenate(outs, axis=0).T.astype(bf16)


def attend_forward(half, index, joined):
    count = index.shape[0] - 3
    seq_len, width = joined.shape[0] // count, joined.shape[1] // 3
    pairs = width // PAIR

    def cols(first):
        return pl.BlockSpec((seq_len, PAIR), lambda s, h, st: (s, first + h))

    return pl.pallas_call(
        functools.partial(attend_forward_body, half * 2 * pairs),
        grid_spec=pltpu.PrefetchScalarGridSpec(
            num_scalar_prefetch=1,
            grid=(count, pairs),
            in_specs=[cols(0), cols(pairs), cols(2 * pairs)],
            out_specs=[cols(0), pl.BlockSpec((1, 1, 2, seq_len), lambda s, h, st: (s, h, 0, 0))],
            scratch_shapes=[pltpu.VMEM((seq_len, seq_len), f32)],
        ),
        out_shape=[
            jax.ShapeDtypeStruct((count * seq_len, width), bf16),
            jax.ShapeDtypeStruct((count, pairs, 2, seq_len), f32),
        ],
        compiler_params=params(24),
        cost_estimate=cost(
            24 * count * seq_len * seq_len * width, 8 * count * seq_len * width, count * seq_len * seq_len * 2 * pairs
        ),
        name="attend_forward",
    )(index, joined, joined, joined)


def attend_backward_body(
    first_head,
    steps,
    index_ref,
    q_ref,
    k_ref,
    v_ref,
    out_ref,
    dout_ref,
    total_ref,
    normed_ref,
    dq_ref,
    dk_ref,
    dv_ref,
    keep_ref,
    send_ref,
    sums_ref,
    pen_ref,
):
    step = pl.program_id(0)
    seq_len = q_ref.shape[0]
    scale = HEAD_DIM**-0.5
    pairs = dq_ref.shape[1] // PAIR
    seq, pair = step // pairs, step % pairs

    @pl.when((step < steps) & (pair == 0))
    def _():
        pen_ref[...] = penalty(index_ref[3 + seq], seq_len)

    @pl.when(step < steps)
    def _():
        queries, keys, values, d_out = q_ref[...], k_ref[...], v_ref[...], dout_ref[...]
        lane = lax.broadcasted_iota(jnp.int32, (seq_len, PAIR), 1)
        keys_t = keys.T
        both_t = (d_out.astype(f32) * out_ref[...].astype(f32)).T
        d_q, d_k, d_v = [], [], []
        for e in range(2):
            chosen = (lane < HEAD_DIM) if e == 0 else (lane >= HEAD_DIM)
            part = slice(e * HEAD_DIM, (e + 1) * HEAD_DIM)
            key_e = jnp.where(chosen, keys * scale, 0).astype(bf16)
            value_e = jnp.where(chosen, values, 0)
            inner = jnp.sum(both_t[part, :], axis=0, keepdims=True)
            scores = dot(key_e, queries, 1, 1) - slope_of(first_head + 2 * pair + e) * pen_ref[...]
            probs = jnp.exp(scores - total_ref[0, 0, e : e + 1, :])
            d_scores = (probs * (dot(value_e, d_out, 1, 1) - inner)).astype(bf16)
            d_v.append(dot(probs.astype(bf16), d_out))
            d_k.append(dot(d_scores, queries))
            d_q.append(dot(keys_t[part, :], d_scores))
        rows = pl.ds(pl.multiple_of(seq * seq_len, seq_len), seq_len)
        cols = pl.ds(pl.multiple_of(pair * PAIR, PAIR), PAIR)
        dq_ref[rows, cols] = (jnp.concatenate(d_q, axis=0) * scale).T.astype(bf16)
        dk_ref[rows, cols] = (jnp.where(lane < HEAD_DIM, d_k[0], d_k[1]) * scale).astype(bf16)
        dv_ref[rows, cols] = jnp.where(lane < HEAD_DIM, d_v[0], d_v[1]).astype(bf16)

    @pl.when(step == steps)
    def _():
        sums_ref[0:1, :] = column_sum(dq_ref[...].astype(f32))
        sums_ref[1:2, :] = column_sum(dv_ref[...].astype(f32))

    @pl.when(step >= steps)
    def _():
        block = keep_ref.shape[2]
        t = step - steps
        k = jnp.where(t < 2, 2 * t + 1, 2 * t - 4)
        left = normed_ref[:, pl.ds(pl.multiple_of((index_ref[0] ^ k) * block, block), block)]
        for i, ref in enumerate((dq_ref, dk_ref, dv_ref)):
            value = dot(left, ref[...], 0, 0).astype(bf16)

            @pl.when(t < 2)
            def _(i=i, value=value):
                send_ref[0, i] = value

            @pl.when(t >= 2)
            def _(i=i, value=value):
                keep_ref[0, i] = value


def attend_backward(half, index, joined, attended, d_attended, totals, normed):
    count = index.shape[0] - 3
    rows, width = joined.shape[0], joined.shape[1] // 3
    seq_len = rows // count
    pairs = width // PAIR
    steps = count * pairs
    model = normed.shape[1]

    def cols(first):
        def where(i, idx):
            at = jnp.minimum(i, steps - 1)
            return (at // pairs, first + at % pairs)

        return pl.BlockSpec((seq_len, PAIR), where)

    def totals_at(i, idx):
        at = jnp.minimum(i, steps - 1)
        return (at // pairs, at % pairs, 0, 0)

    grads = (2, 3, model // SHARDS, width)
    unit = (1,) + grads[1:]
    return pl.pallas_call(
        functools.partial(attend_backward_body, half * 2 * pairs, steps),
        grid_spec=pltpu.PrefetchScalarGridSpec(
            num_scalar_prefetch=1,
            grid=(steps + SHARDS,),
            in_specs=[
                cols(0),
                cols(pairs),
                cols(2 * pairs),
                cols(0),
                cols(half * pairs),
                pl.BlockSpec((1, 1, 2, seq_len), totals_at),
                whole((rows, model)),
            ],
            out_specs=[whole((rows, width))] * 3
            + [
                pl.BlockSpec(unit, lambda i, idx: (jnp.clip(i - steps - 2, 0, 1), 0, 0, 0)),
                pl.BlockSpec(unit, lambda i, idx: (jnp.clip(i - steps, 0, 1), 0, 0, 0)),
                whole((2, width)),
            ],
            scratch_shapes=[pltpu.VMEM((seq_len, seq_len), f32)],
        ),
        out_shape=[jax.ShapeDtypeStruct((rows, width), bf16)] * 3
        + [
            jax.ShapeDtypeStruct(grads, bf16),
            jax.ShapeDtypeStruct(grads, bf16),
            jax.ShapeDtypeStruct((2, width), f32),
        ],
        compiler_params=params(40),
        cost_estimate=cost(
            36 * rows * seq_len * width + 6 * rows * model * width, 16 * rows * width, rows * seq_len * 2 * pairs
        ),
        name="attend_backward",
    )(index, joined, joined, joined, attended, d_attended, totals, normed)


def middle_body(index_ref, *refs):
    pieces, (a_ref, b_ref, tokens_ref, vec_ref, middle_ref, normed_ref, weight_ref, sems) = refs[:6], refs[6:]

    @pl.when(pl.program_id(0) == 0)
    def _():
        rows = pieces[0].shape[0]
        copies = piece_copies(
            index_ref,
            pieces,
            lambda to, first, count: weight_ref.at[
                pl.ds(pl.multiple_of(to * rows + first, 128), count), :
            ],
            sems,
        )
        for copy in copies:
            copy.start()
        for copy in copies:
            copy.wait()

    part = a_ref.shape[1]
    middle = tokens_ref[...].astype(f32) + row_of(vec_ref, "out_bias")
    middle = middle + dot(a_ref[...], weight_ref[:part, :]) + dot(b_ref[...], weight_ref[part:, :])
    middle_ref[...] = middle
    hat, _ = norm_parts(middle)
    normed_ref[...] = (hat * row_of(vec_ref, "ln2_gain") + row_of(vec_ref, "ln2_bias")).astype(bf16)


def middle_product(index, pieces, attended, tokens, vec, block=256):
    rows, width = tokens.shape
    row = pl.BlockSpec((block, width), lambda i, idx: (i, 0))
    part = pl.BlockSpec((block, attended[0].shape[1]), lambda i, idx: (i, 0))
    return pl.pallas_call(
        middle_body,
        grid_spec=pltpu.PrefetchScalarGridSpec(
            num_scalar_prefetch=1,
            grid=(rows // block,),
            in_specs=[any_spec] * 6 + [part, part, row, whole((SHARDS * VEC_ROWS, LANES))],
            out_specs=[row, row, whole((width, width))],
            scratch_shapes=[pltpu.SemaphoreType.DMA((6,))],
        ),
        out_shape=[
            jax.ShapeDtypeStruct((rows, width), f32),
            jax.ShapeDtypeStruct((rows, width), bf16),
            jax.ShapeDtypeStruct((width, width), bf16),
        ],
        compiler_params=params(24),
        cost_estimate=cost(2 * rows * width * width, 10 * rows * width + 4 * width * width),
        name="middle_product",
    )(index, *pieces, *attended, tokens, vec)


def gelu_and_slope(pre):
    cube = 0.044715 * pre * pre
    inner = jnp.tanh(0.7978845608028654 * (pre + cube * pre))
    half = 0.5 * (1.0 + inner)
    slope = half + 0.5 * pre * (1.0 - inner * inner) * (0.7978845608028654 * (1.0 + 3.0 * cube))
    return pre * half, slope


def hidden_body(chunk, fresh, index_ref, *refs):
    pieces, refs = refs[:6], refs[6:]
    if not fresh:
        refs = refs[2:]
    normed_hbm, cot_hbm, vec_ref = refs[:3]
    hidden_out, pre_out, keep_ref, send_ref, bias_ref = refs[3:8]
    normed_ref, cot_ref, up_ref, down_ref, hidden_ref, pre_ref, slope_ref, sems, whole_sems = refs[8:]
    step = pl.program_id(0)
    shard = index_ref[0]
    block = 256

    def loads():
        def rows_of(ref, unit):
            rows = pieces[0].shape[1]
            return piece_copies(
                index_ref,
                [piece.at[unit] for piece in pieces],
                lambda to, first, count: ref.at[pl.ds(pl.multiple_of(to * rows + first, 128), count), :],
                sems.at[unit],
            )

        first = [pltpu.make_async_copy(normed_hbm, normed_ref, whole_sems.at[0])] + rows_of(up_ref, 0)
        second = [pltpu.make_async_copy(cot_hbm, cot_ref, whole_sems.at[1])] + rows_of(down_ref, 1)
        return first, second

    def stores():
        cols = pl.ds(chunk * hidden_ref.shape[1], hidden_ref.shape[1])
        return (
            pltpu.make_async_copy(hidden_ref, hidden_out.at[:, cols], whole_sems.at[2]),
            pltpu.make_async_copy(pre_ref, pre_out.at[:, cols], whole_sems.at[3]),
        )

    @pl.when(step == 0)
    def _():
        first, second = loads()
        for copy in first + second:
            copy.start()
        for copy in first:
            copy.wait()

    @pl.when(step == 1)
    def _():
        for copy in loads()[1]:
            copy.wait()

    rows_each = 256
    count = normed_ref.shape[0] // rows_each

    @pl.when(step == 0)
    def _():
        bias = vec_rows(vec_ref, [(one, VEC["up_bias"][0] + chunk) for one in range(SHARDS)])
        for m in range(count):
            rows = slice(m * rows_each, (m + 1) * rows_each)
            value, slope = gelu_and_slope(dot(normed_ref[rows, :], up_ref[...]) + bias)
            value = value.astype(bf16)
            hidden_ref[rows, :] = value
            slope_ref[rows, :] = slope
        stores()[0].start()

    @pl.when(step == 1)
    def _():
        sums = jnp.zeros(bias_ref.shape, f32)
        for m in range(count):
            rows = slice(m * rows_each, (m + 1) * rows_each)
            d_pre = (dot(cot_ref[rows, :], down_ref[...], 1, 1) * slope_ref[rows, :]).astype(bf16)
            pre_ref[rows, :] = d_pre
            sums = sums + jnp.sum(d_pre.astype(f32), axis=0, keepdims=True)
        bias_ref[...] = sums
        stores()[1].start()

    @pl.when(step >= 2)
    def _():
        k = jnp.where(step < 4, 2 * (step - 2) + 1, 2 * (step - 4))
        cols = pl.ds(pl.multiple_of((shard ^ k) * block, block), block)
        left, right = normed_ref[:, cols], hidden_ref[:, cols]
        one = dot(left, pre_ref[...], 0, 0).astype(bf16)
        two = dot(right, cot_ref[...], 0, 0).astype(bf16)

        @pl.when(step < 4)
        def _():
            send_ref[0, 0] = one
            send_ref[0, 1] = two

        @pl.when(step >= 4)
        def _():
            keep_ref[0, 0] = one
            keep_ref[0, 1] = two

    @pl.when(step == 5)
    def _():
        for copy in stores():
            copy.wait()


def hidden_chunk(chunk, index, pieces, carried, normed, cot, vec, hidden_size):
    rows, width = normed.shape
    size = hidden_size // CHUNKS
    fresh = carried is None
    grads = (2, 2, width // SHARDS, size)
    outs = [
        jax.ShapeDtypeStruct((rows, hidden_size), bf16),
        jax.ShapeDtypeStruct((rows, hidden_size), bf16),
        jax.ShapeDtypeStruct(grads, bf16),
        jax.ShapeDtypeStruct(grads, bf16),
        jax.ShapeDtypeStruct((1, size), f32),
    ]
    unit = (1,) + grads[1:]
    return pl.pallas_call(
        functools.partial(hidden_body, chunk, fresh),
        grid_spec=pltpu.PrefetchScalarGridSpec(
            num_scalar_prefetch=1,
            grid=(6,),
            in_specs=[any_spec] * (8 if fresh else 10) + [whole((SHARDS * VEC_ROWS, LANES))],
            out_specs=[
                any_spec,
                any_spec,
                pl.BlockSpec(unit, lambda i, idx: (jnp.maximum(i - 4, 0), 0, 0, 0)),
                pl.BlockSpec(unit, lambda i, idx: (jnp.clip(i - 2, 0, 1), 0, 0, 0)),
                pl.BlockSpec((1, size), lambda i, idx: (0, 0)),
            ],
            scratch_shapes=[
                pltpu.VMEM((rows, width), bf16),
                pltpu.VMEM((rows, width), bf16),
                pltpu.VMEM((width, size), bf16),
                pltpu.VMEM((size, width), bf16),
                pltpu.VMEM((rows, size), bf16),
                pltpu.VMEM((rows, size), bf16),
                pltpu.VMEM((rows, size), f32),
                pltpu.SemaphoreType.DMA((2, 6)),
                pltpu.SemaphoreType.DMA((4,)),
            ],
        ),
        out_shape=outs,
        input_output_aliases={} if fresh else {7: 0, 8: 1},
        compiler_params=params(48),
        cost_estimate=cost(8 * rows * width * size, 8 * rows * width + 16 * rows * size, rows * size),
        name=f"hidden_chunk{chunk}",
    )(index, *pieces, *(carried or ()), normed, cot, vec)


def norm_back(d_normed, hat, inverse, gain):
    scaled = d_normed * gain
    return inverse * (
        scaled
        - jnp.mean(scaled, axis=-1, keepdims=True)
        - hat * jnp.mean(scaled * hat, axis=-1, keepdims=True)
    )


def column_sum(value):
    return jnp.sum(value, axis=0, keepdims=True)


def chunk_loads(index_ref, pieces, unit, target, sems):
    loads = []
    for chunk in range(CHUNKS):
        group = pieces[6 * chunk : 6 * chunk + 6]
        rows = group[0].shape[1]
        loads.append(
            piece_copies(
                index_ref,
                [piece.at[unit] for piece in group],
                lambda to, first, count, chunk=chunk: target(
                    chunk, pl.multiple_of(to * rows + first, 128), count
                ),
                sems.at[chunk],
            )
        )
    return loads


def block_back_body(index_ref, *refs, blocks):
    pieces, refs = refs[: 6 * CHUNKS], refs[6 * CHUNKS :]
    pre_ref, middle_ref, cot_ref, a_ref, b_ref, weight_ref, vec_ref = refs[:7]
    d_middle_ref, d_attended_ref, keep_ref, send_ref, sums_ref = refs[7:12]
    up_ref, d_one_ref, sems = refs[12:]
    step = pl.program_id(0)
    rows = pre_ref.shape[0]
    size = up_ref.shape[1] // CHUNKS

    def rest(d_normed):
        middle = middle_ref[...]
        cot = cot_ref[...].astype(f32)
        hat, inverse = norm_parts(middle)
        d_middle = cot + norm_back(d_normed, hat, inverse, row_of(vec_ref, "ln2_gain"))
        d_one = d_middle.astype(bf16)
        d_middle_ref[...] = d_middle
        d_one_ref[pl.ds(pl.multiple_of(step * rows, rows), rows), :] = d_one
        sums_ref[0:1, :] += column_sum(d_normed * hat)
        sums_ref[1:2, :] += column_sum(d_normed)
        sums_ref[2:3, :] += column_sum(d_one.astype(f32))
        sums_ref[3:4, :] += column_sum(cot)

    @pl.when(step == 0)
    def _():
        loads = chunk_loads(
            index_ref,
            pieces,
            0,
            lambda chunk, first, count: up_ref.at[pl.ds(first, count), chunk * size : (chunk + 1) * size],
            sems,
        )
        for group in loads:
            for copy in group:
                copy.start()
        sums_ref[...] = jnp.zeros_like(sums_ref)
        d_normed = None
        for chunk, group in enumerate(loads):
            for copy in group:
                copy.wait()
            cols = slice(chunk * size, (chunk + 1) * size)
            term = dot(pre_ref[:, cols], up_ref[:, cols], 1, 1)
            d_normed = term if d_normed is None else d_normed + term
        rest(d_normed)

    @pl.when((step > 0) & (step < blocks))
    def _():
        rest(dot(pre_ref[...], up_ref[...], 1, 1))

    for t, k in enumerate((1, 3, 0, 2)):

        @pl.when(step == blocks + t)
        def _(t=t, k=k):
            block = weight_ref.shape[0] // SHARDS
            part = keep_ref.shape[3]
            d_one = d_one_ref[...]
            d_attended_ref[...] = dot(d_one, weight_ref[t * block : (t + 1) * block, :], 1, 1).astype(bf16)
            shard = index_ref[0] ^ k
            target = send_ref if t < 2 else keep_ref
            cols = pl.ds(pl.multiple_of((shard & 1) * block, block), block)

            def put(ref):
                value = dot(ref[:, cols], d_one, 0, 0).astype(bf16)
                for unit in range(2):
                    target[0, unit] = value[:, unit * part : (unit + 1) * part]

            pl.when(shard < 2)(lambda: put(a_ref))
            pl.when(shard >= 2)(lambda: put(b_ref))


def block_back(index, pieces, d_pre, middle, cot, attended, weight, vec, rows_each=256):
    rows, width = middle.shape
    size = d_pre.shape[1]
    blocks = rows // rows_each
    quarter = width // SHARDS

    def by_rows(cols):
        return pl.BlockSpec((rows_each, cols), lambda i, idx: (jnp.minimum(i, blocks - 1), 0))

    grads = (2, 2, quarter, width // 2)
    unit = (1,) + grads[1:]
    half = whole((rows, attended[0].shape[1]))
    return pl.pallas_call(
        functools.partial(block_back_body, blocks=blocks),
        grid_spec=pltpu.PrefetchScalarGridSpec(
            num_scalar_prefetch=1,
            grid=(blocks + SHARDS,),
            in_specs=[any_spec] * (6 * CHUNKS)
            + [
                by_rows(size),
                by_rows(width),
                by_rows(width),
                half,
                half,
                whole((width, width)),
                whole((SHARDS * VEC_ROWS, LANES)),
            ],
            out_specs=[
                by_rows(width),
                pl.BlockSpec((rows, quarter), lambda i, idx: (0, jnp.maximum(i - blocks, 0))),
                pl.BlockSpec(unit, lambda i, idx: (jnp.maximum(i - blocks - 2, 0), 0, 0, 0)),
                pl.BlockSpec(unit, lambda i, idx: (jnp.clip(i - blocks, 0, 1), 0, 0, 0)),
                whole((8, width)),
            ],
            scratch_shapes=[
                pltpu.VMEM((width, size), bf16),
                pltpu.VMEM((rows, width), bf16),
                pltpu.SemaphoreType.DMA((CHUNKS, 6)),
            ],
        ),
        out_shape=[
            jax.ShapeDtypeStruct((rows, width), f32),
            jax.ShapeDtypeStruct((rows, width), bf16),
            jax.ShapeDtypeStruct(grads, bf16),
            jax.ShapeDtypeStruct(grads, bf16),
            jax.ShapeDtypeStruct((8, width), f32),
        ],
        compiler_params=params(48),
        cost_estimate=cost(2 * rows * width * (size + 2 * width), 2 * rows * size + 2 * width * size + 16 * rows * width),
        name="block_back",
    )(index, *pieces, d_pre, middle, cot, *attended, weight, vec)


def block_out_body(index_ref, *refs):
    pieces, (hidden_ref, middle_ref, vec_ref, out_ref, down_ref, sems) = refs[: 6 * CHUNKS], refs[6 * CHUNKS :]
    step = pl.program_id(0)
    size = down_ref.shape[0] // CHUNKS

    def rest(value):
        out_ref[...] = (middle_ref[...] + row_of(vec_ref, "down_bias") + value).astype(bf16)

    @pl.when(step == 0)
    def _():
        loads = chunk_loads(
            index_ref,
            pieces,
            1,
            lambda chunk, first, count: down_ref.at[pl.ds(chunk * size + first, count), :],
            sems,
        )
        for group in loads:
            for copy in group:
                copy.start()
        total = None
        for chunk, group in enumerate(loads):
            for copy in group:
                copy.wait()
            cols = slice(chunk * size, (chunk + 1) * size)
            term = dot(hidden_ref[:, cols], down_ref[cols, :])
            total = term if total is None else total + term
        rest(total)

    @pl.when(step > 0)
    def _():
        rest(dot(hidden_ref[...], down_ref[...]))


def block_output(index, pieces, hidden, middle, vec, rows_each=256):
    rows, width = middle.shape
    size = hidden.shape[1]

    def by_rows(cols):
        return pl.BlockSpec((rows_each, cols), lambda i, idx: (i, 0))

    return pl.pallas_call(
        block_out_body,
        grid_spec=pltpu.PrefetchScalarGridSpec(
            num_scalar_prefetch=1,
            grid=(rows // rows_each,),
            in_specs=[any_spec] * (6 * CHUNKS) + [by_rows(size), by_rows(width), whole((SHARDS * VEC_ROWS, LANES))],
            out_specs=by_rows(width),
            scratch_shapes=[pltpu.VMEM((size, width), bf16), pltpu.SemaphoreType.DMA((CHUNKS, 6))],
        ),
        out_shape=jax.ShapeDtypeStruct((rows, width), bf16),
        compiler_params=params(48),
        cost_estimate=cost(2 * rows * width * size, 2 * rows * size + 2 * width * size + 6 * rows * width),
        name="block_output",
    )(index, *pieces, hidden, middle, vec)


def input_grad_body(index_ref, *refs, blocks):
    parts, weights = refs[:6], refs[6:8]
    tokens_ref, d_middle_ref, vec_ref, sums_ref, bqv_a_ref, bqv_b_ref = refs[8:14]
    bias_refs = refs[14 : 14 + CHUNKS]
    out_ref, grads_ref, gain_ref, shift_ref = refs[14 + CHUNKS :]
    step = pl.program_id(0)

    @pl.when(step == 0)
    def _():
        gain_ref[...] = jnp.zeros_like(gain_ref)
        shift_ref[...] = jnp.zeros_like(shift_ref)

    d_normed = None
    for half in range(2):
        for i in range(3):
            ref = parts[3 * half + i]
            part = ref.shape[1]
            term = dot(ref[...], weights[half][:, i * part : (i + 1) * part], 1, 1)
            d_normed = term if d_normed is None else d_normed + term
    hat, inverse = norm_parts(tokens_ref[...].astype(f32))
    out_ref[...] = d_middle_ref[...] + norm_back(d_normed, hat, inverse, row_of(vec_ref, "ln1_gain"))
    gain_ref[...] += column_sum(d_normed * hat)
    shift_ref[...] += column_sum(d_normed)

    @pl.when(step == blocks - 1)
    def _():
        grads_ref[...] = jnp.zeros_like(grads_ref)

        def put(name, shard, value, offset=0):
            first = shard * VEC_ROWS + VEC[name][0] + offset
            for i in range(value.shape[1] // LANES):
                grads_ref[first + i : first + i + 1, :] = value[:, i * LANES : (i + 1) * LANES]

        for shard in range(SHARDS):
            cols = slice(shard * 256, (shard + 1) * 256)
            put("ln1_gain", shard, gain_ref[:, cols])
            put("ln1_bias", shard, shift_ref[:, cols])
            put("ln2_gain", shard, sums_ref[0:1, cols])
            put("ln2_bias", shard, sums_ref[1:2, cols])
            put("out_bias", shard, sums_ref[2:3, cols])
            put("down_bias", shard, sums_ref[3:4, cols])
            source = bqv_a_ref if shard % 2 == 0 else bqv_b_ref
            put("b_qv", shard, source[shard // 2 : shard // 2 + 1, :])
            for chunk in range(CHUNKS):
                size = bias_refs[chunk].shape[1] // SHARDS
                put("up_bias", shard, bias_refs[chunk][:, shard * size : (shard + 1) * size], chunk)


def input_gradient(index, parts, weights, tokens, d_middle, vec, sums, bqv, biases, rows_each=256):
    rows, width = tokens.shape
    part = parts[0].shape[1]
    blocks = rows // rows_each

    def by_rows(cols):
        return pl.BlockSpec((rows_each, cols), lambda i, idx: (i, 0))

    return pl.pallas_call(
        functools.partial(input_grad_body, blocks=blocks),
        grid_spec=pltpu.PrefetchScalarGridSpec(
            num_scalar_prefetch=1,
            grid=(blocks,),
            in_specs=[by_rows(part)] * 6
            + [whole((width, 3 * part))] * 2
            + [by_rows(width), by_rows(width), whole((SHARDS * VEC_ROWS, LANES)), whole((8, width))]
            + [whole((2, part))] * 2
            + [whole(bias.shape) for bias in biases],
            out_specs=[by_rows(width), whole((SHARDS * VEC_ROWS, LANES))],
            scratch_shapes=[pltpu.VMEM((1, width), f32), pltpu.VMEM((1, width), f32)],
        ),
        out_shape=[
            jax.ShapeDtypeStruct((rows, width), f32),
            jax.ShapeDtypeStruct((SHARDS * VEC_ROWS, LANES), f32),
        ],
        compiler_params=params(40),
        cost_estimate=cost(12 * rows * width * part, 10 * rows * width + 12 * rows * part + 12 * width * part),
        name="input_gradient",
    )(index, *parts, *weights, tokens, d_middle, vec, sums, *bqv, *biases)


def place_body(index_ref, pair_ref, other_ref, *refs, plan, fresh):
    outs = len(refs) - 2 if fresh else (len(refs) - 2) // 2
    out_refs = refs[-2 - outs : -2]
    scratch, sems = refs[-2:]
    low, mid = index_ref[1], index_ref[2]
    rows = pair_ref.shape[2]
    for a, ref in enumerate((pair_ref, other_ref)):
        for b in range(2):
            first = pl.multiple_of((low ^ a) * (2 * rows) + (mid ^ b) * rows, rows)
            for u in range(pair_ref.shape[1]):
                scratch[u, pl.ds(first, rows), :] = ref[b, u].astype(f32)
    copies = []
    for i, (unit, cols, width, out, row, col) in enumerate(plan):
        copies.append(
            pltpu.make_async_copy(
                scratch.at[unit, :, cols : cols + width],
                out_refs[out].at[row : row + 4 * rows, col : col + width],
                sems.at[i],
            )
        )
    for copy in copies:
        copy.start()
    for copy in copies:
        copy.wait()


def place(index, pieces, plan, shapes, carried, name):
    pair, other = pieces
    _, units, rows, width = pair.shape
    fresh = carried is None
    count = len(shapes)
    return pl.pallas_call(
        functools.partial(place_body, plan=plan, fresh=fresh),
        grid_spec=pltpu.PrefetchScalarGridSpec(
            num_scalar_prefetch=1,
            grid=(1,),
            in_specs=[whole(pair.shape), whole(other.shape)] + ([] if fresh else [any_spec] * count),
            out_specs=[any_spec] * count,
            scratch_shapes=[pltpu.VMEM((units, 4 * rows, width), f32), pltpu.SemaphoreType.DMA((len(plan),))],
        ),
        out_shape=[jax.ShapeDtypeStruct(shape, f32) for shape in shapes],
        input_output_aliases={} if fresh else {3 + i: i for i in range(count)},
        compiler_params=params(16),
        cost_estimate=cost(units * 4 * rows * width, units * 4 * rows * width * 6),
        name=name,
    )(index, pair, other, *(carried or ()))


def body(
    mesh,
    tokens,
    piece_start,
    ln1_gain,
    ln1_bias,
    query_key_value_weight,
    b_qv,
    attention_out_weight,
    attention_out_bias,
    ln2_gain,
    ln2_bias,
    up_weight,
    up_bias,
    down_weight,
    down_bias,
    cotangent,
):
    count, seq_len, width = tokens.shape
    rows = count * seq_len
    hidden_size = up_weight.shape[1]
    tokens = tokens.reshape(rows, width)
    cot = cotangent.reshape(rows, width)
    moves = Moves(mesh, piece_start)
    half = width // 2
    size = hidden_size // CHUNKS
    block = size // SHARDS

    def as_rows(value):
        return value.reshape(-1, LANES)

    def joined_cols(which):
        return jnp.concatenate(
            [
                query_key_value_weight[:, i * width + which * half : i * width + (which + 1) * half]
                for i in range(3)
            ],
            axis=1,
        )

    own_a = joined_cols(0)
    own_vec = jnp.concatenate(
        [
            as_rows(after(value, own_a))
            for value in (ln1_gain, ln1_bias, b_qv, attention_out_bias, ln2_gain, ln2_bias, up_bias, down_bias)
        ]
        + [jnp.zeros((VEC_ROWS - 12, LANES), bf16)]
    )

    def hidden_own(chunk):
        up = jnp.concatenate(
            [
                up_weight[:, s * size + chunk * block : s * size + (chunk + 1) * block]
                for s in range(SHARDS)
            ],
            axis=1,
        )
        return jnp.stack([up, down_weight[chunk * block : (chunk + 1) * block, :]])

    far_a = moves.across(own_a)
    near_a = moves.core(own_a)
    far_vec = moves.across(own_vec)
    near_vec = moves.core(own_vec)
    own_b = joined_cols(1)
    half_b = moves.half(own_b)
    hidden_owns = [hidden_own(chunk) for chunk in range(CHUNKS)]
    hidden_halves = [moves.half(own) for own in hidden_owns]
    out_half = moves.half(attention_out_weight)
    far_near_vec = moves.core(far_vec)
    moves.wait(half_b, out_half, *hidden_halves)
    normed, vec = first_norm(moves.index, tokens, (own_vec, near_vec, far_vec, far_near_vec))
    moves.ran(vec)

    joined, joined_weight, attended, totals = [None] * 2, [None] * 2, [None] * 2, [None] * 2
    hidden_far, hidden_near, hidden_other = [None] * CHUNKS, [None] * CHUNKS, [None] * CHUNKS
    hidden_pieces = [None] * CHUNKS

    def fetch(chunk, kernels):
        hidden_far[chunk] = moves.across(hidden_halves[chunk])
        hidden_near[chunk] = moves.core(hidden_owns[chunk])
        moves.by(kernels, hidden_far[chunk], hidden_near[chunk])

    def relay(chunk, kernels):
        hidden_other[chunk] = moves.rep(hidden_far[chunk], 1)
        moves.by(kernels, hidden_other[chunk])

    far_b = moves.across(half_b)
    near_b = moves.core(own_b)
    moves.by(1, far_b, near_b)
    joined[0], joined_weight[0] = joined_product(
        0, moves.index, (own_a, near_a, far_a, moves.core(far_a)), normed, vec
    )
    moves.ran(joined[0])
    other_b = moves.rep(far_b, 1)
    moves.by(1, other_b)
    fetch(0, 1)
    attended[0], totals[0] = attend_forward(0, moves.index, joined[0])
    moves.ran(totals[0])
    relay(0, 2)
    out_far = moves.across(out_half)
    out_near = moves.core(attention_out_weight)
    moves.by(1, out_far, out_near)
    joined[1], joined_weight[1] = joined_product(
        1, moves.index, (own_b, near_b, far_b, other_b, moves.core(far_b), moves.core(other_b)), normed, vec
    )
    moves.ran(joined[1])
    out_other = moves.rep(out_far, 1)
    moves.by(1, out_other)
    fetch(1, 1)
    attended[1], totals[1] = attend_forward(1, moves.index, joined[1])
    moves.ran(totals[1])
    relay(1, 2)
    fetch(2, 2)
    middle, normed_two, out_weight = middle_product(
        moves.index,
        (attention_out_weight, out_near, out_far, out_other, moves.core(out_far), moves.core(out_other)),
        attended,
        tokens,
        vec,
    )
    moves.ran(normed_two)

    carried = None
    shard_sums, up_biases = [], []

    def hidden_step(chunk):
        nonlocal carried
        far, other = hidden_far[chunk], hidden_other[chunk]
        hidden_pieces[chunk] = (
            hidden_owns[chunk],
            hidden_near[chunk],
            far,
            other,
            moves.core(far),
            moves.core(other),
        )
        *carried, keep, send, bias = hidden_chunk(
            chunk, moves.index, hidden_pieces[chunk], carried, normed_two, cot, vec, hidden_size
        )
        moves.ran(bias)
        up_biases.append(bias)
        shard_sums.append(ShardSum(moves, keep, send))

    fetch(3, 1)
    hidden_step(0)
    relay(2, 1)
    hidden_step(1)
    relay(3, 1)
    shard_sums[0].cross(1)
    hidden_step(2)
    shard_sums[1].cross(1)
    hidden_step(3)
    shard_sums[2].cross(1)
    first_sum = RepSum(moves, shard_sums[:2])
    all_pieces = [piece for pieces in hidden_pieces for piece in pieces]
    hidden, d_pre = carried
    d_middle, d_attended, keep, send, sums = block_back(
        moves.index, all_pieces, d_pre, middle, cot, attended, out_weight, vec
    )
    moves.ran(sums)
    parts, bqv = [], []

    def backward(which):
        *grads, keep, send, bias = attend_backward(
            which, moves.index, joined[which], attended[which], d_attended, totals[which], normed
        )
        parts.extend(grads)
        bqv.append(bias)
        moves.ran(bias)
        return ShardSum(moves, keep, send)

    shard_sums[3].cross(1)
    out_sum = ShardSum(moves, keep, send)
    first_sum.split()
    second_sum = RepSum(moves, shard_sums[2:3])
    a_sum = backward(0)
    out_sum.cross(1)
    first_sum.add()
    second_sum.split()
    third_sum = RepSum(moves, shard_sums[3:4])
    b_sum = backward(1)
    a_sum.cross(1)
    first_sum.spread()
    second_sum.add()
    third_sum.split()
    input_grad, vec_grads = input_gradient(
        moves.index, parts, joined_weight, tokens, d_middle, vec, sums, bqv, up_biases
    )
    moves.ran(vec_grads)
    b_sum.cross(1)
    fourth_sum = RepSum(moves, [out_sum, a_sum])
    first_sum.finish()
    second_sum.spread()
    third_sum.add()
    block_out = block_output(moves.index, all_pieces, hidden, middle, vec)
    moves.ran(block_out)

    def place_hidden(chunks, pieces, grads, name):
        plan = []
        for i, chunk in enumerate(chunks):
            plan += [(2 * i, s * block, block, 0, 0, s * size + chunk * block) for s in range(SHARDS)]
            plan += [(2 * i + 1, 0, width, 1, chunk * block, 0)]
        shapes = [(width // SHARDS, hidden_size), (size, width)]
        grads = place(moves.index, pieces, plan, shapes, grads, name)
        moves.ran(grads[0])
        return grads

    last_sum = RepSum(moves, [b_sum])
    fourth_sum.split()
    second_sum.finish()
    third_sum.spread()
    vec_sum = VecSum(moves, vec_grads)
    grads = place_hidden((0, 1), first_sum.pieces(), None, "place_hidden_first")
    last_sum.split()
    fourth_sum.add()
    third_sum.finish()
    vec_sum.step()
    grads = place_hidden((2,), second_sum.pieces(), grads, "place_hidden_second")
    last_sum.add()
    fourth_sum.spread()
    vec_sum.step()
    grad_up, grad_down = place_hidden((3,), third_sum.pieces(), grads, "place_hidden_third")
    fourth_sum.finish()
    last_sum.spread()
    vec_sum.step()
    last_sum.finish()
    vec_sum = vec_sum.rest()
    third = width // SHARDS
    plan = [(i, 0, half, 0, 0, i * half) for i in range(2)]
    plan += [(2 + i, 0, half, 1, 0, i * width) for i in range(3)]
    shapes = [(third, width), (third, 3 * width)]
    grad_out, grad_joined = place(moves.index, fourth_sum.pieces(), plan, shapes, None, "place_fourth")
    plan = [(i, 0, half, 0, 0, i * width + half) for i in range(3)]
    (grad_joined,) = place(moves.index, last_sum.pieces(), plan, shapes[1:], (grad_joined,), "place_last")

    def vec_part(name):
        first, count = VEC[name]
        return vec_sum[first : first + count].reshape(count * LANES)

    return (
        block_out.reshape(count, seq_len, width),
        input_grad.reshape(count, seq_len, width),
        vec_part("ln1_gain"),
        vec_part("ln1_bias"),
        grad_joined,
        vec_part("b_qv"),
        grad_out,
        vec_part("out_bias"),
        vec_part("ln2_gain"),
        vec_part("ln2_bias"),
        grad_up,
        vec_part("up_bias"),
        grad_down,
        vec_part("down_bias"),
    )


def solution(mesh):
    batch = P(("shard", "rep"), None, None)
    vector, matrix = P("shard"), P("shard", None)
    in_specs = (
        batch,
        P(("shard", "rep")),
        vector,
        vector,
        matrix,
        vector,
        matrix,
        vector,
        vector,
        vector,
        matrix,
        vector,
        matrix,
        vector,
        batch,
    )
    out_specs = (
        batch,
        batch,
        vector,
        vector,
        matrix,
        vector,
        matrix,
        vector,
        vector,
        vector,
        matrix,
        vector,
        matrix,
        vector,
    )
    return jax.shard_map(
        functools.partial(body, mesh), mesh=mesh, in_specs=in_specs, out_specs=out_specs, check_vma=False
    )
```

```python
import functools

import jax
import jax.numpy as jnp
from jax import lax
from jax.experimental import pallas as pl
from jax.experimental.pallas import tpu as pltpu
from jax.sharding import PartitionSpec as P

HEADS = 16
PIECE = 256
HEAD_DIM = 64
PAIR = 2 * HEAD_DIM
SHARDS = 4
CHUNKS = 4
EPS = 1e-05
HIDDEN_PENALTY = 1e33

bf16 = jnp.bfloat16
f32 = jnp.float32

VEC = {
    "ln1_gain": (0, 1),
    "ln1_bias": (1, 1),
    "b_qv": (2, 2),
    "out_bias": (4, 1),
    "ln2_gain": (5, 1),
    "ln2_bias": (6, 1),
    "up_bias": (7, 4),
    "down_bias": (11, 1),
}
VEC_ROWS = 16
LANES = 256

any_spec = pl.BlockSpec(memory_space=pltpu.MemorySpace.HBM)


def dot(left, right, left_dim=1, right_dim=0):
    return lax.dot_general(
        left, right, (((left_dim,), (right_dim,)), ((), ())), preferred_element_type=f32
    )


def params(mib):
    return pltpu.CompilerParams(vmem_limit_bytes=int(mib * 2**20))


def cost(flops, moved, transcendentals=0, scale=8):
    return pl.CostEstimate(
        flops=int(scale * flops), bytes_accessed=int(scale * moved), transcendentals=int(scale * transcendentals)
    )


def vec_rows(vec_ref, rows):
    firsts = [shard * VEC_ROWS + row for shard, row in rows]
    return jnp.concatenate([vec_ref[first : first + 1, :] for first in firsts], axis=1)


def row_of(vec_ref, name):
    return vec_rows(vec_ref, [(shard, VEC[name][0]) for shard in range(SHARDS)])


def whole(shape):
    return pl.BlockSpec(shape, lambda *_: (0,) * len(shape))


def flip(value, axis, size, bit):
    return lax.ppermute(value, axis, [(i, i ^ bit) for i in range(size)])


class Moves:
    def __init__(self, mesh, starts):
        self.reps = mesh.shape["rep"]
        assert mesh.shape["shard"] == SHARDS and self.reps % 4 == 0
        self.shard = lax.axis_index("shard")
        rep = lax.axis_index("rep")
        self.low = rep & 1
        self.mid = (rep >> 1) & 1
        self.index = jnp.concatenate(
            [jnp.stack([self.shard, self.low, self.mid]).astype(jnp.int32), starts]
        )
        self.last = ()
        self.count = 0
        self.due = []

    def wait(self, *values):
        self.index = after(self.index, *values, *self.last)

    def by(self, kernels, *values):
        self.due.append((self.count + kernels, values))

    def ran(self, value):
        self.last = (value,)
        self.count += 1
        ready = [value for when, values in self.due if when <= self.count for value in values]
        self.due = [entry for entry in self.due if entry[0] > self.count]
        self.wait(*ready)
        return value

    def move(self, value, axis, size, bit):
        return flip(after(value, *self.last), axis, size, bit)

    def core(self, value):
        return self.move(value, "shard", SHARDS, 1)

    def across(self, value):
        return self.move(value, "shard", SHARDS, 2)

    def rep(self, value, bit):
        return self.move(value, "rep", self.reps, bit)

    def half(self, own):
        rows = own.shape[-2] // 2
        return lax.dynamic_slice_in_dim(own, self.low * rows, rows, own.ndim - 2)

    def pick(self, value, which, size):
        return lax.dynamic_slice_in_dim(value, which * size, size, 1)


def after(value, *earlier):
    return lax.optimization_barrier((value, *earlier))[0] if earlier else value


class ShardSum:
    def __init__(self, moves, keep, send, kernels=1):
        self.moves, self.keep = moves, keep
        self.got = moves.core(send)
        moves.by(kernels, self.got)

    def cross(self, kernels):
        self.got = after(self.got, *self.moves.last)
        out = self.keep[1] + self.got[1]
        self.mine = self.keep[0] + self.got[0]
        self.moves.wait(out, self.mine)
        self.got = self.moves.across(out)
        self.moves.by(kernels, self.got)

    def halves(self):
        moves, mine = self.moves, self.mine
        got = after(self.got, *moves.last)
        size = mine.shape[1] // 2
        return [
            moves.pick(mine, which, size) + moves.pick(got, which, size)
            for which in (moves.low, 1 - moves.low)
        ]


class RepSum:
    def __init__(self, moves, sums, kernels=1):
        self.moves = moves
        halves = [s.halves() for s in sums]
        self.mine = jnp.concatenate([h[0] for h in halves])
        self.bit = 2
        self.send(jnp.concatenate([h[1] for h in halves]), 1, kernels)

    def send(self, out, bit, kernels):
        self.moves.wait(out, self.mine)
        self.got = self.moves.rep(out, bit)
        self.moves.by(kernels, self.got)

    def split(self, kernels=1):
        moves = self.moves
        got = after(self.got, *moves.last)
        size = self.mine.shape[1] // 2
        out, self.mine = [
            moves.pick(self.mine, which, size) + moves.pick(got, which, size)
            for which in (1 - moves.mid, moves.mid)
        ]
        self.send(out, 2, kernels)

    def add(self, kernels=1):
        self.mine = self.mine + after(self.got, *self.moves.last)
        self.bit *= 2
        self.got = None
        if self.bit < self.moves.reps:
            self.send(self.mine, self.bit, kernels)

    def spread(self, kernels=1):
        while self.got is not None:
            self.add()
        self.send(self.mine, 2, kernels)

    def finish(self, kernels=1):
        self.pair = jnp.stack([self.mine, after(self.got, *self.moves.last)])
        self.send(self.pair, 1, kernels)

    def pieces(self):
        self.moves.wait(self.got)
        return (self.pair, self.got)


class VecSum:
    def __init__(self, moves, value):
        self.moves, self.value = moves, value
        self.plan = [moves.core, moves.across]
        bit = 1
        while bit < moves.reps:
            self.plan.append(functools.partial(moves.rep, bit=bit))
            bit *= 2
        self.at = 0
        self.send()

    def send(self):
        self.got = self.plan[self.at](self.value)
        self.moves.by(1, self.got)
        self.at += 1

    def step(self):
        moves = self.moves
        self.value = self.value + after(self.got, *moves.last)
        if self.at == 2:
            self.value = lax.dynamic_slice_in_dim(self.value, moves.shard * VEC_ROWS, VEC_ROWS, 0)
        moves.wait(self.value)
        if self.at < len(self.plan):
            self.send()

    def rest(self):
        while self.at < len(self.plan):
            self.step()
        self.step()
        return self.value


def piece_copies(index_ref, pieces, target, sems):
    shard, low = index_ref[0], index_ref[1]
    rows = pieces[0].shape[-2]
    if len(pieces) == 4:
        plan = [(piece, shard ^ k, 0, rows) for k, piece in enumerate(pieces)]
    else:
        own, near, far, far_other, far_near, far_other_near = pieces
        half = rows // 2
        plan = (
            (own, shard, 0, rows),
            (near, shard ^ 1, 0, rows),
            (far, shard ^ 2, low * half, half),
            (far_other, shard ^ 2, (1 - low) * half, half),
            (far_near, shard ^ 3, low * half, half),
            (far_other_near, shard ^ 3, (1 - low) * half, half),
        )
    return [
        pltpu.make_async_copy(source, target(to, first, count), sems.at[i])
        for i, (source, to, first, count) in enumerate(plan)
    ]


def norm_parts(value):
    center = value - jnp.mean(value, axis=-1, keepdims=True)
    inverse = lax.rsqrt(jnp.mean(center * center, axis=-1, keepdims=True) + EPS)
    return center * inverse, inverse


def first_norm_body(index_ref, tokens_ref, own_ref, near_ref, far_ref, far_near_ref, normed_ref, vec_ref):
    shard = index_ref[0]

    @pl.when(pl.program_id(0) == 0)
    def _():
        for k, ref in enumerate((own_ref, near_ref, far_ref, far_near_ref)):
            vec_ref[pl.ds(pl.multiple_of((shard ^ k) * VEC_ROWS, VEC_ROWS), VEC_ROWS), :] = ref[...].astype(f32)

    hat, _ = norm_parts(tokens_ref[...].astype(f32))
    normed_ref[...] = (hat * row_of(vec_ref, "ln1_gain") + row_of(vec_ref, "ln1_bias")).astype(bf16)


def first_norm(index, tokens, vec_pieces, block=256):
    rows, width = tokens.shape
    row = pl.BlockSpec((block, width), lambda i, idx: (i, 0))
    return pl.pallas_call(
        first_norm_body,
        grid_spec=pltpu.PrefetchScalarGridSpec(
            num_scalar_prefetch=1,
            grid=(rows // block,),
            in_specs=[row] + [whole((VEC_ROWS, LANES))] * 4,
            out_specs=[row, whole((SHARDS * VEC_ROWS, LANES))],
        ),
        out_shape=[
            jax.ShapeDtypeStruct((rows, width), bf16),
            jax.ShapeDtypeStruct((SHARDS * VEC_ROWS, LANES), f32),
        ],
        compiler_params=params(16),
        cost_estimate=cost(20 * rows * width, 4 * rows * width),
        name="first_norm",
    )(index, tokens, *vec_pieces)


def joined_body(half, index_ref, *refs):
    pieces, (normed_ref, vec_ref, out_ref, weight_ref, sems) = refs[:-5], refs[-5:]

    @pl.when(pl.program_id(0) == 0)
    def _():
        rows = pieces[0].shape[0]
        copies = piece_copies(
            index_ref,
            pieces,
            lambda to, first, count: weight_ref.at[
                pl.ds(pl.multiple_of(to * rows + first, 128), count), :
            ],
            sems,
        )
        for copy in copies:
            copy.start()
        for copy in copies:
            copy.wait()

    part = weight_ref.shape[1] // 3
    first = VEC["b_qv"][0]
    normed = normed_ref[...]
    for i in range(3):
        cols = slice(i * part, (i + 1) * part)
        value = dot(normed, weight_ref[:, cols])
        if i != 1:
            shard = half if i == 0 else 2 + half
            value = value + vec_rows(vec_ref, [(shard, first), (shard, first + 1)])
        out_ref[:, cols] = value.astype(bf16)


def joined_product(half, index, pieces, normed, vec, block=256):
    rows, width = normed.shape
    cols = pieces[0].shape[1]
    return pl.pallas_call(
        functools.partial(joined_body, half),
        grid_spec=pltpu.PrefetchScalarGridSpec(
            num_scalar_prefetch=1,
            grid=(rows // block,),
            in_specs=[any_spec] * len(pieces)
            + [pl.BlockSpec((block, width), lambda i, idx: (i, 0)), whole((SHARDS * VEC_ROWS, LANES))],
            out_specs=pl.BlockSpec((block, cols), lambda i, idx: (i, 0)),
            scratch_shapes=[pltpu.VMEM((width, cols), bf16), pltpu.SemaphoreType.DMA((6,))],
        ),
        out_shape=jax.ShapeDtypeStruct((rows, cols), bf16),
        compiler_params=params(24),
        cost_estimate=cost(2 * rows * width * cols, 2 * (rows * width + rows * cols + 2 * width * cols)),
        name="joined_product",
    )(index, *pieces, normed, vec)


def penalty(start, seq_len):
    key = lax.broadcasted_iota(jnp.int32, (seq_len, seq_len), 0)
    query = lax.broadcasted_iota(jnp.int32, (seq_len, seq_len), 1)
    key_in = (key >= start) & (key < start + PIECE)
    query_in = (query >= start) & (query < start + PIECE)
    seen = (key <= query) | (key_in & query_in)
    return jnp.where(seen, jnp.abs(key - query).astype(f32), HIDDEN_PENALTY)


def slope_of(head):
    return jnp.exp2((jnp.full((1, 1), head, jnp.int32).astype(f32) + 1.0) * (-8.0 / HEADS))


def attend_forward_body(first_head, start_ref, q_ref, k_ref, v_ref, out_ref, total_ref, pen_ref):
    pair = pl.program_id(1)
    seq_len = q_ref.shape[0]

    @pl.when(pair == 0)
    def _():
        pen_ref[...] = penalty(start_ref[3 + pl.program_id(0)], seq_len)

    queries, keys = q_ref[...], k_ref[...]
    values_t = v_ref[...].T
    lane = lax.broadcasted_iota(jnp.int32, (seq_len, PAIR), 1)
    outs = []
    for e in range(2):
        chosen = (lane < HEAD_DIM) if e == 0 else (lane >= HEAD_DIM)
        key_e = jnp.where(chosen, keys * (HEAD_DIM**-0.5), 0).astype(bf16)
        scores = dot(key_e, queries, 1, 1) - slope_of(first_head + 2 * pair + e) * pen_ref[...]
        top = jnp.max(scores, axis=0, keepdims=True)
        weight = jnp.exp(scores - top)
        total = jnp.sum(weight, axis=0, keepdims=True)
        out_t = dot(values_t[e * HEAD_DIM : (e + 1) * HEAD_DIM, :], weight.astype(bf16))
        outs.append(out_t * (1.0 / total))
        total_ref[0, 0, e : e + 1, :] = top + jnp.log(total)
    out_ref[...] = jnp.concatenate(outs, axis=0).T.astype(bf16)


def attend_forward(half, index, joined):
    count = index.shape[0] - 3
    seq_len, width = joined.shape[0] // count, joined.shape[1] // 3
    pairs = width // PAIR

    def cols(first):
        return pl.BlockSpec((seq_len, PAIR), lambda s, h, st: (s, first + h))

    return pl.pallas_call(
        functools.partial(attend_forward_body, half * 2 * pairs),
        grid_spec=pltpu.PrefetchScalarGridSpec(
            num_scalar_prefetch=1,
            grid=(count, pairs),
            in_specs=[cols(0), cols(pairs), cols(2 * pairs)],
            out_specs=[cols(0), pl.BlockSpec((1, 1, 2, seq_len), lambda s, h, st: (s, h, 0, 0))],
            scratch_shapes=[pltpu.VMEM((seq_len, seq_len), f32)],
        ),
        out_shape=[
            jax.ShapeDtypeStruct((count * seq_len, width), bf16),
            jax.ShapeDtypeStruct((count, pairs, 2, seq_len), f32),
        ],
        compiler_params=params(24),
        cost_estimate=cost(
            24 * count * seq_len * seq_len * width, 8 * count * seq_len * width, count * seq_len * seq_len * 2 * pairs
        ),
        name="attend_forward",
    )(index, joined, joined, joined)


def attend_backward_body(
    first_head,
    steps,
    index_ref,
    q_ref,
    k_ref,
    v_ref,
    out_ref,
    dout_ref,
    total_ref,
    normed_ref,
    dq_ref,
    dk_ref,
    dv_ref,
    keep_ref,
    send_ref,
    sums_ref,
    pen_ref,
):
    step = pl.program_id(0)
    seq_len = q_ref.shape[0]
    scale = HEAD_DIM**-0.5
    pairs = dq_ref.shape[1] // PAIR
    seq, pair = step // pairs, step % pairs

    @pl.when((step < steps) & (pair == 0))
    def _():
        pen_ref[...] = penalty(index_ref[3 + seq], seq_len)

    @pl.when(step < steps)
    def _():
        queries, keys, values, d_out = q_ref[...], k_ref[...], v_ref[...], dout_ref[...]
        lane = lax.broadcasted_iota(jnp.int32, (seq_len, PAIR), 1)
        keys_t = keys.T
        both_t = (d_out.astype(f32) * out_ref[...].astype(f32)).T
        d_q, d_k, d_v = [], [], []
        for e in range(2):
            chosen = (lane < HEAD_DIM) if e == 0 else (lane >= HEAD_DIM)
            part = slice(e * HEAD_DIM, (e + 1) * HEAD_DIM)
            key_e = jnp.where(chosen, keys * scale, 0).astype(bf16)
            value_e = jnp.where(chosen, values, 0)
            inner = jnp.sum(both_t[part, :], axis=0, keepdims=True)
            scores = dot(key_e, queries, 1, 1) - slope_of(first_head + 2 * pair + e) * pen_ref[...]
            probs = jnp.exp(scores - total_ref[0, 0, e : e + 1, :])
            d_scores = (probs * (dot(value_e, d_out, 1, 1) - inner)).astype(bf16)
            d_v.append(dot(probs.astype(bf16), d_out))
            d_k.append(dot(d_scores, queries))
            d_q.append(dot(keys_t[part, :], d_scores))
        rows = pl.ds(pl.multiple_of(seq * seq_len, seq_len), seq_len)
        cols = pl.ds(pl.multiple_of(pair * PAIR, PAIR), PAIR)
        dq_ref[rows, cols] = (jnp.concatenate(d_q, axis=0) * scale).T.astype(bf16)
        dk_ref[rows, cols] = (jnp.where(lane < HEAD_DIM, d_k[0], d_k[1]) * scale).astype(bf16)
        dv_ref[rows, cols] = jnp.where(lane < HEAD_DIM, d_v[0], d_v[1]).astype(bf16)

    @pl.when(step == steps)
    def _():
        sums_ref[0:1, :] = column_sum(dq_ref[...].astype(f32))
        sums_ref[1:2, :] = column_sum(dv_ref[...].astype(f32))

    @pl.when(step >= steps)
    def _():
        block = keep_ref.shape[2]
        t = step - steps
        k = jnp.where(t < 2, 2 * t + 1, 2 * t - 4)
        left = normed_ref[:, pl.ds(pl.multiple_of((index_ref[0] ^ k) * block, block), block)]
        for i, ref in enumerate((dq_ref, dk_ref, dv_ref)):
            value = dot(left, ref[...], 0, 0).astype(bf16)

            @pl.when(t < 2)
            def _(i=i, value=value):
                send_ref[0, i] = value

            @pl.when(t >= 2)
            def _(i=i, value=value):
                keep_ref[0, i] = value


def attend_backward(half, index, joined, attended, d_attended, totals, normed):
    count = index.shape[0] - 3
    rows, width = joined.shape[0], joined.shape[1] // 3
    seq_len = rows // count
    pairs = width // PAIR
    steps = count * pairs
    model = normed.shape[1]

    def cols(first):
        def where(i, idx):
            at = jnp.minimum(i, steps - 1)
            return (at // pairs, first + at % pairs)

        return pl.BlockSpec((seq_len, PAIR), where)

    def totals_at(i, idx):
        at = jnp.minimum(i, steps - 1)
        return (at // pairs, at % pairs, 0, 0)

    grads = (2, 3, model // SHARDS, width)
    unit = (1,) + grads[1:]
    return pl.pallas_call(
        functools.partial(attend_backward_body, half * 2 * pairs, steps),
        grid_spec=pltpu.PrefetchScalarGridSpec(
            num_scalar_prefetch=1,
            grid=(steps + SHARDS,),
            in_specs=[
                cols(0),
                cols(pairs),
                cols(2 * pairs),
                cols(0),
                cols(half * pairs),
                pl.BlockSpec((1, 1, 2, seq_len), totals_at),
                whole((rows, model)),
            ],
            out_specs=[whole((rows, width))] * 3
            + [
                pl.BlockSpec(unit, lambda i, idx: (jnp.clip(i - steps - 2, 0, 1), 0, 0, 0)),
                pl.BlockSpec(unit, lambda i, idx: (jnp.clip(i - steps, 0, 1), 0, 0, 0)),
                whole((2, width)),
            ],
            scratch_shapes=[pltpu.VMEM((seq_len, seq_len), f32)],
        ),
        out_shape=[jax.ShapeDtypeStruct((rows, width), bf16)] * 3
        + [
            jax.ShapeDtypeStruct(grads, bf16),
            jax.ShapeDtypeStruct(grads, bf16),
            jax.ShapeDtypeStruct((2, width), f32),
        ],
        compiler_params=params(40),
        cost_estimate=cost(
            36 * rows * seq_len * width + 6 * rows * model * width, 16 * rows * width, rows * seq_len * 2 * pairs
        ),
        name="attend_backward",
    )(index, joined, joined, joined, attended, d_attended, totals, normed)


def middle_body(index_ref, *refs):
    pieces, (a_ref, b_ref, tokens_ref, vec_ref, middle_ref, normed_ref, weight_ref, sems) = refs[:6], refs[6:]

    @pl.when(pl.program_id(0) == 0)
    def _():
        rows = pieces[0].shape[0]
        copies = piece_copies(
            index_ref,
            pieces,
            lambda to, first, count: weight_ref.at[
                pl.ds(pl.multiple_of(to * rows + first, 128), count), :
            ],
            sems,
        )
        for copy in copies:
            copy.start()
        for copy in copies:
            copy.wait()

    part = a_ref.shape[1]
    middle = tokens_ref[...].astype(f32) + row_of(vec_ref, "out_bias")
    middle = middle + dot(a_ref[...], weight_ref[:part, :]) + dot(b_ref[...], weight_ref[part:, :])
    middle_ref[...] = middle
    hat, _ = norm_parts(middle)
    normed_ref[...] = (hat * row_of(vec_ref, "ln2_gain") + row_of(vec_ref, "ln2_bias")).astype(bf16)


def middle_product(index, pieces, attended, tokens, vec, block=256):
    rows, width = tokens.shape
    row = pl.BlockSpec((block, width), lambda i, idx: (i, 0))
    part = pl.BlockSpec((block, attended[0].shape[1]), lambda i, idx: (i, 0))
    return pl.pallas_call(
        middle_body,
        grid_spec=pltpu.PrefetchScalarGridSpec(
            num_scalar_prefetch=1,
            grid=(rows // block,),
            in_specs=[any_spec] * 6 + [part, part, row, whole((SHARDS * VEC_ROWS, LANES))],
            out_specs=[row, row, whole((width, width))],
            scratch_shapes=[pltpu.SemaphoreType.DMA((6,))],
        ),
        out_shape=[
            jax.ShapeDtypeStruct((rows, width), f32),
            jax.ShapeDtypeStruct((rows, width), bf16),
            jax.ShapeDtypeStruct((width, width), bf16),
        ],
        compiler_params=params(24),
        cost_estimate=cost(2 * rows * width * width, 10 * rows * width + 4 * width * width),
        name="middle_product",
    )(index, *pieces, *attended, tokens, vec)


def gelu_and_slope(pre):
    cube = 0.044715 * pre * pre
    inner = jnp.tanh(0.7978845608028654 * (pre + cube * pre))
    half = 0.5 * (1.0 + inner)
    slope = half + 0.5 * pre * (1.0 - inner * inner) * (0.7978845608028654 * (1.0 + 3.0 * cube))
    return pre * half, slope


def hidden_body(chunk, fresh, index_ref, *refs):
    pieces, refs = refs[:6], refs[6:]
    if not fresh:
        refs = refs[2:]
    normed_hbm, cot_hbm, vec_ref = refs[:3]
    hidden_out, pre_out, keep_ref, send_ref, bias_ref = refs[3:8]
    normed_ref, cot_ref, up_ref, down_ref, hidden_ref, pre_ref, slope_ref, sems, whole_sems = refs[8:]
    step = pl.program_id(0)
    shard = index_ref[0]
    block = 256

    def loads():
        def rows_of(ref, unit):
            rows = pieces[0].shape[1]
            return piece_copies(
                index_ref,
                [piece.at[unit] for piece in pieces],
                lambda to, first, count: ref.at[pl.ds(pl.multiple_of(to * rows + first, 128), count), :],
                sems.at[unit],
            )

        first = [pltpu.make_async_copy(normed_hbm, normed_ref, whole_sems.at[0])] + rows_of(up_ref, 0)
        second = [pltpu.make_async_copy(cot_hbm, cot_ref, whole_sems.at[1])] + rows_of(down_ref, 1)
        return first, second

    def stores():
        cols = pl.ds(chunk * hidden_ref.shape[1], hidden_ref.shape[1])
        return (
            pltpu.make_async_copy(hidden_ref, hidden_out.at[:, cols], whole_sems.at[2]),
            pltpu.make_async_copy(pre_ref, pre_out.at[:, cols], whole_sems.at[3]),
        )

    @pl.when(step == 0)
    def _():
        first, second = loads()
        for copy in first + second:
            copy.start()
        for copy in first:
            copy.wait()

    @pl.when(step == 1)
    def _():
        for copy in loads()[1]:
            copy.wait()

    rows_each = 256
    count = normed_ref.shape[0] // rows_each

    @pl.when(step == 0)
    def _():
        bias = vec_rows(vec_ref, [(one, VEC["up_bias"][0] + chunk) for one in range(SHARDS)])
        for m in range(count):
            rows = slice(m * rows_each, (m + 1) * rows_each)
            value, slope = gelu_and_slope(dot(normed_ref[rows, :], up_ref[...]) + bias)
            value = value.astype(bf16)
            hidden_ref[rows, :] = value
            slope_ref[rows, :] = slope
        stores()[0].start()

    @pl.when(step == 1)
    def _():
        sums = jnp.zeros(bias_ref.shape, f32)
        for m in range(count):
            rows = slice(m * rows_each, (m + 1) * rows_each)
            d_pre = (dot(cot_ref[rows, :], down_ref[...], 1, 1) * slope_ref[rows, :]).astype(bf16)
            pre_ref[rows, :] = d_pre
            sums = sums + jnp.sum(d_pre.astype(f32), axis=0, keepdims=True)
        bias_ref[...] = sums
        stores()[1].start()

    @pl.when(step >= 2)
    def _():
        k = jnp.where(step < 4, 2 * (step - 2) + 1, 2 * (step - 4))
        cols = pl.ds(pl.multiple_of((shard ^ k) * block, block), block)
        left, right = normed_ref[:, cols], hidden_ref[:, cols]
        one = dot(left, pre_ref[...], 0, 0).astype(bf16)
        two = dot(right, cot_ref[...], 0, 0).astype(bf16)

        @pl.when(step < 4)
        def _():
            send_ref[0, 0] = one
            send_ref[0, 1] = two

        @pl.when(step >= 4)
        def _():
            keep_ref[0, 0] = one
            keep_ref[0, 1] = two

    @pl.when(step == 5)
    def _():
        for copy in stores():
            copy.wait()


def hidden_chunk(chunk, index, pieces, carried, normed, cot, vec, hidden_size):
    rows, width = normed.shape
    size = hidden_size // CHUNKS
    fresh = carried is None
    grads = (2, 2, width // SHARDS, size)
    outs = [
        jax.ShapeDtypeStruct((rows, hidden_size), bf16),
        jax.ShapeDtypeStruct((rows, hidden_size), bf16),
        jax.ShapeDtypeStruct(grads, bf16),
        jax.ShapeDtypeStruct(grads, bf16),
        jax.ShapeDtypeStruct((1, size), f32),
    ]
    unit = (1,) + grads[1:]
    return pl.pallas_call(
        functools.partial(hidden_body, chunk, fresh),
        grid_spec=pltpu.PrefetchScalarGridSpec(
            num_scalar_prefetch=1,
            grid=(6,),
            in_specs=[any_spec] * (8 if fresh else 10) + [whole((SHARDS * VEC_ROWS, LANES))],
            out_specs=[
                any_spec,
                any_spec,
                pl.BlockSpec(unit, lambda i, idx: (jnp.maximum(i - 4, 0), 0, 0, 0)),
                pl.BlockSpec(unit, lambda i, idx: (jnp.clip(i - 2, 0, 1), 0, 0, 0)),
                pl.BlockSpec((1, size), lambda i, idx: (0, 0)),
            ],
            scratch_shapes=[
                pltpu.VMEM((rows, width), bf16),
                pltpu.VMEM((rows, width), bf16),
                pltpu.VMEM((width, size), bf16),
                pltpu.VMEM((size, width), bf16),
                pltpu.VMEM((rows, size), bf16),
                pltpu.VMEM((rows, size), bf16),
                pltpu.VMEM((rows, size), f32),
                pltpu.SemaphoreType.DMA((2, 6)),
                pltpu.SemaphoreType.DMA((4,)),
            ],
        ),
        out_shape=outs,
        input_output_aliases={} if fresh else {7: 0, 8: 1},
        compiler_params=params(48),
        cost_estimate=cost(8 * rows * width * size, 8 * rows * width + 16 * rows * size, rows * size),
        name=f"hidden_chunk{chunk}",
    )(index, *pieces, *(carried or ()), normed, cot, vec)


def norm_back(d_normed, hat, inverse, gain):
    scaled = d_normed * gain
    return inverse * (
        scaled
        - jnp.mean(scaled, axis=-1, keepdims=True)
        - hat * jnp.mean(scaled * hat, axis=-1, keepdims=True)
    )


def column_sum(value):
    return jnp.sum(value, axis=0, keepdims=True)


def chunk_loads(index_ref, pieces, unit, target, sems):
    loads = []
    for chunk in range(CHUNKS):
        group = pieces[6 * chunk : 6 * chunk + 6]
        rows = group[0].shape[1]
        loads.append(
            piece_copies(
                index_ref,
                [piece.at[unit] for piece in group],
                lambda to, first, count, chunk=chunk: target(
                    chunk, pl.multiple_of(to * rows + first, 128), count
                ),
                sems.at[chunk],
            )
        )
    return loads


def block_back_body(index_ref, *refs, blocks):
    pieces, refs = refs[: 6 * CHUNKS], refs[6 * CHUNKS :]
    pre_ref, middle_ref, cot_ref, a_ref, b_ref, weight_ref, vec_ref = refs[:7]
    d_middle_ref, d_attended_ref, keep_ref, send_ref, sums_ref = refs[7:12]
    up_ref, d_one_ref, sems = refs[12:]
    step = pl.program_id(0)
    rows = pre_ref.shape[0]
    size = up_ref.shape[1] // CHUNKS

    def rest(d_normed):
        middle = middle_ref[...]
        cot = cot_ref[...].astype(f32)
        hat, inverse = norm_parts(middle)
        d_middle = cot + norm_back(d_normed, hat, inverse, row_of(vec_ref, "ln2_gain"))
        d_one = d_middle.astype(bf16)
        d_middle_ref[...] = d_middle
        d_one_ref[pl.ds(pl.multiple_of(step * rows, rows), rows), :] = d_one
        sums_ref[0:1, :] += column_sum(d_normed * hat)
        sums_ref[1:2, :] += column_sum(d_normed)
        sums_ref[2:3, :] += column_sum(d_one.astype(f32))
        sums_ref[3:4, :] += column_sum(cot)

    @pl.when(step == 0)
    def _():
        loads = chunk_loads(
            index_ref,
            pieces,
            0,
            lambda chunk, first, count: up_ref.at[pl.ds(first, count), chunk * size : (chunk + 1) * size],
            sems,
        )
        for group in loads:
            for copy in group:
                copy.start()
        sums_ref[...] = jnp.zeros_like(sums_ref)
        d_normed = None
        for chunk, group in enumerate(loads):
            for copy in group:
                copy.wait()
            cols = slice(chunk * size, (chunk + 1) * size)
            term = dot(pre_ref[:, cols], up_ref[:, cols], 1, 1)
            d_normed = term if d_normed is None else d_normed + term
        rest(d_normed)

    @pl.when((step > 0) & (step < blocks))
    def _():
        rest(dot(pre_ref[...], up_ref[...], 1, 1))

    for t, k in enumerate((1, 3, 0, 2)):

        @pl.when(step == blocks + t)
        def _(t=t, k=k):
            block = weight_ref.shape[0] // SHARDS
            part = keep_ref.shape[3]
            d_one = d_one_ref[...]
            d_attended_ref[...] = dot(d_one, weight_ref[t * block : (t + 1) * block, :], 1, 1).astype(bf16)
            shard = index_ref[0] ^ k
            target = send_ref if t < 2 else keep_ref
            cols = pl.ds(pl.multiple_of((shard & 1) * block, block), block)

            def put(ref):
                value = dot(ref[:, cols], d_one, 0, 0).astype(bf16)
                for unit in range(2):
                    target[0, unit] = value[:, unit * part : (unit + 1) * part]

            pl.when(shard < 2)(lambda: put(a_ref))
            pl.when(shard >= 2)(lambda: put(b_ref))


def block_back(index, pieces, d_pre, middle, cot, attended, weight, vec, rows_each=256):
    rows, width = middle.shape
    size = d_pre.shape[1]
    blocks = rows // rows_each
    quarter = width // SHARDS

    def by_rows(cols):
        return pl.BlockSpec((rows_each, cols), lambda i, idx: (jnp.minimum(i, blocks - 1), 0))

    grads = (2, 2, quarter, width // 2)
    unit = (1,) + grads[1:]
    half = whole((rows, attended[0].shape[1]))
    return pl.pallas_call(
        functools.partial(block_back_body, blocks=blocks),
        grid_spec=pltpu.PrefetchScalarGridSpec(
            num_scalar_prefetch=1,
            grid=(blocks + SHARDS,),
            in_specs=[any_spec] * (6 * CHUNKS)
            + [
                by_rows(size),
                by_rows(width),
                by_rows(width),
                half,
                half,
                whole((width, width)),
                whole((SHARDS * VEC_ROWS, LANES)),
            ],
            out_specs=[
                by_rows(width),
                pl.BlockSpec((rows, quarter), lambda i, idx: (0, jnp.maximum(i - blocks, 0))),
                pl.BlockSpec(unit, lambda i, idx: (jnp.maximum(i - blocks - 2, 0), 0, 0, 0)),
                pl.BlockSpec(unit, lambda i, idx: (jnp.clip(i - blocks, 0, 1), 0, 0, 0)),
                whole((8, width)),
            ],
            scratch_shapes=[
                pltpu.VMEM((width, size), bf16),
                pltpu.VMEM((rows, width), bf16),
                pltpu.SemaphoreType.DMA((CHUNKS, 6)),
            ],
        ),
        out_shape=[
            jax.ShapeDtypeStruct((rows, width), f32),
            jax.ShapeDtypeStruct((rows, width), bf16),
            jax.ShapeDtypeStruct(grads, bf16),
            jax.ShapeDtypeStruct(grads, bf16),
            jax.ShapeDtypeStruct((8, width), f32),
        ],
        compiler_params=params(48),
        cost_estimate=cost(2 * rows * width * (size + 2 * width), 2 * rows * size + 2 * width * size + 16 * rows * width),
        name="block_back",
    )(index, *pieces, d_pre, middle, cot, *attended, weight, vec)


def block_out_body(index_ref, *refs):
    pieces, (hidden_ref, middle_ref, vec_ref, out_ref, down_ref, sems) = refs[: 6 * CHUNKS], refs[6 * CHUNKS :]
    step = pl.program_id(0)
    size = down_ref.shape[0] // CHUNKS

    def rest(value):
        out_ref[...] = (middle_ref[...] + row_of(vec_ref, "down_bias") + value).astype(bf16)

    @pl.when(step == 0)
    def _():
        loads = chunk_loads(
            index_ref,
            pieces,
            1,
            lambda chunk, first, count: down_ref.at[pl.ds(chunk * size + first, count), :],
            sems,
        )
        for group in loads:
            for copy in group:
                copy.start()
        total = None
        for chunk, group in enumerate(loads):
            for copy in group:
                copy.wait()
            cols = slice(chunk * size, (chunk + 1) * size)
            term = dot(hidden_ref[:, cols], down_ref[cols, :])
            total = term if total is None else total + term
        rest(total)

    @pl.when(step > 0)
    def _():
        rest(dot(hidden_ref[...], down_ref[...]))


def block_output(index, pieces, hidden, middle, vec, rows_each=256):
    rows, width = middle.shape
    size = hidden.shape[1]

    def by_rows(cols):
        return pl.BlockSpec((rows_each, cols), lambda i, idx: (i, 0))

    return pl.pallas_call(
        block_out_body,
        grid_spec=pltpu.PrefetchScalarGridSpec(
            num_scalar_prefetch=1,
            grid=(rows // rows_each,),
            in_specs=[any_spec] * (6 * CHUNKS) + [by_rows(size), by_rows(width), whole((SHARDS * VEC_ROWS, LANES))],
            out_specs=by_rows(width),
            scratch_shapes=[pltpu.VMEM((size, width), bf16), pltpu.SemaphoreType.DMA((CHUNKS, 6))],
        ),
        out_shape=jax.ShapeDtypeStruct((rows, width), bf16),
        compiler_params=params(48),
        cost_estimate=cost(2 * rows * width * size, 2 * rows * size + 2 * width * size + 6 * rows * width),
        name="block_output",
    )(index, *pieces, hidden, middle, vec)


def input_grad_body(index_ref, *refs, blocks):
    parts, pieces = refs[:6], (refs[6:10], refs[10:16])
    tokens_ref, d_middle_ref, vec_ref, sums_ref, bqv_a_ref, bqv_b_ref = refs[16:22]
    bias_refs = refs[22 : 22 + CHUNKS]
    out_ref, grads_ref, gain_ref, shift_ref, *weights, sems = refs[22 + CHUNKS :]
    step = pl.program_id(0)

    @pl.when(step == 0)
    def _():
        copies = []
        for half in range(2):
            rows = pieces[half][0].shape[0]
            copies += piece_copies(
                index_ref,
                pieces[half],
                lambda to, first, count, half=half, rows=rows: weights[half].at[
                    pl.ds(pl.multiple_of(to * rows + first, 128), count), :
                ],
                sems.at[half],
            )
        for copy in copies:
            copy.start()
        for copy in copies:
            copy.wait()
        gain_ref[...] = jnp.zeros_like(gain_ref)
        shift_ref[...] = jnp.zeros_like(shift_ref)

    d_normed = None
    for half in range(2):
        for i in range(3):
            ref = parts[3 * half + i]
            part = ref.shape[1]
            term = dot(ref[...], weights[half][:, i * part : (i + 1) * part], 1, 1)
            d_normed = term if d_normed is None else d_normed + term
    hat, inverse = norm_parts(tokens_ref[...].astype(f32))
    out_ref[...] = d_middle_ref[...] + norm_back(d_normed, hat, inverse, row_of(vec_ref, "ln1_gain"))
    gain_ref[...] += column_sum(d_normed * hat)
    shift_ref[...] += column_sum(d_normed)

    @pl.when(step == blocks - 1)
    def _():
        grads_ref[...] = jnp.zeros_like(grads_ref)

        def put(name, shard, value, offset=0):
            first = shard * VEC_ROWS + VEC[name][0] + offset
            for i in range(value.shape[1] // LANES):
                grads_ref[first + i : first + i + 1, :] = value[:, i * LANES : (i + 1) * LANES]

        for shard in range(SHARDS):
            cols = slice(shard * 256, (shard + 1) * 256)
            put("ln1_gain", shard, gain_ref[:, cols])
            put("ln1_bias", shard, shift_ref[:, cols])
            put("ln2_gain", shard, sums_ref[0:1, cols])
            put("ln2_bias", shard, sums_ref[1:2, cols])
            put("out_bias", shard, sums_ref[2:3, cols])
            put("down_bias", shard, sums_ref[3:4, cols])
            source = bqv_a_ref if shard % 2 == 0 else bqv_b_ref
            put("b_qv", shard, source[shard // 2 : shard // 2 + 1, :])
            for chunk in range(CHUNKS):
                size = bias_refs[chunk].shape[1] // SHARDS
                put("up_bias", shard, bias_refs[chunk][:, shard * size : (shard + 1) * size], chunk)


def input_gradient(index, parts, weights, tokens, d_middle, vec, sums, bqv, biases, rows_each=256):
    rows, width = tokens.shape
    part = parts[0].shape[1]
    blocks = rows // rows_each

    def by_rows(cols):
        return pl.BlockSpec((rows_each, cols), lambda i, idx: (i, 0))

    return pl.pallas_call(
        functools.partial(input_grad_body, blocks=blocks),
        grid_spec=pltpu.PrefetchScalarGridSpec(
            num_scalar_prefetch=1,
            grid=(blocks,),
            in_specs=[by_rows(part)] * 6
            + [any_spec] * 10
            + [by_rows(width), by_rows(width), whole((SHARDS * VEC_ROWS, LANES)), whole((8, width))]
            + [whole((2, part))] * 2
            + [whole(bias.shape) for bias in biases],
            out_specs=[by_rows(width), whole((SHARDS * VEC_ROWS, LANES))],
            scratch_shapes=[pltpu.VMEM((1, width), f32)] * 2
            + [pltpu.VMEM((width, 3 * part), bf16)] * 2
            + [pltpu.SemaphoreType.DMA((2, 6))],
        ),
        out_shape=[
            jax.ShapeDtypeStruct((rows, width), f32),
            jax.ShapeDtypeStruct((SHARDS * VEC_ROWS, LANES), f32),
        ],
        compiler_params=params(40),
        cost_estimate=cost(12 * rows * width * part, 10 * rows * width + 12 * rows * part + 12 * width * part),
        name="input_gradient",
    )(index, *parts, *weights, tokens, d_middle, vec, sums, *bqv, *biases)


def place_body(index_ref, pair_ref, other_ref, *refs, plan, fresh):
    outs = len(refs) - 2 if fresh else (len(refs) - 2) // 2
    out_refs = refs[-2 - outs : -2]
    scratch, sems = refs[-2:]
    low, mid = index_ref[1], index_ref[2]
    rows = pair_ref.shape[2]
    for a, ref in enumerate((pair_ref, other_ref)):
        for b in range(2):
            first = pl.multiple_of((low ^ a) * (2 * rows) + (mid ^ b) * rows, rows)
            for u in range(pair_ref.shape[1]):
                scratch[u, pl.ds(first, rows), :] = ref[b, u].astype(f32)
    copies = []
    for i, (unit, cols, width, out, row, col) in enumerate(plan):
        copies.append(
            pltpu.make_async_copy(
                scratch.at[unit, :, cols : cols + width],
                out_refs[out].at[row : row + 4 * rows, col : col + width],
                sems.at[i],
            )
        )
    for copy in copies:
        copy.start()
    for copy in copies:
        copy.wait()


def place(index, pieces, plan, shapes, carried, name):
    pair, other = pieces
    _, units, rows, width = pair.shape
    fresh = carried is None
    count = len(shapes)
    return pl.pallas_call(
        functools.partial(place_body, plan=plan, fresh=fresh),
        grid_spec=pltpu.PrefetchScalarGridSpec(
            num_scalar_prefetch=1,
            grid=(1,),
            in_specs=[whole(pair.shape), whole(other.shape)] + ([] if fresh else [any_spec] * count),
            out_specs=[any_spec] * count,
            scratch_shapes=[pltpu.VMEM((units, 4 * rows, width), f32), pltpu.SemaphoreType.DMA((len(plan),))],
        ),
        out_shape=[jax.ShapeDtypeStruct(shape, f32) for shape in shapes],
        input_output_aliases={} if fresh else {3 + i: i for i in range(count)},
        compiler_params=params(16),
        cost_estimate=cost(units * 4 * rows * width, units * 4 * rows * width * 6),
        name=name,
    )(index, pair, other, *(carried or ()))


def body(
    mesh,
    tokens,
    piece_start,
    ln1_gain,
    ln1_bias,
    query_key_value_weight,
    b_qv,
    attention_out_weight,
    attention_out_bias,
    ln2_gain,
    ln2_bias,
    up_weight,
    up_bias,
    down_weight,
    down_bias,
    cotangent,
):
    count, seq_len, width = tokens.shape
    rows = count * seq_len
    hidden_size = up_weight.shape[1]
    tokens = tokens.reshape(rows, width)
    cot = cotangent.reshape(rows, width)
    moves = Moves(mesh, piece_start)
    half = width // 2
    size = hidden_size // CHUNKS
    block = size // SHARDS

    def as_rows(value):
        return value.reshape(-1, LANES)

    def joined_cols(which):
        return jnp.concatenate(
            [
                query_key_value_weight[:, i * width + which * half : i * width + (which + 1) * half]
                for i in range(3)
            ],
            axis=1,
        )

    own_a = joined_cols(0)
    own_vec = jnp.concatenate(
        [
            as_rows(after(value, own_a))
            for value in (ln1_gain, ln1_bias, b_qv, attention_out_bias, ln2_gain, ln2_bias, up_bias, down_bias)
        ]
        + [jnp.zeros((VEC_ROWS - 12, LANES), bf16)]
    )

    def hidden_own(chunk):
        up = jnp.concatenate(
            [
                up_weight[:, s * size + chunk * block : s * size + (chunk + 1) * block]
                for s in range(SHARDS)
            ],
            axis=1,
        )
        return jnp.stack([up, down_weight[chunk * block : (chunk + 1) * block, :]])

    far_a = moves.across(own_a)
    near_a = moves.core(own_a)
    far_vec = moves.across(own_vec)
    near_vec = moves.core(own_vec)
    own_b = joined_cols(1)
    half_b = moves.half(own_b)
    hidden_owns = [hidden_own(chunk) for chunk in range(CHUNKS)]
    hidden_halves = [moves.half(own) for own in hidden_owns]
    out_half = moves.half(attention_out_weight)
    far_near_vec = moves.core(far_vec)
    moves.wait(half_b, out_half, *hidden_halves)
    normed, vec = first_norm(moves.index, tokens, (own_vec, near_vec, far_vec, far_near_vec))
    moves.ran(vec)

    joined, attended, totals = [None] * 2, [None] * 2, [None] * 2
    hidden_far, hidden_near, hidden_other = [None] * CHUNKS, [None] * CHUNKS, [None] * CHUNKS
    hidden_pieces = [None] * CHUNKS

    def fetch(chunk, kernels):
        hidden_far[chunk] = moves.across(hidden_halves[chunk])
        hidden_near[chunk] = moves.core(hidden_owns[chunk])
        moves.by(kernels, hidden_far[chunk], hidden_near[chunk])

    def relay(chunk, kernels):
        hidden_other[chunk] = moves.rep(hidden_far[chunk], 1)
        moves.by(kernels, hidden_other[chunk])

    far_b = moves.across(half_b)
    near_b = moves.core(own_b)
    moves.by(1, far_b, near_b)
    joined_pieces = [(own_a, near_a, far_a, moves.core(far_a))]
    joined[0] = joined_product(0, moves.index, joined_pieces[0], normed, vec)
    moves.ran(joined[0])
    other_b = moves.rep(far_b, 1)
    moves.by(1, other_b)
    fetch(0, 1)
    attended[0], totals[0] = attend_forward(0, moves.index, joined[0])
    moves.ran(totals[0])
    relay(0, 2)
    out_far = moves.across(out_half)
    out_near = moves.core(attention_out_weight)
    moves.by(1, out_far, out_near)
    joined_pieces.append((own_b, near_b, far_b, other_b, moves.core(far_b), moves.core(other_b)))
    joined[1] = joined_product(1, moves.index, joined_pieces[1], normed, vec)
    moves.ran(joined[1])
    out_other = moves.rep(out_far, 1)
    moves.by(1, out_other)
    fetch(1, 1)
    attended[1], totals[1] = attend_forward(1, moves.index, joined[1])
    moves.ran(totals[1])
    relay(1, 2)
    fetch(2, 2)
    middle, normed_two, out_weight = middle_product(
        moves.index,
        (attention_out_weight, out_near, out_far, out_other, moves.core(out_far), moves.core(out_other)),
        attended,
        tokens,
        vec,
    )
    moves.ran(normed_two)

    carried = None
    shard_sums, up_biases = [], []

    def hidden_step(chunk):
        nonlocal carried
        far, other = hidden_far[chunk], hidden_other[chunk]
        hidden_pieces[chunk] = (
            hidden_owns[chunk],
            hidden_near[chunk],
            far,
            other,
            moves.core(far),
            moves.core(other),
        )
        *carried, keep, send, bias = hidden_chunk(
            chunk, moves.index, hidden_pieces[chunk], carried, normed_two, cot, vec, hidden_size
        )
        moves.ran(bias)
        up_biases.append(bias)
        shard_sums.append(ShardSum(moves, keep, send))

    fetch(3, 1)
    hidden_step(0)
    relay(2, 1)
    hidden_step(1)
    relay(3, 1)
    shard_sums[0].cross(1)
    hidden_step(2)
    shard_sums[1].cross(1)
    hidden_step(3)
    shard_sums[2].cross(1)
    first_sum = RepSum(moves, shard_sums[:2])
    all_pieces = [piece for pieces in hidden_pieces for piece in pieces]
    hidden, d_pre = carried
    d_middle, d_attended, keep, send, sums = block_back(
        moves.index, all_pieces, d_pre, middle, cot, attended, out_weight, vec
    )
    moves.ran(sums)
    parts, bqv = [], []

    def backward(which):
        *grads, keep, send, bias = attend_backward(
            which, moves.index, joined[which], attended[which], d_attended, totals[which], normed
        )
        parts.extend(grads)
        bqv.append(bias)
        moves.ran(bias)
        return ShardSum(moves, keep, send)

    shard_sums[3].cross(1)
    out_sum = ShardSum(moves, keep, send)
    first_sum.split()
    second_sum = RepSum(moves, shard_sums[2:3])
    a_sum = backward(0)
    out_sum.cross(1)
    first_sum.add()
    second_sum.split()
    third_sum = RepSum(moves, shard_sums[3:4])
    b_sum = backward(1)
    a_sum.cross(1)
    first_sum.spread()
    second_sum.add()
    third_sum.split()
    input_grad, vec_grads = input_gradient(
        moves.index, parts, joined_pieces[0] + joined_pieces[1], tokens, d_middle, vec, sums, bqv, up_biases
    )
    moves.ran(vec_grads)
    b_sum.cross(1)
    fourth_sum = RepSum(moves, [out_sum, a_sum])
    first_sum.finish()
    second_sum.spread()
    third_sum.add()
    block_out = block_output(moves.index, all_pieces, hidden, middle, vec)
    moves.ran(block_out)

    def place_hidden(chunks, pieces, grads, name):
        plan = []
        for i, chunk in enumerate(chunks):
            plan += [(2 * i, s * block, block, 0, 0, s * size + chunk * block) for s in range(SHARDS)]
            plan += [(2 * i + 1, 0, width, 1, chunk * block, 0)]
        shapes = [(width // SHARDS, hidden_size), (size, width)]
        grads = place(moves.index, pieces, plan, shapes, grads, name)
        moves.ran(grads[0])
        return grads

    last_sum = RepSum(moves, [b_sum])
    fourth_sum.split()
    second_sum.finish()
    third_sum.spread()
    vec_sum = VecSum(moves, vec_grads)
    grads = place_hidden((0, 1), first_sum.pieces(), None, "place_hidden_first")
    last_sum.split()
    fourth_sum.add()
    third_sum.finish()
    vec_sum.step()
    grads = place_hidden((2,), second_sum.pieces(), grads, "place_hidden_second")
    last_sum.add()
    fourth_sum.spread()
    vec_sum.step()
    grad_up, grad_down = place_hidden((3,), third_sum.pieces(), grads, "place_hidden_third")
    fourth_sum.finish()
    last_sum.spread()
    vec_sum.step()
    last_sum.finish()
    vec_sum = vec_sum.rest()
    third = width // SHARDS
    plan = [(i, 0, half, 0, 0, i * half) for i in range(2)]
    plan += [(2 + i, 0, half, 1, 0, i * width) for i in range(3)]
    shapes = [(third, width), (third, 3 * width)]
    grad_out, grad_joined = place(moves.index, fourth_sum.pieces(), plan, shapes, None, "place_fourth")
    plan = [(i, 0, half, 0, 0, i * width + half) for i in range(3)]
    (grad_joined,) = place(moves.index, last_sum.pieces(), plan, shapes[1:], (grad_joined,), "place_last")

    def vec_part(name):
        first, count = VEC[name]
        return vec_sum[first : first + count].reshape(count * LANES)

    return (
        block_out.reshape(count, seq_len, width),
        input_grad.reshape(count, seq_len, width),
        vec_part("ln1_gain"),
        vec_part("ln1_bias"),
        grad_joined,
        vec_part("b_qv"),
        grad_out,
        vec_part("out_bias"),
        vec_part("ln2_gain"),
        vec_part("ln2_bias"),
        grad_up,
        vec_part("up_bias"),
        grad_down,
        vec_part("down_bias"),
    )


def solution(mesh):
    batch = P(("shard", "rep"), None, None)
    vector, matrix = P("shard"), P("shard", None)
    in_specs = (
        batch,
        P(("shard", "rep")),
        vector,
        vector,
        matrix,
        vector,
        matrix,
        vector,
        vector,
        vector,
        matrix,
        vector,
        matrix,
        vector,
        batch,
    )
    out_specs = (
        batch,
        batch,
        vector,
        vector,
        matrix,
        vector,
        matrix,
        vector,
        vector,
        vector,
        matrix,
        vector,
        matrix,
        vector,
    )
    return jax.shard_map(
        functools.partial(body, mesh), mesh=mesh, in_specs=in_specs, out_specs=out_specs, check_vma=False
    )
```

```python
import functools

import jax
import jax.numpy as jnp
from jax import lax
from jax.experimental import pallas as pl
from jax.experimental.pallas import tpu as pltpu
from jax.sharding import PartitionSpec as P

HEADS = 16
PIECE = 256
HEAD_DIM = 64
PAIR = 2 * HEAD_DIM
SHARDS = 4
CHUNKS = 4
EPS = 1e-05
HIDDEN_PENALTY = 1e33

bf16 = jnp.bfloat16
f32 = jnp.float32

VEC = {
    "ln1_gain": (0, 1),
    "ln1_bias": (1, 1),
    "b_qv": (2, 2),
    "out_bias": (4, 1),
    "ln2_gain": (5, 1),
    "ln2_bias": (6, 1),
    "up_bias": (7, 4),
    "down_bias": (11, 1),
}
VEC_ROWS = 16
LANES = 256

any_spec = pl.BlockSpec(memory_space=pltpu.MemorySpace.HBM)


def dot(left, right, left_dim=1, right_dim=0):
    return lax.dot_general(
        left, right, (((left_dim,), (right_dim,)), ((), ())), preferred_element_type=f32
    )


def params(mib):
    return pltpu.CompilerParams(vmem_limit_bytes=int(mib * 2**20))


def cost(flops, moved, transcendentals=0, scale=8):
    return pl.CostEstimate(
        flops=int(scale * flops), bytes_accessed=int(scale * moved), transcendentals=int(scale * transcendentals)
    )


def vec_rows(vec_ref, rows):
    firsts = [shard * VEC_ROWS + row for shard, row in rows]
    return jnp.concatenate([vec_ref[first : first + 1, :] for first in firsts], axis=1)


def row_of(vec_ref, name):
    return vec_rows(vec_ref, [(shard, VEC[name][0]) for shard in range(SHARDS)])


def whole(shape):
    return pl.BlockSpec(shape, lambda *_: (0,) * len(shape))


def flip(value, axis, size, bit):
    return lax.ppermute(value, axis, [(i, i ^ bit) for i in range(size)])


class Moves:
    def __init__(self, mesh, starts):
        self.reps = mesh.shape["rep"]
        assert mesh.shape["shard"] == SHARDS and self.reps % 4 == 0
        self.shard = lax.axis_index("shard")
        rep = lax.axis_index("rep")
        self.low = rep & 1
        self.mid = (rep >> 1) & 1
        self.index = jnp.concatenate(
            [jnp.stack([self.shard, self.low, self.mid]).astype(jnp.int32), starts]
        )
        self.last = ()
        self.count = 0
        self.due = []

    def wait(self, *values):
        self.index = after(self.index, *values, *self.last)

    def by(self, kernels, *values):
        self.due.append((self.count + kernels, values))

    def ran(self, value):
        self.last = (value,)
        self.count += 1
        ready = [value for when, values in self.due if when <= self.count for value in values]
        self.due = [entry for entry in self.due if entry[0] > self.count]
        self.wait(*ready)
        return value

    def move(self, value, axis, size, bit):
        return flip(after(value, *self.last), axis, size, bit)

    def core(self, value):
        return self.move(value, "shard", SHARDS, 1)

    def across(self, value):
        return self.move(value, "shard", SHARDS, 2)

    def rep(self, value, bit):
        return self.move(value, "rep", self.reps, bit)

    def half(self, own):
        rows = own.shape[-2] // 2
        return lax.dynamic_slice_in_dim(own, self.low * rows, rows, own.ndim - 2)

    def pick(self, value, which, size):
        return lax.dynamic_slice_in_dim(value, which * size, size, 1)


def after(value, *earlier):
    return lax.optimization_barrier((value, *earlier))[0] if earlier else value


class ShardSum:
    def __init__(self, moves, keep, send, kernels=1):
        self.moves, self.keep = moves, keep
        self.got = moves.core(send)
        moves.by(kernels, self.got)

    def cross(self, kernels):
        self.got = after(self.got, *self.moves.last)
        out = self.keep[1] + self.got[1]
        self.mine = self.keep[0] + self.got[0]
        self.moves.wait(out, self.mine)
        self.got = self.moves.across(out)
        self.moves.by(kernels, self.got)

    def halves(self):
        moves, mine = self.moves, self.mine
        got = after(self.got, *moves.last)
        size = mine.shape[1] // 2
        return [
            moves.pick(mine, which, size) + moves.pick(got, which, size)
            for which in (moves.low, 1 - moves.low)
        ]


class RepSum:
    def __init__(self, moves, sums, kernels=1):
        self.moves = moves
        halves = [s.halves() for s in sums]
        self.mine = jnp.concatenate([h[0] for h in halves])
        self.bit = 2
        self.send(jnp.concatenate([h[1] for h in halves]), 1, kernels)

    def send(self, out, bit, kernels):
        self.moves.wait(out, self.mine)
        self.got = self.moves.rep(out, bit)
        self.moves.by(kernels, self.got)

    def split(self, kernels=1):
        moves = self.moves
        got = after(self.got, *moves.last)
        size = self.mine.shape[1] // 2
        out, self.mine = [
            moves.pick(self.mine, which, size) + moves.pick(got, which, size)
            for which in (1 - moves.mid, moves.mid)
        ]
        self.send(out, 2, kernels)

    def add(self, kernels=1):
        self.mine = self.mine + after(self.got, *self.moves.last)
        self.bit *= 2
        self.got = None
        if self.bit < self.moves.reps:
            self.send(self.mine, self.bit, kernels)

    def spread(self, kernels=1):
        while self.got is not None:
            self.add()
        self.send(self.mine, 2, kernels)

    def finish(self, kernels=1):
        self.pair = jnp.stack([self.mine, after(self.got, *self.moves.last)])
        self.send(self.pair, 1, kernels)

    def pieces(self):
        self.moves.wait(self.got)
        return (self.pair, self.got)


class VecSum:
    def __init__(self, moves, value):
        self.moves, self.value = moves, value
        self.plan = [moves.core, moves.across]
        bit = 1
        while bit < moves.reps:
            self.plan.append(functools.partial(moves.rep, bit=bit))
            bit *= 2
        self.at = 0
        self.send()

    def send(self):
        self.got = self.plan[self.at](self.value)
        self.moves.by(1, self.got)
        self.at += 1

    def step(self):
        moves = self.moves
        self.value = self.value + after(self.got, *moves.last)
        if self.at == 2:
            self.value = lax.dynamic_slice_in_dim(self.value, moves.shard * VEC_ROWS, VEC_ROWS, 0)
        moves.wait(self.value)
        if self.at < len(self.plan):
            self.send()

    def rest(self):
        while self.at < len(self.plan):
            self.step()
        self.step()
        return self.value


def piece_copies(index_ref, pieces, target, sems):
    shard, low = index_ref[0], index_ref[1]
    rows = pieces[0].shape[-2]
    if len(pieces) == 4:
        plan = [(piece, shard ^ k, 0, rows) for k, piece in enumerate(pieces)]
    else:
        own, near, far, far_other, far_near, far_other_near = pieces
        half = rows // 2
        plan = (
            (own, shard, 0, rows),
            (near, shard ^ 1, 0, rows),
            (far, shard ^ 2, low * half, half),
            (far_other, shard ^ 2, (1 - low) * half, half),
            (far_near, shard ^ 3, low * half, half),
            (far_other_near, shard ^ 3, (1 - low) * half, half),
        )
    return [
        pltpu.make_async_copy(source, target(to, first, count), sems.at[i])
        for i, (source, to, first, count) in enumerate(plan)
    ]


def norm_parts(value):
    center = value - jnp.mean(value, axis=-1, keepdims=True)
    inverse = lax.rsqrt(jnp.mean(center * center, axis=-1, keepdims=True) + EPS)
    return center * inverse, inverse


def first_norm_body(index_ref, tokens_ref, own_ref, near_ref, far_ref, far_near_ref, normed_ref, vec_ref):
    shard = index_ref[0]

    @pl.when(pl.program_id(0) == 0)
    def _():
        for k, ref in enumerate((own_ref, near_ref, far_ref, far_near_ref)):
            vec_ref[pl.ds(pl.multiple_of((shard ^ k) * VEC_ROWS, VEC_ROWS), VEC_ROWS), :] = ref[...].astype(f32)

    hat, _ = norm_parts(tokens_ref[...].astype(f32))
    normed_ref[...] = (hat * row_of(vec_ref, "ln1_gain") + row_of(vec_ref, "ln1_bias")).astype(bf16)


def first_norm(index, tokens, vec_pieces, block=256):
    rows, width = tokens.shape
    row = pl.BlockSpec((block, width), lambda i, idx: (i, 0))
    return pl.pallas_call(
        first_norm_body,
        grid_spec=pltpu.PrefetchScalarGridSpec(
            num_scalar_prefetch=1,
            grid=(rows // block,),
            in_specs=[row] + [whole((VEC_ROWS, LANES))] * 4,
            out_specs=[row, whole((SHARDS * VEC_ROWS, LANES))],
        ),
        out_shape=[
            jax.ShapeDtypeStruct((rows, width), bf16),
            jax.ShapeDtypeStruct((SHARDS * VEC_ROWS, LANES), f32),
        ],
        compiler_params=params(16),
        cost_estimate=cost(20 * rows * width, 4 * rows * width),
        name="first_norm",
    )(index, tokens, *vec_pieces)


def joined_body(half, index_ref, *refs):
    pieces, (normed_ref, vec_ref, out_ref, weight_ref, sems) = refs[:-5], refs[-5:]

    @pl.when(pl.program_id(0) == 0)
    def _():
        rows = pieces[0].shape[0]
        copies = piece_copies(
            index_ref,
            pieces,
            lambda to, first, count: weight_ref.at[
                pl.ds(pl.multiple_of(to * rows + first, 128), count), :
            ],
            sems,
        )
        for copy in copies:
            copy.start()
        for copy in copies:
            copy.wait()

    part = weight_ref.shape[1] // 3
    first = VEC["b_qv"][0]
    normed = normed_ref[...]
    for i in range(3):
        cols = slice(i * part, (i + 1) * part)
        value = dot(normed, weight_ref[:, cols])
        if i != 1:
            shard = half if i == 0 else 2 + half
            value = value + vec_rows(vec_ref, [(shard, first), (shard, first + 1)])
        out_ref[:, cols] = value.astype(bf16)


def joined_product(half, index, pieces, normed, vec, block=256):
    rows, width = normed.shape
    cols = pieces[0].shape[1]
    return pl.pallas_call(
        functools.partial(joined_body, half),
        grid_spec=pltpu.PrefetchScalarGridSpec(
            num_scalar_prefetch=1,
            grid=(rows // block,),
            in_specs=[any_spec] * len(pieces)
            + [pl.BlockSpec((block, width), lambda i, idx: (i, 0)), whole((SHARDS * VEC_ROWS, LANES))],
            out_specs=pl.BlockSpec((block, cols), lambda i, idx: (i, 0)),
            scratch_shapes=[pltpu.VMEM((width, cols), bf16), pltpu.SemaphoreType.DMA((6,))],
        ),
        out_shape=jax.ShapeDtypeStruct((rows, cols), bf16),
        compiler_params=params(24),
        cost_estimate=cost(2 * rows * width * cols, 2 * (rows * width + rows * cols + 2 * width * cols)),
        name="joined_product",
    )(index, *pieces, normed, vec)


def penalty(start, seq_len):
    key = lax.broadcasted_iota(jnp.int32, (seq_len, seq_len), 0)
    query = lax.broadcasted_iota(jnp.int32, (seq_len, seq_len), 1)
    key_in = (key >= start) & (key < start + PIECE)
    query_in = (query >= start) & (query < start + PIECE)
    seen = (key <= query) | (key_in & query_in)
    return jnp.where(seen, jnp.abs(key - query).astype(f32), HIDDEN_PENALTY)


def slope_of(head):
    return jnp.exp2((jnp.full((1, 1), head, jnp.int32).astype(f32) + 1.0) * (-8.0 / HEADS))


def attend_forward_body(first_head, start_ref, q_ref, k_ref, v_ref, out_ref, total_ref, pen_ref):
    pair = pl.program_id(1)
    seq_len = q_ref.shape[0]

    @pl.when(pair == 0)
    def _():
        pen_ref[...] = penalty(start_ref[3 + pl.program_id(0)], seq_len)

    queries, keys = q_ref[...], k_ref[...]
    values_t = v_ref[...].T
    lane = lax.broadcasted_iota(jnp.int32, (seq_len, PAIR), 1)
    outs = []
    for e in range(2):
        chosen = (lane < HEAD_DIM) if e == 0 else (lane >= HEAD_DIM)
        key_e = jnp.where(chosen, keys * (HEAD_DIM**-0.5), 0).astype(bf16)
        scores = dot(key_e, queries, 1, 1) - slope_of(first_head + 2 * pair + e) * pen_ref[...]
        top = jnp.max(scores, axis=0, keepdims=True)
        weight = jnp.exp(scores - top)
        total = jnp.sum(weight, axis=0, keepdims=True)
        out_t = dot(values_t[e * HEAD_DIM : (e + 1) * HEAD_DIM, :], weight.astype(bf16))
        outs.append(out_t * (1.0 / total))
        total_ref[0, 0, e : e + 1, :] = top + jnp.log(total)
    out_ref[...] = jnp.concatenate(outs, axis=0).T.astype(bf16)


def attend_forward(half, index, joined):
    count = index.shape[0] - 3
    seq_len, width = joined.shape[0] // count, joined.shape[1] // 3
    pairs = width // PAIR

    def cols(first):
        return pl.BlockSpec((seq_len, PAIR), lambda s, h, st: (s, first + h))

    return pl.pallas_call(
        functools.partial(attend_forward_body, half * 2 * pairs),
        grid_spec=pltpu.PrefetchScalarGridSpec(
            num_scalar_prefetch=1,
            grid=(count, pairs),
            in_specs=[cols(0), cols(pairs), cols(2 * pairs)],
            out_specs=[cols(0), pl.BlockSpec((1, 1, 2, seq_len), lambda s, h, st: (s, h, 0, 0))],
            scratch_shapes=[pltpu.VMEM((seq_len, seq_len), f32)],
        ),
        out_shape=[
            jax.ShapeDtypeStruct((count * seq_len, width), bf16),
            jax.ShapeDtypeStruct((count, pairs, 2, seq_len), f32),
        ],
        compiler_params=params(24),
        cost_estimate=cost(
            24 * count * seq_len * seq_len * width, 8 * count * seq_len * width, count * seq_len * seq_len * 2 * pairs
        ),
        name="attend_forward",
    )(index, joined, joined, joined)


def attend_backward_body(
    first_head,
    steps,
    index_ref,
    q_ref,
    k_ref,
    v_ref,
    out_ref,
    dout_ref,
    total_ref,
    normed_ref,
    dq_ref,
    dk_ref,
    dv_ref,
    keep_ref,
    send_ref,
    sums_ref,
    pen_ref,
):
    step = pl.program_id(0)
    seq_len = q_ref.shape[0]
    scale = HEAD_DIM**-0.5
    pairs = dq_ref.shape[1] // PAIR
    seq, pair = step // pairs, step % pairs

    @pl.when((step < steps) & (pair == 0))
    def _():
        pen_ref[...] = penalty(index_ref[3 + seq], seq_len)

    @pl.when(step < steps)
    def _():
        queries, keys, values, d_out = q_ref[...], k_ref[...], v_ref[...], dout_ref[...]
        lane = lax.broadcasted_iota(jnp.int32, (seq_len, PAIR), 1)
        keys_t = keys.T
        both_t = (d_out.astype(f32) * out_ref[...].astype(f32)).T
        d_q, d_k, d_v = [], [], []
        for e in range(2):
            chosen = (lane < HEAD_DIM) if e == 0 else (lane >= HEAD_DIM)
            part = slice(e * HEAD_DIM, (e + 1) * HEAD_DIM)
            key_e = jnp.where(chosen, keys * scale, 0).astype(bf16)
            value_e = jnp.where(chosen, values, 0)
            inner = jnp.sum(both_t[part, :], axis=0, keepdims=True)
            scores = dot(key_e, queries, 1, 1) - slope_of(first_head + 2 * pair + e) * pen_ref[...]
            probs = jnp.exp(scores - total_ref[0, 0, e : e + 1, :])
            d_scores = (probs * (dot(value_e, d_out, 1, 1) - inner)).astype(bf16)
            d_v.append(dot(probs.astype(bf16), d_out))
            d_k.append(dot(d_scores, queries))
            d_q.append(dot(keys_t[part, :], d_scores))
        rows = pl.ds(pl.multiple_of(seq * seq_len, seq_len), seq_len)
        cols = pl.ds(pl.multiple_of(pair * PAIR, PAIR), PAIR)
        dq_ref[rows, cols] = (jnp.concatenate(d_q, axis=0) * scale).T.astype(bf16)
        dk_ref[rows, cols] = (jnp.where(lane < HEAD_DIM, d_k[0], d_k[1]) * scale).astype(bf16)
        dv_ref[rows, cols] = jnp.where(lane < HEAD_DIM, d_v[0], d_v[1]).astype(bf16)

    @pl.when(step == steps)
    def _():
        sums_ref[0:1, :] = column_sum(dq_ref[...].astype(f32))
        sums_ref[1:2, :] = column_sum(dv_ref[...].astype(f32))

    @pl.when(step >= steps)
    def _():
        block = keep_ref.shape[2]
        t = step - steps
        k = jnp.where(t < 2, 2 * t + 1, 2 * t - 4)
        left = normed_ref[:, pl.ds(pl.multiple_of((index_ref[0] ^ k) * block, block), block)]
        for i, ref in enumerate((dq_ref, dk_ref, dv_ref)):
            value = dot(left, ref[...], 0, 0).astype(bf16)

            @pl.when(t < 2)
            def _(i=i, value=value):
                send_ref[0, i] = value

            @pl.when(t >= 2)
            def _(i=i, value=value):
                keep_ref[0, i] = value


def attend_backward(half, index, joined, attended, d_attended, totals, normed):
    count = index.shape[0] - 3
    rows, width = joined.shape[0], joined.shape[1] // 3
    seq_len = rows // count
    pairs = width // PAIR
    steps = count * pairs
    model = normed.shape[1]

    def cols(first):
        def where(i, idx):
            at = jnp.minimum(i, steps - 1)
            return (at // pairs, first + at % pairs)

        return pl.BlockSpec((seq_len, PAIR), where)

    def totals_at(i, idx):
        at = jnp.minimum(i, steps - 1)
        return (at // pairs, at % pairs, 0, 0)

    grads = (2, 3, model // SHARDS, width)
    unit = (1,) + grads[1:]
    return pl.pallas_call(
        functools.partial(attend_backward_body, half * 2 * pairs, steps),
        grid_spec=pltpu.PrefetchScalarGridSpec(
            num_scalar_prefetch=1,
            grid=(steps + SHARDS,),
            in_specs=[
                cols(0),
                cols(pairs),
                cols(2 * pairs),
                cols(0),
                cols(half * pairs),
                pl.BlockSpec((1, 1, 2, seq_len), totals_at),
                whole((rows, model)),
            ],
            out_specs=[whole((rows, width))] * 3
            + [
                pl.BlockSpec(unit, lambda i, idx: (jnp.clip(i - steps - 2, 0, 1), 0, 0, 0)),
                pl.BlockSpec(unit, lambda i, idx: (jnp.clip(i - steps, 0, 1), 0, 0, 0)),
                whole((2, width)),
            ],
            scratch_shapes=[pltpu.VMEM((seq_len, seq_len), f32)],
        ),
        out_shape=[jax.ShapeDtypeStruct((rows, width), bf16)] * 3
        + [
            jax.ShapeDtypeStruct(grads, bf16),
            jax.ShapeDtypeStruct(grads, bf16),
            jax.ShapeDtypeStruct((2, width), f32),
        ],
        compiler_params=params(40),
        cost_estimate=cost(
            36 * rows * seq_len * width + 6 * rows * model * width, 16 * rows * width, rows * seq_len * 2 * pairs
        ),
        name="attend_backward",
    )(index, joined, joined, joined, attended, d_attended, totals, normed)


def middle_body(index_ref, *refs):
    pieces, (a_ref, b_ref, tokens_ref, vec_ref, middle_ref, normed_ref, weight_ref, sems) = refs[:6], refs[6:]

    @pl.when(pl.program_id(0) == 0)
    def _():
        rows = pieces[0].shape[0]
        copies = piece_copies(
            index_ref,
            pieces,
            lambda to, first, count: weight_ref.at[
                pl.ds(pl.multiple_of(to * rows + first, 128), count), :
            ],
            sems,
        )
        for copy in copies:
            copy.start()
        for copy in copies:
            copy.wait()

    part = a_ref.shape[1]
    middle = tokens_ref[...].astype(f32) + row_of(vec_ref, "out_bias")
    middle = middle + dot(a_ref[...], weight_ref[:part, :]) + dot(b_ref[...], weight_ref[part:, :])
    middle_ref[...] = middle
    hat, _ = norm_parts(middle)
    normed_ref[...] = (hat * row_of(vec_ref, "ln2_gain") + row_of(vec_ref, "ln2_bias")).astype(bf16)


def middle_product(index, pieces, attended, tokens, vec, block=256):
    rows, width = tokens.shape
    row = pl.BlockSpec((block, width), lambda i, idx: (i, 0))
    part = pl.BlockSpec((block, attended[0].shape[1]), lambda i, idx: (i, 0))
    return pl.pallas_call(
        middle_body,
        grid_spec=pltpu.PrefetchScalarGridSpec(
            num_scalar_prefetch=1,
            grid=(rows // block,),
            in_specs=[any_spec] * 6 + [part, part, row, whole((SHARDS * VEC_ROWS, LANES))],
            out_specs=[row, row, whole((width, width))],
            scratch_shapes=[pltpu.SemaphoreType.DMA((6,))],
        ),
        out_shape=[
            jax.ShapeDtypeStruct((rows, width), f32),
            jax.ShapeDtypeStruct((rows, width), bf16),
            jax.ShapeDtypeStruct((width, width), bf16),
        ],
        compiler_params=params(24),
        cost_estimate=cost(2 * rows * width * width, 10 * rows * width + 4 * width * width),
        name="middle_product",
    )(index, *pieces, *attended, tokens, vec)


def gelu_and_slope(pre):
    cube = 0.044715 * pre * pre
    inner = jnp.tanh(0.7978845608028654 * (pre + cube * pre))
    half = 0.5 * (1.0 + inner)
    slope = half + 0.5 * pre * (1.0 - inner * inner) * (0.7978845608028654 * (1.0 + 3.0 * cube))
    return pre * half, slope


def hidden_body(chunk, fresh, index_ref, *refs):
    pieces, refs = refs[:6], refs[6:]
    if not fresh:
        refs = refs[2:]
    normed_hbm, cot_hbm, vec_ref = refs[:3]
    hidden_out, pre_out, keep_ref, send_ref, bias_ref = refs[3:8]
    normed_ref, cot_ref, up_ref, down_ref, hidden_ref, pre_ref, slope_ref, sems, whole_sems = refs[8:]
    step = pl.program_id(0)
    shard = index_ref[0]
    block = 256

    def loads():
        def rows_of(ref, unit):
            rows = pieces[0].shape[1]
            return piece_copies(
                index_ref,
                [piece.at[unit] for piece in pieces],
                lambda to, first, count: ref.at[pl.ds(pl.multiple_of(to * rows + first, 128), count), :],
                sems.at[unit],
            )

        first = [pltpu.make_async_copy(normed_hbm, normed_ref, whole_sems.at[0])] + rows_of(up_ref, 0)
        second = [pltpu.make_async_copy(cot_hbm, cot_ref, whole_sems.at[1])] + rows_of(down_ref, 1)
        return first, second

    def stores():
        cols = pl.ds(chunk * hidden_ref.shape[1], hidden_ref.shape[1])
        return (
            pltpu.make_async_copy(hidden_ref, hidden_out.at[:, cols], whole_sems.at[2]),
            pltpu.make_async_copy(pre_ref, pre_out.at[:, cols], whole_sems.at[3]),
        )

    @pl.when(step == 0)
    def _():
        first, second = loads()
        for copy in first + second:
            copy.start()
        for copy in first:
            copy.wait()

    @pl.when(step == 1)
    def _():
        for copy in loads()[1]:
            copy.wait()

    rows_each = 256
    count = normed_ref.shape[0] // rows_each

    @pl.when(step == 0)
    def _():
        bias = vec_rows(vec_ref, [(one, VEC["up_bias"][0] + chunk) for one in range(SHARDS)])
        for m in range(count):
            rows = slice(m * rows_each, (m + 1) * rows_each)
            value, slope = gelu_and_slope(dot(normed_ref[rows, :], up_ref[...]) + bias)
            value = value.astype(bf16)
            hidden_ref[rows, :] = value
            slope_ref[rows, :] = slope
        stores()[0].start()

    @pl.when(step == 1)
    def _():
        sums = jnp.zeros(bias_ref.shape, f32)
        for m in range(count):
            rows = slice(m * rows_each, (m + 1) * rows_each)
            d_pre = (dot(cot_ref[rows, :], down_ref[...], 1, 1) * slope_ref[rows, :]).astype(bf16)
            pre_ref[rows, :] = d_pre
            sums = sums + jnp.sum(d_pre.astype(f32), axis=0, keepdims=True)
        bias_ref[...] = sums
        stores()[1].start()

    @pl.when(step >= 2)
    def _():
        k = jnp.where(step < 4, 2 * (step - 2) + 1, 2 * (step - 4))
        cols = pl.ds(pl.multiple_of((shard ^ k) * block, block), block)
        left, right = normed_ref[:, cols], hidden_ref[:, cols]
        one = dot(left, pre_ref[...], 0, 0).astype(bf16)
        two = dot(right, cot_ref[...], 0, 0).astype(bf16)

        @pl.when(step < 4)
        def _():
            send_ref[0, 0] = one
            send_ref[0, 1] = two

        @pl.when(step >= 4)
        def _():
            keep_ref[0, 0] = one
            keep_ref[0, 1] = two

    @pl.when(step == 5)
    def _():
        for copy in stores():
            copy.wait()


def hidden_chunk(chunk, index, pieces, carried, normed, cot, vec, hidden_size):
    rows, width = normed.shape
    size = hidden_size // CHUNKS
    fresh = carried is None
    grads = (2, 2, width // SHARDS, size)
    outs = [
        jax.ShapeDtypeStruct((rows, hidden_size), bf16),
        jax.ShapeDtypeStruct((rows, hidden_size), bf16),
        jax.ShapeDtypeStruct(grads, bf16),
        jax.ShapeDtypeStruct(grads, bf16),
        jax.ShapeDtypeStruct((1, size), f32),
    ]
    unit = (1,) + grads[1:]
    return pl.pallas_call(
        functools.partial(hidden_body, chunk, fresh),
        grid_spec=pltpu.PrefetchScalarGridSpec(
            num_scalar_prefetch=1,
            grid=(6,),
            in_specs=[any_spec] * (8 if fresh else 10) + [whole((SHARDS * VEC_ROWS, LANES))],
            out_specs=[
                any_spec,
                any_spec,
                pl.BlockSpec(unit, lambda i, idx: (jnp.maximum(i - 4, 0), 0, 0, 0)),
                pl.BlockSpec(unit, lambda i, idx: (jnp.clip(i - 2, 0, 1), 0, 0, 0)),
                pl.BlockSpec((1, size), lambda i, idx: (0, 0)),
            ],
            scratch_shapes=[
                pltpu.VMEM((rows, width), bf16),
                pltpu.VMEM((rows, width), bf16),
                pltpu.VMEM((width, size), bf16),
                pltpu.VMEM((size, width), bf16),
                pltpu.VMEM((rows, size), bf16),
                pltpu.VMEM((rows, size), bf16),
                pltpu.VMEM((rows, size), f32),
                pltpu.SemaphoreType.DMA((2, 6)),
                pltpu.SemaphoreType.DMA((4,)),
            ],
        ),
        out_shape=outs,
        input_output_aliases={} if fresh else {7: 0, 8: 1},
        compiler_params=params(48),
        cost_estimate=cost(8 * rows * width * size, 8 * rows * width + 16 * rows * size, rows * size),
        name=f"hidden_chunk{chunk}",
    )(index, *pieces, *(carried or ()), normed, cot, vec)


def norm_back(d_normed, hat, inverse, gain):
    scaled = d_normed * gain
    return inverse * (
        scaled
        - jnp.mean(scaled, axis=-1, keepdims=True)
        - hat * jnp.mean(scaled * hat, axis=-1, keepdims=True)
    )


def column_sum(value):
    return jnp.sum(value, axis=0, keepdims=True)


def chunk_loads(index_ref, pieces, unit, target, sems):
    loads = []
    for chunk in range(CHUNKS):
        group = pieces[6 * chunk : 6 * chunk + 6]
        rows = group[0].shape[1]
        loads.append(
            piece_copies(
                index_ref,
                [piece.at[unit] for piece in group],
                lambda to, first, count, chunk=chunk: target(
                    chunk, pl.multiple_of(to * rows + first, 128), count
                ),
                sems.at[chunk],
            )
        )
    return loads


def block_back_body(index_ref, *refs, blocks):
    pieces, refs = refs[: 6 * CHUNKS], refs[6 * CHUNKS :]
    pre_ref, middle_ref, cot_ref, a_ref, b_ref, weight_ref, vec_ref = refs[:7]
    d_middle_ref, d_attended_ref, keep_ref, send_ref, sums_ref = refs[7:12]
    up_ref, d_one_ref, sems = refs[12:]
    step = pl.program_id(0)
    rows = pre_ref.shape[0]
    size = up_ref.shape[1] // CHUNKS

    def rest(d_normed):
        middle = middle_ref[...]
        cot = cot_ref[...].astype(f32)
        hat, inverse = norm_parts(middle)
        d_middle = cot + norm_back(d_normed, hat, inverse, row_of(vec_ref, "ln2_gain"))
        d_one = d_middle.astype(bf16)
        d_middle_ref[...] = d_middle
        d_one_ref[pl.ds(pl.multiple_of(step * rows, rows), rows), :] = d_one
        sums_ref[0:1, :] += column_sum(d_normed * hat)
        sums_ref[1:2, :] += column_sum(d_normed)
        sums_ref[2:3, :] += column_sum(d_one.astype(f32))
        sums_ref[3:4, :] += column_sum(cot)

    @pl.when(step == 0)
    def _():
        loads = chunk_loads(
            index_ref,
            pieces,
            0,
            lambda chunk, first, count: up_ref.at[pl.ds(first, count), chunk * size : (chunk + 1) * size],
            sems,
        )
        for group in loads:
            for copy in group:
                copy.start()
        sums_ref[...] = jnp.zeros_like(sums_ref)
        d_normed = None
        for chunk, group in enumerate(loads):
            for copy in group:
                copy.wait()
            cols = slice(chunk * size, (chunk + 1) * size)
            term = dot(pre_ref[:, cols], up_ref[:, cols], 1, 1)
            d_normed = term if d_normed is None else d_normed + term
        rest(d_normed)

    @pl.when((step > 0) & (step < blocks))
    def _():
        rest(dot(pre_ref[...], up_ref[...], 1, 1))

    for t, k in enumerate((1, 3, 0, 2)):

        @pl.when(step == blocks + t)
        def _(t=t, k=k):
            block = weight_ref.shape[0] // SHARDS
            part = keep_ref.shape[3]
            d_one = d_one_ref[...]
            d_attended_ref[...] = dot(d_one, weight_ref[t * block : (t + 1) * block, :], 1, 1).astype(bf16)
            shard = index_ref[0] ^ k
            target = send_ref if t < 2 else keep_ref
            cols = pl.ds(pl.multiple_of((shard & 1) * block, block), block)

            def put(ref):
                value = dot(ref[:, cols], d_one, 0, 0).astype(bf16)
                for unit in range(2):
                    target[0, unit] = value[:, unit * part : (unit + 1) * part]

            pl.when(shard < 2)(lambda: put(a_ref))
            pl.when(shard >= 2)(lambda: put(b_ref))


def block_back(index, pieces, d_pre, middle, cot, attended, weight, vec, rows_each=256):
    rows, width = middle.shape
    size = d_pre.shape[1]
    blocks = rows // rows_each
    quarter = width // SHARDS

    def by_rows(cols):
        return pl.BlockSpec((rows_each, cols), lambda i, idx: (jnp.minimum(i, blocks - 1), 0))

    grads = (2, 2, quarter, width // 2)
    unit = (1,) + grads[1:]
    half = whole((rows, attended[0].shape[1]))
    return pl.pallas_call(
        functools.partial(block_back_body, blocks=blocks),
        grid_spec=pltpu.PrefetchScalarGridSpec(
            num_scalar_prefetch=1,
            grid=(blocks + SHARDS,),
            in_specs=[any_spec] * (6 * CHUNKS)
            + [
                by_rows(size),
                by_rows(width),
                by_rows(width),
                half,
                half,
                whole((width, width)),
                whole((SHARDS * VEC_ROWS, LANES)),
            ],
            out_specs=[
                by_rows(width),
                pl.BlockSpec((rows, quarter), lambda i, idx: (0, jnp.maximum(i - blocks, 0))),
                pl.BlockSpec(unit, lambda i, idx: (jnp.maximum(i - blocks - 2, 0), 0, 0, 0)),
                pl.BlockSpec(unit, lambda i, idx: (jnp.clip(i - blocks, 0, 1), 0, 0, 0)),
                whole((8, width)),
            ],
            scratch_shapes=[
                pltpu.VMEM((width, size), bf16),
                pltpu.VMEM((rows, width), bf16),
                pltpu.SemaphoreType.DMA((CHUNKS, 6)),
            ],
        ),
        out_shape=[
            jax.ShapeDtypeStruct((rows, width), f32),
            jax.ShapeDtypeStruct((rows, width), bf16),
            jax.ShapeDtypeStruct(grads, bf16),
            jax.ShapeDtypeStruct(grads, bf16),
            jax.ShapeDtypeStruct((8, width), f32),
        ],
        compiler_params=params(48),
        cost_estimate=cost(2 * rows * width * (size + 2 * width), 2 * rows * size + 2 * width * size + 16 * rows * width),
        name="block_back",
    )(index, *pieces, d_pre, middle, cot, *attended, weight, vec)


def block_out_body(index_ref, *refs):
    pieces, (hidden_ref, middle_ref, vec_ref, out_ref, down_ref, sems) = refs[: 6 * CHUNKS], refs[6 * CHUNKS :]
    step = pl.program_id(0)
    size = down_ref.shape[0] // CHUNKS

    def rest(value):
        out_ref[...] = (middle_ref[...] + row_of(vec_ref, "down_bias") + value).astype(bf16)

    @pl.when(step == 0)
    def _():
        loads = chunk_loads(
            index_ref,
            pieces,
            1,
            lambda chunk, first, count: down_ref.at[pl.ds(chunk * size + first, count), :],
            sems,
        )
        for group in loads:
            for copy in group:
                copy.start()
        total = None
        for chunk, group in enumerate(loads):
            for copy in group:
                copy.wait()
            cols = slice(chunk * size, (chunk + 1) * size)
            term = dot(hidden_ref[:, cols], down_ref[cols, :])
            total = term if total is None else total + term
        rest(total)

    @pl.when(step > 0)
    def _():
        rest(dot(hidden_ref[...], down_ref[...]))


def block_output(index, pieces, hidden, middle, vec, rows_each=256):
    rows, width = middle.shape
    size = hidden.shape[1]

    def by_rows(cols):
        return pl.BlockSpec((rows_each, cols), lambda i, idx: (i, 0))

    return pl.pallas_call(
        block_out_body,
        grid_spec=pltpu.PrefetchScalarGridSpec(
            num_scalar_prefetch=1,
            grid=(rows // rows_each,),
            in_specs=[any_spec] * (6 * CHUNKS) + [by_rows(size), by_rows(width), whole((SHARDS * VEC_ROWS, LANES))],
            out_specs=by_rows(width),
            scratch_shapes=[pltpu.VMEM((size, width), bf16), pltpu.SemaphoreType.DMA((CHUNKS, 6))],
        ),
        out_shape=jax.ShapeDtypeStruct((rows, width), bf16),
        compiler_params=params(48),
        cost_estimate=cost(2 * rows * width * size, 2 * rows * size + 2 * width * size + 6 * rows * width),
        name="block_output",
    )(index, *pieces, hidden, middle, vec)


def input_grad_body(index_ref, *refs, blocks):
    parts, pieces = refs[:6], (refs[6:10], refs[10:16])
    tokens_ref, d_middle_ref, vec_ref, sums_ref, bqv_a_ref, bqv_b_ref = refs[16:22]
    bias_refs = refs[22 : 22 + CHUNKS]
    out_ref, grads_ref, gain_ref, shift_ref, *weights, sems = refs[22 + CHUNKS :]
    step = pl.program_id(0)

    @pl.when(step == 0)
    def _():
        copies = []
        for half in range(2):
            rows = pieces[half][0].shape[0]
            copies += piece_copies(
                index_ref,
                pieces[half],
                lambda to, first, count, half=half, rows=rows: weights[half].at[
                    pl.ds(pl.multiple_of(to * rows + first, 128), count), :
                ],
                sems.at[half],
            )
        for copy in copies:
            copy.start()
        for copy in copies:
            copy.wait()
        gain_ref[...] = jnp.zeros_like(gain_ref)
        shift_ref[...] = jnp.zeros_like(shift_ref)

    d_normed = None
    for half in range(2):
        for i in range(3):
            ref = parts[3 * half + i]
            part = ref.shape[1]
            term = dot(ref[...], weights[half][:, i * part : (i + 1) * part], 1, 1)
            d_normed = term if d_normed is None else d_normed + term
    hat, inverse = norm_parts(tokens_ref[...].astype(f32))
    out_ref[...] = d_middle_ref[...] + norm_back(d_normed, hat, inverse, row_of(vec_ref, "ln1_gain"))
    gain_ref[...] += column_sum(d_normed * hat)
    shift_ref[...] += column_sum(d_normed)

    @pl.when(step == blocks - 1)
    def _():
        grads_ref[...] = jnp.zeros_like(grads_ref)

        def put(name, shard, value, offset=0):
            first = shard * VEC_ROWS + VEC[name][0] + offset
            for i in range(value.shape[1] // LANES):
                grads_ref[first + i : first + i + 1, :] = value[:, i * LANES : (i + 1) * LANES]

        for shard in range(SHARDS):
            cols = slice(shard * 256, (shard + 1) * 256)
            put("ln1_gain", shard, gain_ref[:, cols])
            put("ln1_bias", shard, shift_ref[:, cols])
            put("ln2_gain", shard, sums_ref[0:1, cols])
            put("ln2_bias", shard, sums_ref[1:2, cols])
            put("out_bias", shard, sums_ref[2:3, cols])
            put("down_bias", shard, sums_ref[3:4, cols])
            source = bqv_a_ref if shard % 2 == 0 else bqv_b_ref
            put("b_qv", shard, source[shard // 2 : shard // 2 + 1, :])
            for chunk in range(CHUNKS):
                size = bias_refs[chunk].shape[1] // SHARDS
                put("up_bias", shard, bias_refs[chunk][:, shard * size : (shard + 1) * size], chunk)


def input_gradient(index, parts, weights, tokens, d_middle, vec, sums, bqv, biases, rows_each=256):
    rows, width = tokens.shape
    part = parts[0].shape[1]
    blocks = rows // rows_each

    def by_rows(cols):
        return pl.BlockSpec((rows_each, cols), lambda i, idx: (i, 0))

    return pl.pallas_call(
        functools.partial(input_grad_body, blocks=blocks),
        grid_spec=pltpu.PrefetchScalarGridSpec(
            num_scalar_prefetch=1,
            grid=(blocks,),
            in_specs=[by_rows(part)] * 6
            + [any_spec] * 10
            + [by_rows(width), by_rows(width), whole((SHARDS * VEC_ROWS, LANES)), whole((8, width))]
            + [whole((2, part))] * 2
            + [whole(bias.shape) for bias in biases],
            out_specs=[by_rows(width), whole((SHARDS * VEC_ROWS, LANES))],
            scratch_shapes=[pltpu.VMEM((1, width), f32)] * 2
            + [pltpu.VMEM((width, 3 * part), bf16)] * 2
            + [pltpu.SemaphoreType.DMA((2, 6))],
        ),
        out_shape=[
            jax.ShapeDtypeStruct((rows, width), f32),
            jax.ShapeDtypeStruct((SHARDS * VEC_ROWS, LANES), f32),
        ],
        compiler_params=params(40),
        cost_estimate=cost(12 * rows * width * part, 10 * rows * width + 12 * rows * part + 12 * width * part),
        name="input_gradient",
    )(index, *parts, *weights, tokens, d_middle, vec, sums, *bqv, *biases)


def place_body(index_ref, pair_ref, other_ref, *refs, plan, fresh):
    outs = len(refs) - 2 if fresh else (len(refs) - 2) // 2
    out_refs = refs[-2 - outs : -2]
    scratch, sems = refs[-2:]
    low, mid = index_ref[1], index_ref[2]
    rows = pair_ref.shape[2]
    for a, ref in enumerate((pair_ref, other_ref)):
        for b in range(2):
            first = pl.multiple_of((low ^ a) * (2 * rows) + (mid ^ b) * rows, rows)
            for u in range(pair_ref.shape[1]):
                scratch[u, pl.ds(first, rows), :] = ref[b, u].astype(f32)
    copies = []
    for i, (unit, cols, width, out, row, col) in enumerate(plan):
        copies.append(
            pltpu.make_async_copy(
                scratch.at[unit, :, cols : cols + width],
                out_refs[out].at[row : row + 4 * rows, col : col + width],
                sems.at[i],
            )
        )
    for copy in copies:
        copy.start()
    for copy in copies:
        copy.wait()


def place(index, pieces, plan, shapes, carried, name):
    pair, other = pieces
    _, units, rows, width = pair.shape
    fresh = carried is None
    count = len(shapes)
    return pl.pallas_call(
        functools.partial(place_body, plan=plan, fresh=fresh),
        grid_spec=pltpu.PrefetchScalarGridSpec(
            num_scalar_prefetch=1,
            grid=(1,),
            in_specs=[whole(pair.shape), whole(other.shape)] + ([] if fresh else [any_spec] * count),
            out_specs=[any_spec] * count,
            scratch_shapes=[pltpu.VMEM((units, 4 * rows, width), f32), pltpu.SemaphoreType.DMA((len(plan),))],
        ),
        out_shape=[jax.ShapeDtypeStruct(shape, f32) for shape in shapes],
        input_output_aliases={} if fresh else {3 + i: i for i in range(count)},
        compiler_params=params(16),
        cost_estimate=cost(units * 4 * rows * width, units * 4 * rows * width * 6),
        name=name,
    )(index, pair, other, *(carried or ()))


def body(
    mesh,
    tokens,
    piece_start,
    ln1_gain,
    ln1_bias,
    query_key_value_weight,
    b_qv,
    attention_out_weight,
    attention_out_bias,
    ln2_gain,
    ln2_bias,
    up_weight,
    up_bias,
    down_weight,
    down_bias,
    cotangent,
):
    count, seq_len, width = tokens.shape
    rows = count * seq_len
    hidden_size = up_weight.shape[1]
    tokens = tokens.reshape(rows, width)
    cot = cotangent.reshape(rows, width)
    moves = Moves(mesh, piece_start)
    half = width // 2
    size = hidden_size // CHUNKS
    block = size // SHARDS

    def as_rows(value):
        return value.reshape(-1, LANES)

    def joined_cols(which):
        return jnp.concatenate(
            [
                query_key_value_weight[:, i * width + which * half : i * width + (which + 1) * half]
                for i in range(3)
            ],
            axis=1,
        )

    own_a = joined_cols(0)
    own_vec = jnp.concatenate(
        [
            as_rows(after(value, own_a))
            for value in (ln1_gain, ln1_bias, b_qv, attention_out_bias, ln2_gain, ln2_bias, up_bias, down_bias)
        ]
        + [jnp.zeros((VEC_ROWS - 12, LANES), bf16)]
    )

    def hidden_own(chunk):
        up = jnp.concatenate(
            [
                up_weight[:, s * size + chunk * block : s * size + (chunk + 1) * block]
                for s in range(SHARDS)
            ],
            axis=1,
        )
        return jnp.stack([up, down_weight[chunk * block : (chunk + 1) * block, :]])

    far_a = moves.across(own_a)
    near_a = moves.core(own_a)
    far_vec = moves.across(own_vec)
    near_vec = moves.core(own_vec)
    own_b = joined_cols(1)
    half_b = moves.half(own_b)
    hidden_owns = [hidden_own(chunk) for chunk in range(CHUNKS)]
    hidden_halves = [moves.half(own) for own in hidden_owns]
    out_half = moves.half(attention_out_weight)
    far_near_vec = moves.core(far_vec)
    moves.wait(half_b, out_half, *hidden_halves)
    normed, vec = first_norm(moves.index, tokens, (own_vec, near_vec, far_vec, far_near_vec))
    moves.ran(vec)

    joined, attended, totals = [None] * 2, [None] * 2, [None] * 2
    hidden_far, hidden_near, hidden_other = [None] * CHUNKS, [None] * CHUNKS, [None] * CHUNKS
    hidden_pieces = [None] * CHUNKS

    def fetch(chunk, kernels):
        hidden_far[chunk] = moves.across(hidden_halves[chunk])
        hidden_near[chunk] = moves.core(hidden_owns[chunk])
        moves.by(kernels, hidden_far[chunk], hidden_near[chunk])

    def relay(chunk, kernels):
        hidden_other[chunk] = moves.rep(hidden_far[chunk], 1)
        moves.by(kernels, hidden_other[chunk])

    far_b = moves.across(half_b)
    near_b = moves.core(own_b)
    moves.by(1, far_b, near_b)
    joined_pieces = [(own_a, near_a, far_a, moves.core(far_a))]
    joined[0] = joined_product(0, moves.index, joined_pieces[0], normed, vec)
    moves.ran(joined[0])
    other_b = moves.rep(far_b, 1)
    moves.by(1, other_b)
    fetch(0, 1)
    attended[0], totals[0] = attend_forward(0, moves.index, joined[0])
    moves.ran(totals[0])
    relay(0, 2)
    out_far = moves.across(out_half)
    out_near = moves.core(attention_out_weight)
    moves.by(1, out_far, out_near)
    joined_pieces.append((own_b, near_b, far_b, other_b, moves.core(far_b), moves.core(other_b)))
    joined[1] = joined_product(1, moves.index, joined_pieces[1], normed, vec)
    moves.ran(joined[1])
    out_other = moves.rep(out_far, 1)
    moves.by(1, out_other)
    fetch(1, 1)
    attended[1], totals[1] = attend_forward(1, moves.index, joined[1])
    moves.ran(totals[1])
    relay(1, 2)
    fetch(2, 2)
    middle, normed_two, out_weight = middle_product(
        moves.index,
        (attention_out_weight, out_near, out_far, out_other, moves.core(out_far), moves.core(out_other)),
        attended,
        tokens,
        vec,
    )
    moves.ran(normed_two)

    carried = None
    shard_sums, up_biases = [], []

    def hidden_step(chunk):
        nonlocal carried
        far, other = hidden_far[chunk], hidden_other[chunk]
        hidden_pieces[chunk] = (
            hidden_owns[chunk],
            hidden_near[chunk],
            far,
            other,
            moves.core(far),
            moves.core(other),
        )
        *carried, keep, send, bias = hidden_chunk(
            chunk, moves.index, hidden_pieces[chunk], carried, normed_two, cot, vec, hidden_size
        )
        moves.ran(bias)
        up_biases.append(bias)
        shard_sums.append(ShardSum(moves, keep, send))

    fetch(3, 1)
    hidden_step(0)
    relay(2, 1)
    hidden_step(1)
    relay(3, 1)
    shard_sums[0].cross(1)
    hidden_step(2)
    shard_sums[1].cross(1)
    hidden_step(3)
    shard_sums[2].cross(1)
    first_sum = RepSum(moves, shard_sums[:2])
    all_pieces = [piece for pieces in hidden_pieces for piece in pieces]
    hidden, d_pre = carried
    d_middle, d_attended, keep, send, sums = block_back(
        moves.index, all_pieces, d_pre, middle, cot, attended, out_weight, vec
    )
    moves.ran(sums)
    parts, bqv = [], []

    def backward(which):
        *grads, keep, send, bias = attend_backward(
            which, moves.index, joined[which], attended[which], d_attended, totals[which], normed
        )
        parts.extend(grads)
        bqv.append(bias)
        moves.ran(bias)
        return ShardSum(moves, keep, send)

    shard_sums[3].cross(1)
    out_sum = ShardSum(moves, keep, send)
    first_sum.split()
    second_sum = RepSum(moves, shard_sums[2:3])
    a_sum = backward(0)
    out_sum.cross(1)
    first_sum.add()
    second_sum.split()
    third_sum = RepSum(moves, shard_sums[3:4])
    b_sum = backward(1)
    a_sum.cross(1)
    first_sum.spread()
    second_sum.add()
    third_sum.split()
    input_grad, vec_grads = input_gradient(
        moves.index, parts, joined_pieces[0] + joined_pieces[1], tokens, d_middle, vec, sums, bqv, up_biases
    )
    moves.ran(vec_grads)
    b_sum.cross(1)
    fourth_sum = RepSum(moves, [out_sum, a_sum])
    first_sum.finish()
    second_sum.spread()
    block_out = block_output(moves.index, all_pieces, hidden, middle, vec)
    moves.ran(block_out)

    def place_hidden(chunks, pieces, grads, name):
        plan = []
        for i, chunk in enumerate(chunks):
            plan += [(2 * i, s * block, block, 0, 0, s * size + chunk * block) for s in range(SHARDS)]
            plan += [(2 * i + 1, 0, width, 1, chunk * block, 0)]
        shapes = [(width // SHARDS, hidden_size), (size, width)]
        grads = place(moves.index, pieces, plan, shapes, grads, name)
        moves.ran(grads[0])
        return grads

    last_sum = RepSum(moves, [b_sum])
    fourth_sum.split()
    second_sum.finish()
    third_sum.add()
    vec_sum = VecSum(moves, vec_grads)
    grads = place_hidden((0, 1), first_sum.pieces(), None, "place_hidden_first")
    last_sum.split()
    fourth_sum.add()
    third_sum.spread()
    vec_sum.step()
    grads = place_hidden((2,), second_sum.pieces(), grads, "place_hidden_second")
    last_sum.add()
    fourth_sum.spread()
    third_sum.finish()
    vec_sum.step()
    fourth_sum.finish()
    last_sum.spread()
    grad_up, grad_down = place_hidden((3,), third_sum.pieces(), grads, "place_hidden_third")
    vec_sum.step()
    last_sum.finish()
    vec_sum = vec_sum.rest()
    third = width // SHARDS
    plan = [(i, 0, half, 0, 0, i * half) for i in range(2)]
    plan += [(2 + i, 0, half, 1, 0, i * width) for i in range(3)]
    shapes = [(third, width), (third, 3 * width)]
    grad_out, grad_joined = place(moves.index, fourth_sum.pieces(), plan, shapes, None, "place_fourth")
    plan = [(i, 0, half, 0, 0, i * width + half) for i in range(3)]
    (grad_joined,) = place(moves.index, last_sum.pieces(), plan, shapes[1:], (grad_joined,), "place_last")

    def vec_part(name):
        first, count = VEC[name]
        return vec_sum[first : first + count].reshape(count * LANES)

    return (
        block_out.reshape(count, seq_len, width),
        input_grad.reshape(count, seq_len, width),
        vec_part("ln1_gain"),
        vec_part("ln1_bias"),
        grad_joined,
        vec_part("b_qv"),
        grad_out,
        vec_part("out_bias"),
        vec_part("ln2_gain"),
        vec_part("ln2_bias"),
        grad_up,
        vec_part("up_bias"),
        grad_down,
        vec_part("down_bias"),
    )


def solution(mesh):
    batch = P(("shard", "rep"), None, None)
    vector, matrix = P("shard"), P("shard", None)
    in_specs = (
        batch,
        P(("shard", "rep")),
        vector,
        vector,
        matrix,
        vector,
        matrix,
        vector,
        vector,
        vector,
        matrix,
        vector,
        matrix,
        vector,
        batch,
    )
    out_specs = (
        batch,
        batch,
        vector,
        vector,
        matrix,
        vector,
        matrix,
        vector,
        vector,
        vector,
        matrix,
        vector,
        matrix,
        vector,
    )
    return jax.shard_map(
        functools.partial(body, mesh), mesh=mesh, in_specs=in_specs, out_specs=out_specs, check_vma=False
    )
```
